32 devices in a mesh: tile: 16 (over z, x, core), group: 2 (over y).
Axes of the slice: x: 2, y: 2, z: 4, core: 2. Of those that a mesh axis runs over, the one named last changes fastest.
Arguments:
- state: float32 [8, 5, 16, 128, 128], P('group', None, 'tile'), may hold values from -6 to 6
- courant_x: float32 [8], P('group'), may hold values from -0.35 to 0.35
- courant_y: float32 [8], P('group'), may hold values from -0.35 to 0.35
- diffusion: float32 [5], replicated, may hold values from 0.02 to 0.07
- neighbours: int32 [9, 16, 128, 128], P(None, 'tile'), may hold values from 0 to 16899, as said below
- w_in: bfloat16 [360, 256], replicated, may hold values from -0.3125 to 0.3125
- w_mid: bfloat16 [256, 256], replicated, may hold values from -0.375 to 0.375
- w_out: bfloat16 [256, 40], replicated, may hold values from -0.375 to 0.375
Outputs:
- updated: float32 [8, 5, 16, 128, 128], P('group', None, 'tile')
The draws below stay inside these ranges and needn't reach their ends.
Inputs may be any that keep to these rules, and one draw needn't show every extreme that they name: `neighbours`: for each column the nine entries name the cells of its 3 x 3 neighbourhood, each once, in one of eight rotated or mirrored orders; cells are numbered in the tile extended by one cell on every side, row by row with 130 cells a row.
All inputs are finite; a program needn't handle non-finite values.
Results may differ from the reference program's by a relative error of at most 0.0016.
Values may be sent and summed in bfloat16 or wider, within the bound.
No kernel may reach another device: no remote copies, remote signals or barrier semaphores. Data moves between devices by JAX's collectives and lax.ppermute only.
A program may use at most 128 MiB of HBM per device.

```python
import math
import jax
import jax.numpy as jnp
from jax import lax

LEV = 8
F = 5
HID = 256
TILE_ROWS = 8
CX = 128
CY = 128
TILES = 16
C = 40
FEAT = 360


def draw_neighbours(key, part):
    offset_a = jnp.array([-1, -1, -1, 0, 0, 0, 1, 1, 1], jnp.int32)[:, None, None, None]
    offset_b = jnp.array([-1, 0, 1, -1, 0, 1, -1, 0, 1], jnp.int32)[:, None, None, None]
    turns = jax.random.randint(key, (1, TILES, CX, CY), 0, 8).astype(jnp.int32)
    offset_b = jnp.where(turns >= 4, -offset_b, offset_b)
    quarter = turns % 4
    rot_a = jnp.where(quarter == 0, offset_a, jnp.where(quarter == 1, -offset_b, jnp.where(quarter == 2, -offset_a, offset_b)))
    rot_b = jnp.where(quarter == 0, offset_b, jnp.where(quarter == 1, offset_a, jnp.where(quarter == 2, -offset_b, -offset_a)))
    rows_i = jnp.arange(CX, dtype=jnp.int32)[None, None, :, None]
    cols_j = jnp.arange(CY, dtype=jnp.int32)[None, None, None, :]
    return ((rows_i + 1 + rot_a) * (CY + 2) + cols_j + 1 + rot_b).astype(jnp.int32)


def levels(rng, shape, split, low, top_value):
    gain, own = 1.0, jax.random.fold_in(rng, 6)
    for axis_at, shards_of in split:
        heights = jnp.exp(jax.random.uniform(jax.random.fold_in(own, axis_at), (shards_of,), jnp.float32, low / len(split), top_value / len(split)))
        gain = gain * jnp.repeat(heights, shape[axis_at] // shards_of).reshape([-1 if axis == axis_at else 1 for axis in range(len(shape))])
    return gain


def centred(key, shape, deviation, limit, split=(), kind=jnp.bfloat16):
    entries = jax.random.normal(key, shape, jnp.float32) * deviation
    if len(split) > 0:
        entries = levels(key, shape, split, -0.22, 0.18) * entries
    return jnp.clip(entries, min=-limit, max=limit).astype(kind)


def setup_inputs(seed: int = 0) -> dict:
    key_of = jax.random.split(jax.random.key(seed), 9)
    state = centred(key_of[0], (LEV, F, TILES, CX, CY), 1.0, 6.0, ((0, 2), (2, 16)), jnp.float32)
    courant_x = jnp.clip(jax.random.uniform(key_of[1], (LEV,), jnp.float32, -0.35, 0.35) * levels(key_of[1], (LEV,), ((0, 2),), -0.4, 0.0), -0.35, 0.35)
    courant_y = jnp.clip(jax.random.uniform(key_of[2], (LEV,), jnp.float32, -0.35, 0.35) * levels(key_of[2], (LEV,), ((0, 2),), -0.4, 0.0), -0.35, 0.35)
    diffusion = jnp.clip(jnp.exp(jax.random.uniform(key_of[3], (F,), jnp.float32, math.log(0.02), math.log(0.07))), 0.02, 0.07)
    neighbours = draw_neighbours(jax.random.fold_in(key_of[8], 71), 0)
    w_in = centred(key_of[5], (FEAT, HID), FEAT ** -0.5, 0.3125)
    w_mid = centred(key_of[6], (HID, HID), HID ** -0.5, 0.375)
    w_out = centred(key_of[7], (HID, C), HID ** -0.5, 0.375)
    return {"state": state, "courant_x": courant_x, "courant_y": courant_y, "diffusion": diffusion, "neighbours": neighbours, "w_in": w_in, "w_mid": w_mid, "w_out": w_out}


def to_grid(blocks):
    rows_x = TILES // TILE_ROWS
    grid = blocks.reshape(LEV * F, rows_x, TILE_ROWS, CX, CY).transpose(0, 1, 3, 2, 4)
    return grid.reshape(LEV * F, rows_x * CX, TILE_ROWS * CY)


def from_grid(grid):
    rows_x = TILES // TILE_ROWS
    blocks = grid.reshape(LEV, F, rows_x, CX, TILE_ROWS, CY).transpose(0, 1, 2, 4, 3, 5)
    return blocks.reshape(LEV, F, TILES, CX, CY)


def pad_border(grid):
    wrapped = jnp.pad(grid, ((0, 0), (1, 1), (0, 0)), mode="wrap")
    return jnp.pad(wrapped, ((0, 0), (0, 0), (1, 1)))


def advance(padded, speed_x, speed_y, spread):
    center = padded[:, 1:-1, 1:-1]
    lower_x = padded[:, :-2, 1:-1]
    upper_x = padded[:, 2:, 1:-1]
    lower_y = padded[:, 1:-1, :-2]
    upper_y = padded[:, 1:-1, 2:]
    result = center - jnp.maximum(speed_x, 0.0) * (center - lower_x) - jnp.minimum(speed_x, 0.0) * (upper_x - center)
    result = result - jnp.maximum(speed_y, 0.0) * (center - lower_y) - jnp.minimum(speed_y, 0.0) * (upper_y - center)
    return result + spread * (lower_x + upper_x + lower_y + upper_y - 4.0 * center)


def physics_terms(stacked, w_in, w_mid, w_out):
    contract = (((0,), (0,)), ((), ()))
    first = jax.nn.silu(lax.dot_general(w_in, stacked, contract, preferred_element_type=jnp.float32)).astype(jnp.bfloat16)
    second = jax.nn.silu(lax.dot_general(w_mid, first, contract, preferred_element_type=jnp.float32)).astype(jnp.bfloat16)
    return lax.dot_general(w_out, second, contract, preferred_element_type=jnp.float32).astype(jnp.bfloat16)


def reference(state, courant_x, courant_y, diffusion, neighbours, w_in, w_mid, w_out):
    grid = to_grid(state)
    speed_x = jnp.repeat(courant_x, F)[:, None, None]
    speed_y = jnp.repeat(courant_y, F)[:, None, None]
    spread = jnp.tile(diffusion, LEV)[:, None, None]
    for sweep in range(2):
        grid = advance(pad_border(grid), speed_x, speed_y, spread)
    padded = pad_border(grid).astype(jnp.bfloat16)

    def tile_terms(tile_number):
        start_x = ((tile_number // TILE_ROWS) * CX).astype(jnp.int32)
        start_y = ((tile_number % TILE_ROWS) * CY).astype(jnp.int32)
        window = lax.dynamic_slice(padded, (jnp.int32(0), start_x, start_y), (LEV * F, CX + 2, CY + 2))
        flat = window.reshape(LEV * F, (CX + 2) * (CY + 2))
        index = lax.dynamic_index_in_dim(neighbours, tile_number, 1, False).reshape(9, CX * CY)
        stacked = jnp.take(flat, index, axis=1).reshape(LEV * F * 9, CX * CY)
        return physics_terms(stacked, w_in, w_mid, w_out)

    terms = lax.map(tile_terms, jnp.arange(TILES, dtype=jnp.int32))
    terms = terms.reshape(TILES, LEV, F, CX, CY).transpose(1, 2, 0, 3, 4)
    return from_grid(grid) + terms.astype(jnp.float32)
```

```python
import functools

import jax
import jax.numpy as jnp
from jax import lax
from jax.experimental import pallas as pl
from jax.experimental.pallas import tpu as pltpu
from jax.sharding import PartitionSpec as P

TILE_ROWS = 8
DEEP = 3
EXTRA = 16
ROW_UNROLL = 2

F32 = jnp.float32
BF16 = jnp.bfloat16
VMEM_SPEC = pl.BlockSpec(memory_space=pltpu.VMEM)
ANY_SPEC = pl.BlockSpec(memory_space=pl.ANY)
PARAMS = pltpu.CompilerParams(vmem_limit_bytes=56 << 20)


def whole(ref):
    return ref[...]


def lanes_of(shape):
    return lax.broadcasted_iota(jnp.int32, shape, len(shape) - 1)


def edge_kernel(state_ref, east_ref, west_ref, rows_ref):
    chans, cells_x, cells_y = state_ref.shape
    slot = lax.broadcasted_iota(jnp.int32, (16, cells_y), 0)
    lane = lanes_of((16, cells_y))
    wanted = jnp.where(slot < 8, slot + cells_y - DEEP, slot - 8)
    valid = (slot % 8) < DEEP
    pick = jnp.where(valid & (lane == wanted), 1.0, 0.0).astype(BF16)
    for c in range(chans):
        block = state_ref[c].astype(BF16)
        strips = lax.dot_general(
            pick, block, (((1,), (1,)), ((), ())), preferred_element_type=F32
        ).astype(BF16)
        east_ref[c] = strips[0:8]
        west_ref[c] = strips[8:16]
        rows_ref[c] = jnp.concatenate(
            [state_ref[c, 0:8], state_ref[c, cells_x - 8 : cells_x]], axis=0
        ).astype(BF16)


def transport_kernel(
    state_ref, coef_ref, west_ref, east_ref, up_ref, upw_ref, upe_ref,
    down_ref, downw_ref, downe_ref, *rest, cells_x,
):
    moved_ref, mine0, mine1, theirs0, theirs1 = rest[:5]
    raw, once, twice, strips, border, extra = rest[5:]
    chans = state_ref.shape[0] // cells_x
    width = state_ref.shape[1]
    half = cells_x // 2
    part = half // 2
    own = lax.axis_index("group")
    place = lax.axis_index("tile") % TILE_ROWS
    lane = lanes_of((chans, width))
    is_east = lane < width // 2
    keep = jnp.where(
        is_east,
        jnp.where(place == TILE_ROWS - 1, 0.0, 1.0),
        jnp.where(place == 0, 0.0, 1.0),
    )
    for s, refs in enumerate(
        ((west_ref, east_ref), (upw_ref, upe_ref), (downw_ref, downe_ref))
    ):
        for side in range(2):
            strips[s, side] = refs[side][...].astype(F32)
    border[0] = up_ref[...].astype(F32)
    border[1] = down_ref[...].astype(F32)

    def edge_slab(source, row):
        slab = jnp.zeros((chans, width), F32)
        for k in range(DEEP):
            wk = strips[source, 0, pl.ds(k, chans, stride=8), :]
            ek = strips[source, 1, pl.ds(k, chans, stride=8), :]
            at = width - DEEP + k
            slab = jnp.where(lane == at, pltpu.roll(wk, lax.rem(at - row + width, width), 1), slab)
            slab = jnp.where(lane == k, pltpu.roll(ek, lax.rem(k - row + width, width), 1), slab)
        return slab

    def fill(i, _):
        raw[i + DEEP, 0] = state_ref[pl.ds(i, chans, stride=cells_x), :]
        raw[i + DEEP, 1] = edge_slab(0, i)
        return 0

    lax.fori_loop(0, cells_x, fill, 0, unroll=4)
    for k in range(DEEP):
        raw[k, 0] = border[0, pl.ds(16 - DEEP + k, chans, stride=16), :]
        raw[k, 1] = edge_slab(1, jnp.int32(cells_x - DEEP + k))
        raw[cells_x + DEEP + k, 0] = border[1, pl.ds(k, chans, stride=16), :]
        raw[cells_x + DEEP + k, 1] = edge_slab(2, jnp.int32(k))

    def sweep(src, r):
        c0, cxl, cxu, cyl, cyu = [coef_ref[n] for n in range(5)]
        q, e = src[r, 0], src[r, 1]
        ql, el = pltpu.roll(q, 1, 1), pltpu.roll(e, 1, 1)
        qu, eu = pltpu.roll(q, width - 1, 1), pltpu.roll(e, width - 1, 1)
        first, last = lane == 0, lane == width - 1
        ql, el = jnp.where(first, el, ql), jnp.where(first, ql, el)
        qu, eu = jnp.where(last, eu, qu), jnp.where(last, qu, eu)
        q2 = c0 * q + cxl * src[r - 1, 0] + cxu * src[r + 1, 0] + cyl * ql + cyu * qu
        e2 = c0 * e + cxl * src[r - 1, 1] + cxu * src[r + 1, 1] + cyl * el + cyu * eu
        return q2, e2 * keep

    def first_sweep(r, _):
        q2, e2 = sweep(raw, r)
        once[r, 0] = q2
        once[r, 1] = e2
        return 0

    lax.fori_loop(1, cells_x + 2 * DEEP - 1, first_sweep, 0, unroll=ROW_UNROLL)

    def second_sweep(i, _):
        q2, e2 = sweep(once, i + DEEP)
        moved_ref[pl.ds(i, chans, stride=cells_x), :] = q2
        twice[i + 1] = e2
        return 0

    lax.fori_loop(0, cells_x, second_sweep, 0, unroll=ROW_UNROLL)
    above, twice[0] = sweep(once, DEEP - 1)
    below, twice[cells_x + 1] = sweep(once, cells_x + DEEP)

    def row(i):
        if i < 0:
            return above
        if i >= cells_x:
            return below
        return moved_ref[pl.ds(i, chans, stride=cells_x), :]

    for q in range(2):
        base = q * half

        def gather(l, carry):
            aw, ae = carry
            e2 = twice[base + l]
            aw = jnp.where(lane == l, pltpu.roll(e2, lax.rem(l + 1, width), 1), aw)
            ae = jnp.where(lane == l, pltpu.roll(e2, l, 1), ae)
            return aw, ae

        zero = jnp.zeros((chans, width), F32)
        aw, ae = lax.fori_loop(0, half + 2, gather, (zero, zero), unroll=2)
        items = (row(base - 1), row(base + half), aw, ae, row(base + part))
        for k in range(EXTRA):
            extra[q, pl.ds(k, chans, stride=EXTRA), :] = items[k] if k < len(items) else zero

    for c in range(chans):
        for dst0, dst1, q in ((mine0, mine1, own), (theirs0, theirs1, 1 - own)):
            start = pl.multiple_of(c * cells_x + q * half, 8)
            dst0[c, 0:EXTRA] = extra[q, pl.ds(c * EXTRA, EXTRA), :].astype(BF16)
            dst0[c, EXTRA : EXTRA + part] = moved_ref[pl.ds(start, part), :].astype(BF16)
            dst1[c] = moved_ref[pl.ds(start + part, part), :].astype(BF16)


def physics_kernel(chunk, table_ref, w1_ref, w2_ref, w3_ref, *rest):
    count = 2 if chunk == 0 else 4
    ins, rest = rest[:count], rest[count:]
    own_out, other_out, wide0, wide1, slab, packed, mask, table, stacked, terms, sem = rest
    chans, part, width = own_out.shape
    half = 2 * part
    pad = slab.shape[1] // 2
    both = 2 * pad
    own = lax.axis_index("group")
    top = own * half + chunk * part
    copies = []
    for n, k in enumerate((5, 7)):
        copies.append(
            pltpu.make_async_copy(table_ref.at[k, 0, pl.ds(top, part)], table.at[n], sem.at[n])
        )
        copies[-1].start()
    height0 = EXTRA + part
    for s in range(2):
        wide0[s] = ins[s][...].reshape(chans * height0, width).astype(F32)
        if chunk:
            wide1[s] = ins[2 + s][...].reshape(chans * part, width).astype(F32)

    slab[...] = jnp.zeros_like(slab)

    def source(s, l):
        if chunk == 0:
            if l < 0:
                return wide0[s, pl.ds(0, chans, stride=height0), :]
            if l >= part:
                return wide0[s, pl.ds(4, chans, stride=height0), :]
            return wide0[s, pl.ds(EXTRA + l, chans, stride=height0), :]
        if l < 0:
            return wide0[s, pl.ds(height0 - 1, chans, stride=height0), :]
        if l >= part:
            return wide0[s, pl.ds(1, chans, stride=height0), :]
        return wide1[s, pl.ds(l, chans, stride=part), :]

    for s in range(2):
        for l in range(-1, part + 1):
            slab[l + 1, pl.ds(s * pad, chans)] = source(s, l)
        for k in range(2):
            slab[part + 2 + k, pl.ds(s * pad, chans)] = wide0[s, pl.ds(2 + k, chans, stride=height0), :]

    lane = lanes_of((both, width))

    def shift(r, _):
        q = slab[r]
        idx = r + chunk * part
        low = jnp.where(lane == 0, pltpu.roll(slab[part + 2], lax.rem(width - idx, width), 1), pltpu.roll(q, 1, 1))
        high = jnp.where(lane == width - 1, pltpu.roll(slab[part + 3], lax.rem(2 * width - 1 - idx, width), 1), pltpu.roll(q, width - 1, 1))
        packed[0, r] = low.astype(BF16)
        packed[1, r] = q.astype(BF16)
        packed[2, r] = high.astype(BF16)
        return 0

    lax.fori_loop(0, part + 2, shift, 0, unroll=2)
    for copy in copies:
        copy.wait()
    rows_i = lax.broadcasted_iota(jnp.int32, (part, width), 0) + top
    centre = (rows_i + 1) * (width + 2) + lanes_of((part, width)) + 1
    along_y = table[0] - centre
    along_x = table[1] - centre
    turned = jnp.abs(along_x) == 1
    mask[0] = jnp.where(jnp.where(turned, along_y, along_x) < 0, 1.0, 0.0)
    mask[1] = jnp.where(jnp.where(turned, along_x, along_y) < 0, 1.0, 0.0)
    mask[2] = jnp.where(turned, 1.0, 0.0)

    rows_step = stacked.shape[1] // width

    def choose(m, a, b):
        return jnp.where(m, a, b), jnp.where(m, b, a)

    def block(b, _):
        for u in range(rows_step):
            l = b * rows_step + u
            m = []
            for n in range(3):
                line = jnp.broadcast_to(mask[n, pl.ds(l, 1), :], (16, width)).astype(BF16)
                m.append(jnp.concatenate([line] * (both // 16), axis=0) > 0.5)
            x = [[packed[bb, l + aa] for bb in range(3)] for aa in range(3)]
            for bb in range(3):
                x[0][bb], x[2][bb] = choose(m[0], x[2][bb], x[0][bb])
            for aa in range(3):
                x[aa][0], x[aa][2] = choose(m[1], x[aa][2], x[aa][0])
            for aa, bb in ((0, 1), (0, 2), (1, 2)):
                x[aa][bb], x[bb][aa] = choose(m[2], x[bb][aa], x[aa][bb])
            for k in range(9):
                stacked[pl.ds(k * both, both), pl.ds(u * width, width)] = x[k // 3][k % 3]
        dot = functools.partial(
            lax.dot_general,
            dimension_numbers=(((1,), (0,)), ((), ())),
            preferred_element_type=F32,
        )

        def silu(v):
            h = v * 0.5
            return (h * jnp.tanh(h) + h).astype(BF16)

        first = silu(dot(w1_ref[...], stacked[...]))
        second = silu(dot(w2_ref[...], first))
        tend = dot(w3_ref[...], second)
        for u in range(rows_step):
            l = b * rows_step + u
            cols = slice(u * width, (u + 1) * width)
            terms[0, pl.ds(l, chans, stride=part), :] = tend[0:chans, cols]
            terms[1, pl.ds(l, chans, stride=part), :] = tend[pad : pad + chans, cols]
        return 0

    lax.fori_loop(0, part // rows_step, block, 0)
    own_out[...] = terms[0].reshape(chans, part, width).astype(BF16)
    other_out[...] = terms[1].reshape(chans, part, width).astype(BF16)


def finish_kernel(moved_ref, a0, a1, b0, b1, out_ref):
    chans, part, width = a0.shape
    own = lax.axis_index("group")
    for q, pair in ((own, (a0, a1)), (1 - own, (b0, b1))):
        for n in range(2):
            rows = pl.ds(pl.multiple_of(q * 2 * part + n * part, 8), part)
            out_ref[:, rows, :] = moved_ref[:, rows, :] + pair[n][...].astype(F32)


def call(kernel, name, outs, ins, scratch=(), **cost):
    return pl.pallas_call(
        kernel,
        out_shape=outs,
        in_specs=ins,
        out_specs=jax.tree.map(lambda _: VMEM_SPEC, outs),
        scratch_shapes=list(scratch),
        compiler_params=PARAMS,
        name=name,
    )


def shards(state, courant_x, courant_y, diffusion, neighbours, w_in, w_mid, w_out):
    levels, fields, single, cells_x, cells_y = state.shape
    chans = levels * fields
    hidden = w_mid.shape[0]
    tiles = lax.axis_size("tile")
    half, part = cells_x // 2, cells_x // 4
    pad = -(-chans // 8) * 8
    block = state.reshape(chans, cells_x, cells_y)
    sds = jax.ShapeDtypeStruct

    strip = sds((chans, 8, cells_y), BF16)
    to_east, to_west, rows = call(
        edge_kernel, "edges", (strip, strip, sds((chans, 16, cells_y), BF16)), [VMEM_SPEC]
    )(block)

    def beside(by):
        return [(i, i + by) for i in range(tiles) if 0 <= i % TILE_ROWS + by < TILE_ROWS]

    from_west = lax.ppermute(to_east, "tile", beside(1))
    from_east = lax.ppermute(to_west, "tile", beside(-1))
    message = jnp.concatenate([rows, from_west, from_east], axis=1)

    def across(x, by):
        return lax.ppermute(x, "tile", [(i, (i + by) % tiles) for i in range(tiles)])

    up = across(message, TILE_ROWS)
    down = up if tiles == 2 * TILE_ROWS else across(message, -TILE_ROWS)

    ax = jnp.repeat(courant_x, fields)
    ay = jnp.repeat(courant_y, fields)
    nu = jnp.tile(diffusion, levels)
    coef = jnp.stack(
        [
            1.0 - jnp.abs(ax) - jnp.abs(ay) - 4.0 * nu,
            jnp.maximum(ax, 0.0) + nu,
            nu - jnp.minimum(ax, 0.0),
            jnp.maximum(ay, 0.0) + nu,
            nu - jnp.minimum(ay, 0.0),
        ]
    )
    coef = jnp.broadcast_to(coef[:, :, None], (5, chans, cells_y))

    def flat(x):
        return x.reshape(-1, cells_y)

    def split(x):
        return flat(x[:, 0:16]), flat(x[:, 16:24]), flat(x[:, 24:32])

    win0 = sds((chans, EXTRA + part, cells_y), BF16)
    win1 = sds((chans, part, cells_y), BF16)
    slabs = pltpu.VMEM((cells_x + 2 * DEEP, 2, chans, cells_y), F32)
    moved, mine0, mine1, theirs0, theirs1 = call(
        functools.partial(transport_kernel, cells_x=cells_x),
        "transport",
        (sds((chans * cells_x, cells_y), F32), win0, win1, win0, win1),
        [VMEM_SPEC] * 10,
        [
            slabs,
            slabs,
            pltpu.VMEM((cells_x + 2, chans, cells_y), F32),
            pltpu.VMEM((3, 2, chans * 8, cells_y), F32),
            pltpu.VMEM((2, chans * 16, cells_y), F32),
            pltpu.VMEM((2, chans * EXTRA, cells_y), F32),
        ],
    )(block.reshape(chans * cells_x, cells_y), coef, flat(from_west), flat(from_east), *split(up), *split(down))

    def swap(x):
        return lax.ppermute(x, "group", [(0, 1), (1, 0)])

    got0 = swap(theirs0)
    got1 = swap(theirs1)

    own = lax.axis_index("group")
    both = 2 * pad

    def ordered(w):
        return jnp.where(own == 0, w, w[::-1])

    w1 = ordered(w_in.reshape(2, chans, 9, hidden)).transpose(3, 2, 0, 1)
    w1 = jnp.pad(w1, ((0, 0), (0, 0), (0, 0), (0, pad - chans))).reshape(hidden, 9 * both)
    w3 = ordered(w_out.T.reshape(2, chans, hidden))
    w3 = jnp.pad(w3, ((0, 0), (0, pad - chans), (0, 0))).reshape(both, hidden)
    w2 = w_mid.T

    def physics(chunk, *windows):
        return call(
            functools.partial(physics_kernel, chunk),
            f"physics{chunk}",
            (win1, win1),
            [ANY_SPEC] + [VMEM_SPEC] * (3 + len(windows)),
            [
                pltpu.VMEM((2, chans * (EXTRA + part), cells_y), F32),
                pltpu.VMEM((2, chans * part, cells_y), F32),
                pltpu.VMEM((part + 4, both, cells_y), F32),
                pltpu.VMEM((3, part + 2, both, cells_y), BF16),
                pltpu.VMEM((3, part, cells_y), F32),
                pltpu.VMEM((2, part, cells_y), jnp.int32),
                pltpu.VMEM((9 * both, 16 * cells_y), BF16),
                pltpu.VMEM((2, chans * part, cells_y), F32),
                pltpu.SemaphoreType.DMA((2,)),
            ],
        )(neighbours, w1, w2, w3, *windows)

    own0, other0 = physics(0, mine0, got0)
    back0 = swap(other0)
    own1, other1 = physics(1, mine0, got0, mine1, got1)
    back1 = swap(other1)
    updated = call(
        finish_kernel, "finish", sds((chans, cells_x, cells_y), F32), [VMEM_SPEC] * 5
    )(moved.reshape(chans, cells_x, cells_y), own0, own1, back0, back1)
    return updated.reshape(levels, fields, single, cells_x, cells_y)


def solution(mesh):
    return jax.shard_map(
        shards,
        mesh=mesh,
        in_specs=(
            P("group", None, "tile", None, None),
            P("group"),
            P("group"),
            P(),
            P(None, "tile", None, None),
            P(),
            P(),
            P(),
        ),
        out_specs=P("group", None, "tile", None, None),
        check_vma=False,
    )
```

```python
import functools

import jax
import jax.numpy as jnp
from jax import lax
from jax.experimental import pallas as pl
from jax.experimental.pallas import tpu as pltpu
from jax.sharding import PartitionSpec as P

TILE_ROWS = 8
DEEP = 3
EXTRA = 16
ROW_UNROLL = 7

F32 = jnp.float32
BF16 = jnp.bfloat16
VMEM_SPEC = pl.BlockSpec(memory_space=pltpu.VMEM)
ANY_SPEC = pl.BlockSpec(memory_space=pl.ANY)
PARAMS = pltpu.CompilerParams(vmem_limit_bytes=56 << 20)


def whole(ref):
    return ref[...]


def lanes_of(shape):
    return lax.broadcasted_iota(jnp.int32, shape, len(shape) - 1)


def edge_kernel(state_ref, east_ref, west_ref, rows_ref):
    chans, cells_x, cells_y = state_ref.shape
    slot = lax.broadcasted_iota(jnp.int32, (16, cells_y), 0)
    lane = lanes_of((16, cells_y))
    wanted = jnp.where(slot < 8, slot + cells_y - DEEP, slot - 8)
    valid = (slot % 8) < DEEP
    pick = jnp.where(valid & (lane == wanted), 1.0, 0.0).astype(BF16)
    for c in range(chans):
        block = state_ref[c].astype(BF16)
        strips = lax.dot_general(
            pick, block, (((1,), (1,)), ((), ())), preferred_element_type=F32
        ).astype(BF16)
        east_ref[c] = strips[0:8]
        west_ref[c] = strips[8:16]
        rows_ref[c] = jnp.concatenate(
            [state_ref[c, 0:8], state_ref[c, cells_x - 8 : cells_x]], axis=0
        ).astype(BF16)


def transport_kernel(
    state_ref, coef_ref, here_ref, up_ref, down_ref,
    moved_ref, mine0, mine1, theirs0, theirs1, border, extra, *, cells_x,
):
    chans = state_ref.shape[0] // cells_x
    width = state_ref.shape[1]
    half = cells_x // 2
    part = half // 2
    message = here_ref.shape[0] // chans
    own = lax.axis_index("group")
    place = lax.axis_index("tile") % TILE_ROWS
    lane = lanes_of((chans, width))
    first, last = lane == 0, lane == width - 1
    low_lanes = lane < width // 2
    for s, ref in enumerate((here_ref, up_ref, down_ref)):
        border[s] = ref[...].astype(F32)
    coefs = [coef_ref[n] for n in range(5)]

    def line(s, k):
        return border[s, pl.ds(k, chans, stride=message), :]

    def pair(k):
        return line(0, k), jnp.where(low_lanes, line(2, k), line(1, k))

    def roll(x, by):
        return pltpu.roll(x, by, 1)

    def both_ways(main, aux):
        ml, al = roll(main, 1), roll(aux, 1)
        mu, au = roll(main, width - 1), roll(aux, width - 1)
        lower = jnp.where(first, al, ml), jnp.where(first, ml, al)
        upper = jnp.where(last, au, mu), jnp.where(last, mu, au)
        return lower, upper

    def stencil(q, xl, xu, yl, yu):
        c0, cxl, cxu, cyl, cyu = coefs
        return c0 * q + cxl * xl + cxu * xu + cyl * yl + cyu * yu

    def column(west, mid, east, keep):
        lower, upper = both_ways(*mid)
        return tuple(
            stencil(mid[n], lower[n], upper[n], west[n], east[n]) * keep for n in range(2)
        )

    keeps = (
        jnp.where(place == 0, 0.0, 1.0),
        jnp.where(place == TILE_ROWS - 1, 0.0, 1.0),
    )
    edges = []
    for side in range(2):
        raw = [pair(16 + 8 * side + k) for k in range(5)]
        keep = keeps[side]
        inside = 3 if side == 0 else 1
        once = [
            column(raw[k - 1], raw[k], raw[k + 1], 1.0 if k == inside else keep)
            for k in (1, 2, 3)
        ]
        edges.append((raw[2], once[1], column(once[0], once[1], once[2], keep)))

    for q in range(2):
        for side in range(2):
            main, aux = edges[side][2]
            if q == 0:
                lineup = jnp.where(first, roll(aux, 1), roll(main, 1))
            else:
                by = width - half + 1
                lineup = jnp.where(lane <= half, roll(main, by), roll(aux, by))
            extra[q, pl.ds(2 + side, chans, stride=EXTRA), :] = lineup

    def sweep(level, i, q, xl, xu, aux=False):
        west, east = edges[0][level][int(aux)], edges[1][level][int(aux)]
        if isinstance(i, int):
            to_first, to_last = -i % width, (width - 1 - i) % width
        else:
            to_first, to_last = lax.rem(width - i, width), width - 1 - i
        yl = jnp.where(first, roll(west, to_first), roll(q, 1))
        yu = jnp.where(last, roll(east, to_last), roll(q, width - 1))
        return stencil(q, xl, xu, yl, yu)

    def raw(i):
        if isinstance(i, int) and i < 0:
            return line(1, 16 + i)
        if isinstance(i, int) and i >= cells_x:
            return line(2, i - cells_x)
        return state_ref[pl.ds(i, chans, stride=cells_x), :]

    def outside(i):
        return isinstance(i, int) and not 0 <= i < cells_x

    def step(i, carry):
        r0, r1, o0, o1 = carry
        r2 = raw(i + 2)
        o2 = sweep(0, i + 1, r1, r0, r2, outside(i + 1))
        moved = sweep(1, i, o1, o0, o2, outside(i))
        return moved, (r1, r2, o1, o2)

    def put(i, moved):
        moved_ref[pl.ds(i, chans, stride=cells_x), :] = moved

    ra, rb, rc, rd = raw(-3), raw(-2), raw(-1), raw(0)
    carry = (rc, rd, sweep(0, -2, rb, ra, rc, True), sweep(0, -1, rc, rb, rd, True))
    above, carry = step(-1, carry)

    def rows(n, carry):
        for u in range(ROW_UNROLL):
            i = n * ROW_UNROLL + u
            moved, carry = step(i, carry)
            put(i, moved)
        return carry

    steps = (cells_x - 2) // ROW_UNROLL
    carry = lax.fori_loop(0, steps, rows, carry)
    for i in range(steps * ROW_UNROLL, cells_x):
        moved, carry = step(i, carry)
        put(i, moved)
    below, _ = step(cells_x, carry)

    def row(i):
        if i < 0:
            return above
        if i >= cells_x:
            return below
        return moved_ref[pl.ds(i, chans, stride=cells_x), :]

    zero = jnp.zeros((chans, width), F32)
    for q in range(2):
        base = q * half
        items = {0: row(base - 1), 1: row(base + half), 4: row(base + part)}
        for k in range(EXTRA):
            if k not in (2, 3):
                extra[q, pl.ds(k, chans, stride=EXTRA), :] = items.get(k, zero)

    for c in range(chans):
        for dst0, dst1, q in ((mine0, mine1, own), (theirs0, theirs1, 1 - own)):
            start = pl.multiple_of(c * cells_x + q * half, 8)
            dst0[c, 0:EXTRA] = extra[q, pl.ds(c * EXTRA, EXTRA), :].astype(BF16)
            dst0[c, EXTRA : EXTRA + part] = moved_ref[pl.ds(start, part), :].astype(BF16)
            dst1[c] = moved_ref[pl.ds(start + part, part), :].astype(BF16)


def physics_kernel(chunk, table_ref, w1_ref, w2_ref, w3_ref, *rest):
    count = 2 if chunk == 0 else 4
    ins, rest = rest[:count], rest[count + (chunk > 0) :]
    own_out, other_out, wide0, wide1, slab, packed, mask, table, stacked, terms, sem = rest
    chans, part, width = own_out.shape
    half = 2 * part
    pad = slab.shape[1] // 2
    both = 2 * pad
    own = lax.axis_index("group")
    top = own * half + chunk * part
    copies = []
    for n, k in enumerate((5, 7)):
        copies.append(
            pltpu.make_async_copy(table_ref.at[k, 0, pl.ds(top, part)], table.at[n], sem.at[n])
        )
        copies[-1].start()
    height0 = EXTRA + part
    for s in range(2):
        wide0[s] = ins[s][...].reshape(chans * height0, width).astype(F32)
        if chunk:
            wide1[s] = ins[2 + s][...].reshape(chans * part, width).astype(F32)

    slab[...] = jnp.zeros_like(slab)

    def source(s, l):
        if chunk == 0:
            if l < 0:
                return wide0[s, pl.ds(0, chans, stride=height0), :]
            if l >= part:
                return wide0[s, pl.ds(4, chans, stride=height0), :]
            return wide0[s, pl.ds(EXTRA + l, chans, stride=height0), :]
        if l < 0:
            return wide0[s, pl.ds(height0 - 1, chans, stride=height0), :]
        if l >= part:
            return wide0[s, pl.ds(1, chans, stride=height0), :]
        return wide1[s, pl.ds(l, chans, stride=part), :]

    for s in range(2):
        for l in range(-1, part + 1):
            slab[l + 1, pl.ds(s * pad, chans)] = source(s, l)
        for k in range(2):
            slab[part + 2 + k, pl.ds(s * pad, chans)] = wide0[s, pl.ds(2 + k, chans, stride=height0), :]

    lane = lanes_of((both, width))

    def shift(r, _):
        q = slab[r]
        idx = r + chunk * part
        low = jnp.where(lane == 0, pltpu.roll(slab[part + 2], lax.rem(width - idx, width), 1), pltpu.roll(q, 1, 1))
        high = jnp.where(lane == width - 1, pltpu.roll(slab[part + 3], lax.rem(2 * width - 1 - idx, width), 1), pltpu.roll(q, width - 1, 1))
        packed[0, r] = low.astype(BF16)
        packed[1, r] = q.astype(BF16)
        packed[2, r] = high.astype(BF16)
        return 0

    lax.fori_loop(0, part + 2, shift, 0, unroll=2)
    for copy in copies:
        copy.wait()
    rows_i = lax.broadcasted_iota(jnp.int32, (part, width), 0) + top
    centre = (rows_i + 1) * (width + 2) + lanes_of((part, width)) + 1
    along_y = table[0] - centre
    along_x = table[1] - centre
    turned = jnp.abs(along_x) == 1
    mask[0] = jnp.where(jnp.where(turned, along_y, along_x) < 0, 1.0, 0.0)
    mask[1] = jnp.where(jnp.where(turned, along_x, along_y) < 0, 1.0, 0.0)
    mask[2] = jnp.where(turned, 1.0, 0.0)

    rows_step = stacked.shape[1] // width

    def choose(m, a, b):
        return jnp.where(m, a, b), jnp.where(m, b, a)

    def block(b, _):
        for u in range(rows_step):
            l = b * rows_step + u
            m = []
            for n in range(3):
                line = jnp.broadcast_to(mask[n, pl.ds(l, 1), :], (16, width)).astype(BF16)
                m.append(jnp.concatenate([line] * (both // 16), axis=0) > 0.5)
            x = [[packed[bb, l + aa] for bb in range(3)] for aa in range(3)]
            for bb in range(3):
                x[0][bb], x[2][bb] = choose(m[0], x[2][bb], x[0][bb])
            for aa in range(3):
                x[aa][0], x[aa][2] = choose(m[1], x[aa][2], x[aa][0])
            for aa, bb in ((0, 1), (0, 2), (1, 2)):
                x[aa][bb], x[bb][aa] = choose(m[2], x[bb][aa], x[aa][bb])
            for k in range(9):
                stacked[pl.ds(k * both, both), pl.ds(u * width, width)] = x[k // 3][k % 3]
        dot = functools.partial(
            lax.dot_general,
            dimension_numbers=(((1,), (0,)), ((), ())),
            preferred_element_type=F32,
        )

        def silu(v):
            h = v * 0.5
            return (h * jnp.tanh(h) + h).astype(BF16)

        first = silu(dot(w1_ref[...], stacked[...]))
        second = silu(dot(w2_ref[...], first))
        tend = dot(w3_ref[...], second)
        for u in range(rows_step):
            l = b * rows_step + u
            cols = slice(u * width, (u + 1) * width)
            terms[0, pl.ds(l, chans, stride=part), :] = tend[0:chans, cols]
            terms[1, pl.ds(l, chans, stride=part), :] = tend[pad : pad + chans, cols]
        return 0

    lax.fori_loop(0, part // rows_step, block, 0)
    own_out[...] = terms[0].reshape(chans, part, width).astype(BF16)
    other_out[...] = terms[1].reshape(chans, part, width).astype(BF16)


def finish_kernel(moved_ref, a0, a1, b0, b1, out_ref):
    chans, part, width = a0.shape
    own = lax.axis_index("group")
    for q, pair in ((own, (a0, a1)), (1 - own, (b0, b1))):
        for n in range(2):
            rows = pl.ds(pl.multiple_of(q * 2 * part + n * part, 8), part)
            out_ref[:, rows, :] = moved_ref[:, rows, :] + pair[n][...].astype(F32)


def call(kernel, name, outs, ins, scratch=(), **cost):
    return pl.pallas_call(
        kernel,
        out_shape=outs,
        in_specs=ins,
        out_specs=jax.tree.map(lambda _: VMEM_SPEC, outs),
        scratch_shapes=list(scratch),
        compiler_params=PARAMS,
        name=name,
    )


def shards(state, courant_x, courant_y, diffusion, neighbours, w_in, w_mid, w_out):
    levels, fields, single, cells_x, cells_y = state.shape
    chans = levels * fields
    hidden = w_mid.shape[0]
    tiles = lax.axis_size("tile")
    half, part = cells_x // 2, cells_x // 4
    pad = -(-chans // 8) * 8
    block = state.reshape(chans, cells_x, cells_y)
    sds = jax.ShapeDtypeStruct

    strip = sds((chans, 8, cells_y), BF16)
    to_east, to_west, rows = call(
        edge_kernel, "edges", (strip, strip, sds((chans, 16, cells_y), BF16)), [VMEM_SPEC]
    )(block)

    def beside(by):
        return [(i, i + by) for i in range(tiles) if 0 <= i % TILE_ROWS + by < TILE_ROWS]

    from_west = lax.ppermute(to_east, "tile", beside(1))
    from_east = lax.ppermute(to_west, "tile", beside(-1))
    spare = jnp.zeros((chans, 3, cells_y), BF16)
    message = jnp.concatenate(
        [rows, from_west[:, :3], to_west[:, :2], spare, to_east[:, 1:3], from_east[:, :3], spare],
        axis=1,
    )

    def across(x, by):
        return lax.ppermute(x, "tile", [(i, (i + by) % tiles) for i in range(tiles)])

    up = across(message, TILE_ROWS)
    down = up if tiles == 2 * TILE_ROWS else across(message, -TILE_ROWS)

    ax = jnp.repeat(courant_x, fields)
    ay = jnp.repeat(courant_y, fields)
    nu = jnp.tile(diffusion, levels)
    coef = jnp.stack(
        [
            1.0 - jnp.abs(ax) - jnp.abs(ay) - 4.0 * nu,
            jnp.maximum(ax, 0.0) + nu,
            nu - jnp.minimum(ax, 0.0),
            jnp.maximum(ay, 0.0) + nu,
            nu - jnp.minimum(ay, 0.0),
        ]
    )
    coef = jnp.broadcast_to(coef[:, :, None], (5, chans, cells_y))

    def flat(x):
        return x.reshape(-1, cells_y)

    win0 = sds((chans, EXTRA + part, cells_y), BF16)
    win1 = sds((chans, part, cells_y), BF16)
    moved, mine0, mine1, theirs0, theirs1 = call(
        functools.partial(transport_kernel, cells_x=cells_x),
        "transport",
        (sds((chans * cells_x, cells_y), F32), win0, win1, win0, win1),
        [VMEM_SPEC] * 5,
        [
            pltpu.VMEM((3, chans * message.shape[1], cells_y), F32),
            pltpu.VMEM((2, chans * EXTRA, cells_y), F32),
        ],
    )(flat(block), coef, flat(message), flat(up), flat(down))

    def swap(x):
        return lax.ppermute(x, "group", [(0, 1), (1, 0)])

    got0 = swap(theirs0)
    got1 = swap(theirs1)

    own = lax.axis_index("group")
    both = 2 * pad

    def ordered(w):
        return jnp.where(own == 0, w, w[::-1])

    w1 = ordered(w_in.reshape(2, chans, 9, hidden)).transpose(3, 2, 0, 1)
    w1 = jnp.pad(w1, ((0, 0), (0, 0), (0, 0), (0, pad - chans))).reshape(hidden, 9 * both)
    w3 = ordered(w_out.T.reshape(2, chans, hidden))
    w3 = jnp.pad(w3, ((0, 0), (0, pad - chans), (0, 0))).reshape(both, hidden)
    w2 = w_mid.T

    def physics(chunk, *windows):
        return call(
            functools.partial(physics_kernel, chunk),
            f"physics{chunk}",
            (win1, win1),
            [ANY_SPEC] + [VMEM_SPEC] * (3 + 2 + 2 * chunk) + [ANY_SPEC] * chunk,
            [
                pltpu.VMEM((2, chans * (EXTRA + part), cells_y), F32),
                pltpu.VMEM((2, chans * part, cells_y), F32),
                pltpu.VMEM((part + 4, both, cells_y), F32),
                pltpu.VMEM((3, part + 2, both, cells_y), BF16),
                pltpu.VMEM((3, part, cells_y), F32),
                pltpu.VMEM((2, part, cells_y), jnp.int32),
                pltpu.VMEM((9 * both, 16 * cells_y), BF16),
                pltpu.VMEM((2, chans * part, cells_y), F32),
                pltpu.SemaphoreType.DMA((2,)),
            ],
        )(neighbours, w1, w2, w3, *windows)

    own0, other0 = physics(0, mine0, got0)
    back0 = swap(other0)
    own1, other1 = physics(1, mine0, got0, mine1, got1, own0)
    back1 = swap(other1)
    updated = call(
        finish_kernel, "finish", sds((chans, cells_x, cells_y), F32), [VMEM_SPEC] * 5
    )(moved.reshape(chans, cells_x, cells_y), own0, own1, back0, back1)
    return updated.reshape(levels, fields, single, cells_x, cells_y)


def solution(mesh):
    return jax.shard_map(
        shards,
        mesh=mesh,
        in_specs=(
            P("group", None, "tile", None, None),
            P("group"),
            P("group"),
            P(),
            P(None, "tile", None, None),
            P(),
            P(),
            P(),
        ),
        out_specs=P("group", None, "tile", None, None),
        check_vma=False,
    )
```

```python
import functools

import jax
import jax.numpy as jnp
from jax import lax
from jax.experimental import pallas as pl
from jax.experimental.pallas import tpu as pltpu
from jax.sharding import PartitionSpec as P

TILE_ROWS = 8
DEEP = 3
EXTRA = 16
MARGIN = 16
GROUP = 4

F32 = jnp.float32
BF16 = jnp.bfloat16
VMEM_SPEC = pl.BlockSpec(memory_space=pltpu.VMEM)
ANY_SPEC = pl.BlockSpec(memory_space=pl.ANY)
PARAMS = pltpu.CompilerParams(vmem_limit_bytes=56 << 20)


def whole(ref):
    return ref[...]


def lanes_of(shape):
    return lax.broadcasted_iota(jnp.int32, shape, len(shape) - 1)


def edge_kernel(state_ref, east_ref, west_ref, rows_ref):
    chans, cells_x, cells_y = state_ref.shape
    slot = lax.broadcasted_iota(jnp.int32, (16, cells_y), 0)
    lane = lanes_of((16, cells_y))
    wanted = jnp.where(slot < 8, slot + cells_y - DEEP, slot - 8)
    valid = (slot % 8) < DEEP
    pick = jnp.where(valid & (lane == wanted), 1.0, 0.0).astype(BF16)
    for c in range(chans):
        block = state_ref[c].astype(BF16)
        strips = lax.dot_general(
            pick, block, (((1,), (1,)), ((), ())), preferred_element_type=F32
        ).astype(BF16)
        east_ref[c] = strips[0:8]
        west_ref[c] = strips[8:16]
        rows_ref[c] = jnp.concatenate(
            [state_ref[c, 0:8], state_ref[c, cells_x - 8 : cells_x]], axis=0
        ).astype(BF16)


def shift_matrix(width):
    k = lax.broadcasted_iota(jnp.int32, (4 * width, 2 * width), 0)
    n = lax.broadcasted_iota(jnp.int32, (4 * width, 2 * width), 1)
    m = k % width
    lower = (n < width) & (n == m + 1)
    upper = (n >= width) & (n - width == m - 1)
    west = (k >= 2 * width) & (k < 3 * width) & (n == 0)
    east = (k >= 3 * width) & (n == 2 * width - 1)
    return jnp.where(((k < 2 * width) & (lower | upper)) | west | east, 1.0, 0.0).astype(BF16)


def transport_kernel(
    state_ref, speed_ref, coef_ref, here_ref, up_ref, down_ref,
    moved_ref, mine0, mine1, theirs0, theirs1,
    border, extra, raw_s, once_s, last_s, line_s, matrix, sem, *, chans,
):
    cells_x, width = state_ref.shape[1:]
    half = cells_x // 2
    part = half // 2
    message = here_ref.shape[0] // chans
    own = lax.axis_index("group")
    place = lax.axis_index("tile") % TILE_ROWS
    fetch = pltpu.make_async_copy(state_ref, raw_s.at[:, pl.ds(MARGIN, cells_x)], sem.at[0])
    fetch.start()
    lane = lanes_of((chans, width))
    first, last = lane == 0, lane == width - 1
    low_lanes = lane < width // 2
    for s, ref in enumerate((here_ref, up_ref, down_ref)):
        border[s] = ref[...].astype(F32)
    coefs = [coef_ref[n] for n in range(5)]
    matrix[...] = shift_matrix(width)

    def line(s, k):
        return border[s, pl.ds(k, chans, stride=message), :]

    def pair(k):
        return line(0, k), jnp.where(low_lanes, line(2, k), line(1, k))

    def roll(x, by):
        return pltpu.roll(x, by, 1)

    def both_ways(main, aux):
        ml, al = roll(main, 1), roll(aux, 1)
        mu, au = roll(main, width - 1), roll(aux, width - 1)
        lower = jnp.where(first, al, ml), jnp.where(first, ml, al)
        upper = jnp.where(last, au, mu), jnp.where(last, mu, au)
        return lower, upper

    def column(west, mid, east, keep):
        c0, cxl, cxu, cyl, cyu = coefs
        lower, upper = both_ways(*mid)
        return tuple(
            (c0 * mid[n] + cxl * lower[n] + cxu * upper[n] + cyl * west[n] + cyu * east[n]) * keep
            for n in range(2)
        )

    keeps = (
        jnp.where(place == 0, 0.0, 1.0),
        jnp.where(place == TILE_ROWS - 1, 0.0, 1.0),
    )
    for side in range(2):
        raw = [pair(16 + 8 * side + k) for k in range(5)]
        keep = keeps[side]
        inside = 3 if side == 0 else 1
        once = [
            column(raw[k - 1], raw[k], raw[k + 1], 1.0 if k == inside else keep)
            for k in (1, 2, 3)
        ]
        main, aux = column(once[0], once[1], once[2], keep)
        for level, edge in enumerate((raw[2], once[1])):
            for n in range(2):
                line_s[level, side, n] = edge[n]
        for q in range(2):
            if q == 0:
                lineup = jnp.where(first, roll(aux, 1), roll(main, 1))
            else:
                by = width - half + 1
                lineup = jnp.where(lane <= half, roll(main, by), roll(aux, by))
            extra[q, pl.ds(2 + side, chans, stride=EXTRA), :] = lineup

    rows = cells_x + 16
    at = lax.broadcasted_iota(jnp.int32, (rows, width), 0) - 8
    diagonal = (at + width) % width == lanes_of((rows, width))
    fetch.wait()

    group = next(n for n in (GROUP, 2, 1) if chans % n == 0)

    def sweep(level, src, dst, base):
        parts = []
        for g in range(group):
            c = base + g
            q = src[c, pl.ds(8, rows), :]
            hi = q.astype(BF16)
            lo = (q - hi.astype(F32)).astype(BF16)
            sides = []
            for side in range(2):
                main = line_s[level, side, 0, pl.ds(c, 1), :]
                aux = line_s[level, side, 1, pl.ds(c, 1), :]
                values = jnp.concatenate(
                    [
                        jnp.broadcast_to(aux, (8, width)),
                        jnp.broadcast_to(main, (cells_x, width)),
                        jnp.broadcast_to(aux, (8, width)),
                    ],
                    axis=0,
                )
                sides.append(jnp.where(diagonal, values, 0.0).astype(BF16))
            parts.append(jnp.concatenate([hi, lo] + sides, axis=1))
        near = lax.dot_general(
            jnp.concatenate(parts, axis=0),
            matrix[...],
            (((1,), (0,)), ((), ())),
            preferred_element_type=F32,
        )
        for g in range(group):
            c = base + g
            lower, upper = near[g * rows : (g + 1) * rows, :width], near[g * rows : (g + 1) * rows, width:]
            c0, cxl, cxu, cyl, cyu = [speed_ref[n, c] for n in range(5)]
            dst[c, pl.ds(8, rows), :] = (
                c0 * src[c, pl.ds(8, rows), :]
                + cxl * src[c, pl.ds(7, rows), :]
                + cxu * src[c, pl.ds(9, rows), :]
                + cyl * lower
                + cyu * upper
            )

    def finish(base):
        for g in range(group):
            c = base + g
            moved_ref[c] = last_s[c, pl.ds(MARGIN, cells_x), :]
            for q in range(2):
                for k, i in ((0, -1), (1, half), (4, part)):
                    extra[q, pl.ds(c * EXTRA + k, 1), :] = last_s[c, pl.ds(MARGIN + q * half + i, 1), :]
            for dst0, dst1, q in ((mine0, mine1, own), (theirs0, theirs1, 1 - own)):
                start = pl.multiple_of(MARGIN + q * half, 8)
                dst0[c, 0:EXTRA] = extra[q, pl.ds(c * EXTRA, EXTRA), :].astype(BF16)
                dst0[c, EXTRA : EXTRA + part] = last_s[c, pl.ds(start, part), :].astype(BF16)
                dst1[c] = last_s[c, pl.ds(start + part, part), :].astype(BF16)

    for c in range(chans):
        raw_s[c, pl.ds(MARGIN - DEEP, DEEP), :] = border[1, pl.ds(c * message + 16 - DEEP, DEEP), :]
        raw_s[c, pl.ds(MARGIN + cells_x, DEEP), :] = border[2, pl.ds(c * message, DEEP), :]
    for base in range(0, chans + group, group):
        if base < chans:
            sweep(0, raw_s, once_s, base)
        if base:
            sweep(1, once_s, last_s, base - group)
            finish(base - group)


def physics_kernel(chunk, table_ref, w1_ref, w2_ref, w3_ref, *rest):
    count = 2 if chunk == 0 else 4
    ins, rest = rest[:count], rest[count + (chunk > 0) :]
    own_out, other_out, wide0, wide1, slab, packed, mask, table, stacked, terms, sem = rest
    chans, part, width = own_out.shape
    half = 2 * part
    pad = slab.shape[1] // 2
    both = 2 * pad
    own = lax.axis_index("group")
    top = own * half + chunk * part
    copies = []
    for n, k in enumerate((5, 7)):
        copies.append(
            pltpu.make_async_copy(table_ref.at[k, 0, pl.ds(top, part)], table.at[n], sem.at[n])
        )
        copies[-1].start()
    height0 = EXTRA + part
    for s in range(2):
        wide0[s] = ins[s][...].reshape(chans * height0, width).astype(F32)
        if chunk:
            wide1[s] = ins[2 + s][...].reshape(chans * part, width).astype(F32)

    slab[...] = jnp.zeros_like(slab)

    def source(s, l):
        if chunk == 0:
            if l < 0:
                return wide0[s, pl.ds(0, chans, stride=height0), :]
            if l >= part:
                return wide0[s, pl.ds(4, chans, stride=height0), :]
            return wide0[s, pl.ds(EXTRA + l, chans, stride=height0), :]
        if l < 0:
            return wide0[s, pl.ds(height0 - 1, chans, stride=height0), :]
        if l >= part:
            return wide0[s, pl.ds(1, chans, stride=height0), :]
        return wide1[s, pl.ds(l, chans, stride=part), :]

    for s in range(2):
        for l in range(-1, part + 1):
            slab[l + 1, pl.ds(s * pad, chans)] = source(s, l)
        for k in range(2):
            slab[part + 2 + k, pl.ds(s * pad, chans)] = wide0[s, pl.ds(2 + k, chans, stride=height0), :]

    lane = lanes_of((both, width))

    def shift(r, _):
        q = slab[r]
        idx = r + chunk * part
        low = jnp.where(lane == 0, pltpu.roll(slab[part + 2], lax.rem(width - idx, width), 1), pltpu.roll(q, 1, 1))
        high = jnp.where(lane == width - 1, pltpu.roll(slab[part + 3], lax.rem(2 * width - 1 - idx, width), 1), pltpu.roll(q, width - 1, 1))
        packed[0, r] = low.astype(BF16)
        packed[1, r] = q.astype(BF16)
        packed[2, r] = high.astype(BF16)
        return 0

    lax.fori_loop(0, part + 2, shift, 0, unroll=2)
    for copy in copies:
        copy.wait()
    rows_i = lax.broadcasted_iota(jnp.int32, (part, width), 0) + top
    centre = (rows_i + 1) * (width + 2) + lanes_of((part, width)) + 1
    along_y = table[0] - centre
    along_x = table[1] - centre
    turned = jnp.abs(along_x) == 1
    mask[0] = jnp.where(jnp.where(turned, along_y, along_x) < 0, 1.0, 0.0)
    mask[1] = jnp.where(jnp.where(turned, along_x, along_y) < 0, 1.0, 0.0)
    mask[2] = jnp.where(turned, 1.0, 0.0)

    rows_step = stacked.shape[1] // width

    def choose(m, a, b):
        return jnp.where(m, a, b), jnp.where(m, b, a)

    def block(b, _):
        for u in range(rows_step):
            l = b * rows_step + u
            m = []
            for n in range(3):
                line = jnp.broadcast_to(mask[n, pl.ds(l, 1), :], (16, width)).astype(BF16)
                m.append(jnp.concatenate([line] * (both // 16), axis=0) > 0.5)
            x = [[packed[bb, l + aa] for bb in range(3)] for aa in range(3)]
            for bb in range(3):
                x[0][bb], x[2][bb] = choose(m[0], x[2][bb], x[0][bb])
            for aa in range(3):
                x[aa][0], x[aa][2] = choose(m[1], x[aa][2], x[aa][0])
            for aa, bb in ((0, 1), (0, 2), (1, 2)):
                x[aa][bb], x[bb][aa] = choose(m[2], x[bb][aa], x[aa][bb])
            for k in range(9):
                stacked[pl.ds(k * both, both), pl.ds(u * width, width)] = x[k // 3][k % 3]
        dot = functools.partial(
            lax.dot_general,
            dimension_numbers=(((1,), (0,)), ((), ())),
            preferred_element_type=F32,
        )

        def silu(v):
            h = v * 0.5
            return (h * jnp.tanh(h) + h).astype(BF16)

        first = silu(dot(w1_ref[...], stacked[...]))
        second = silu(dot(w2_ref[...], first))
        tend = dot(w3_ref[...], second)
        for u in range(rows_step):
            l = b * rows_step + u
            cols = slice(u * width, (u + 1) * width)
            terms[0, pl.ds(l, chans, stride=part), :] = tend[0:chans, cols]
            terms[1, pl.ds(l, chans, stride=part), :] = tend[pad : pad + chans, cols]
        return 0

    lax.fori_loop(0, part // rows_step, block, 0)
    own_out[...] = terms[0].reshape(chans, part, width).astype(BF16)
    other_out[...] = terms[1].reshape(chans, part, width).astype(BF16)


def finish_kernel(moved_ref, a0, a1, b0, b1, out_ref):
    chans, part, width = a0.shape
    own = lax.axis_index("group")
    for q, pair in ((own, (a0, a1)), (1 - own, (b0, b1))):
        for n in range(2):
            rows = pl.ds(pl.multiple_of(q * 2 * part + n * part, 8), part)
            out_ref[:, rows, :] = moved_ref[:, rows, :] + pair[n][...].astype(F32)


def call(kernel, name, outs, ins, scratch=(), **cost):
    return pl.pallas_call(
        kernel,
        out_shape=outs,
        in_specs=ins,
        out_specs=jax.tree.map(lambda _: VMEM_SPEC, outs),
        scratch_shapes=list(scratch),
        compiler_params=PARAMS,
        name=name,
    )


def shards(state, courant_x, courant_y, diffusion, neighbours, w_in, w_mid, w_out):
    levels, fields, single, cells_x, cells_y = state.shape
    chans = levels * fields
    hidden = w_mid.shape[0]
    tiles = lax.axis_size("tile")
    half, part = cells_x // 2, cells_x // 4
    pad = -(-chans // 8) * 8
    block = state.reshape(chans, cells_x, cells_y)
    sds = jax.ShapeDtypeStruct

    strip = sds((chans, 8, cells_y), BF16)
    to_east, to_west, rows = call(
        edge_kernel, "edges", (strip, strip, sds((chans, 16, cells_y), BF16)), [VMEM_SPEC]
    )(block)

    def beside(by):
        return [(i, i + by) for i in range(tiles) if 0 <= i % TILE_ROWS + by < TILE_ROWS]

    from_west = lax.ppermute(to_east, "tile", beside(1))
    from_east = lax.ppermute(to_west, "tile", beside(-1))
    spare = jnp.zeros((chans, 3, cells_y), BF16)
    message = jnp.concatenate(
        [rows, from_west[:, :3], to_west[:, :2], spare, to_east[:, 1:3], from_east[:, :3], spare],
        axis=1,
    )

    def across(x, by):
        return lax.ppermute(x, "tile", [(i, (i + by) % tiles) for i in range(tiles)])

    up = across(message, TILE_ROWS)
    down = up if tiles == 2 * TILE_ROWS else across(message, -TILE_ROWS)

    ax = jnp.repeat(courant_x, fields)
    ay = jnp.repeat(courant_y, fields)
    nu = jnp.tile(diffusion, levels)
    coef = jnp.stack(
        [
            1.0 - jnp.abs(ax) - jnp.abs(ay) - 4.0 * nu,
            jnp.maximum(ax, 0.0) + nu,
            nu - jnp.minimum(ax, 0.0),
            jnp.maximum(ay, 0.0) + nu,
            nu - jnp.minimum(ay, 0.0),
        ]
    )
    wide_coef = jnp.broadcast_to(coef[:, :, None], (5, chans, cells_y))

    def flat(x):
        return x.reshape(-1, cells_y)

    win0 = sds((chans, EXTRA + part, cells_y), BF16)
    win1 = sds((chans, part, cells_y), BF16)
    tall = pltpu.VMEM((chans, cells_x + 2 * MARGIN, cells_y), F32)
    moved, mine0, mine1, theirs0, theirs1 = call(
        functools.partial(transport_kernel, chans=chans),
        "transport",
        (sds((chans, cells_x, cells_y), F32), win0, win1, win0, win1),
        [ANY_SPEC, pl.BlockSpec(memory_space=pltpu.SMEM)] + [VMEM_SPEC] * 4,
        [
            pltpu.VMEM((3, chans * message.shape[1], cells_y), F32),
            pltpu.VMEM((2, chans * EXTRA, cells_y), F32),
            tall,
            tall,
            tall,
            pltpu.VMEM((2, 2, 2, chans, cells_y), F32),
            pltpu.VMEM((4 * cells_y, 2 * cells_y), BF16),
            pltpu.SemaphoreType.DMA((1,)),
        ],
    )(block, coef, wide_coef, flat(message), flat(up), flat(down))

    def swap(x):
        return lax.ppermute(x, "group", [(0, 1), (1, 0)])

    got0 = swap(theirs0)
    got1 = swap(theirs1)

    own = lax.axis_index("group")
    both = 2 * pad

    def ordered(w):
        return jnp.where(own == 0, w, w[::-1])

    w1 = ordered(w_in.reshape(2, chans, 9, hidden)).transpose(3, 2, 0, 1)
    w1 = jnp.pad(w1, ((0, 0), (0, 0), (0, 0), (0, pad - chans))).reshape(hidden, 9 * both)
    w3 = ordered(w_out.T.reshape(2, chans, hidden))
    w3 = jnp.pad(w3, ((0, 0), (0, pad - chans), (0, 0))).reshape(both, hidden)
    w2 = w_mid.T

    def physics(chunk, *windows):
        return call(
            functools.partial(physics_kernel, chunk),
            f"physics{chunk}",
            (win1, win1),
            [ANY_SPEC] + [VMEM_SPEC] * (3 + 2 + 2 * chunk) + [ANY_SPEC] * chunk,
            [
                pltpu.VMEM((2, chans * (EXTRA + part), cells_y), F32),
                pltpu.VMEM((2, chans * part, cells_y), F32),
                pltpu.VMEM((part + 4, both, cells_y), F32),
                pltpu.VMEM((3, part + 2, both, cells_y), BF16),
                pltpu.VMEM((3, part, cells_y), F32),
                pltpu.VMEM((2, part, cells_y), jnp.int32),
                pltpu.VMEM((9 * both, 16 * cells_y), BF16),
                pltpu.VMEM((2, chans * part, cells_y), F32),
                pltpu.SemaphoreType.DMA((2,)),
            ],
        )(neighbours, w1, w2, w3, *windows)

    own0, other0 = physics(0, mine0, got0)
    back0 = swap(other0)
    own1, other1 = physics(1, mine0, got0, mine1, got1, own0)
    back1 = swap(other1)
    updated = call(
        finish_kernel, "finish", sds((chans, cells_x, cells_y), F32), [VMEM_SPEC] * 5
    )(moved, own0, own1, back0, back1)
    return updated.reshape(levels, fields, single, cells_x, cells_y)


def solution(mesh):
    return jax.shard_map(
        shards,
        mesh=mesh,
        in_specs=(
            P("group", None, "tile", None, None),
            P("group"),
            P("group"),
            P(),
            P(None, "tile", None, None),
            P(),
            P(),
            P(),
        ),
        out_specs=P("group", None, "tile", None, None),
        check_vma=False,
    )
```

```python
import functools

import jax
import jax.numpy as jnp
from jax import lax
from jax.experimental import pallas as pl
from jax.experimental.pallas import tpu as pltpu
from jax.sharding import PartitionSpec as P


TILE_ROWS = 8
DEEP = 3
EXTRA = 16
MARGIN = 16
GROUP = 4

F32 = jnp.float32
BF16 = jnp.bfloat16
VMEM_SPEC = pl.BlockSpec(memory_space=pltpu.VMEM)
ANY_SPEC = pl.BlockSpec(memory_space=pl.ANY)
PARAMS = pltpu.CompilerParams(vmem_limit_bytes=56 << 20)


def lanes_of(shape):
    return lax.broadcasted_iota(jnp.int32, shape, len(shape) - 1)


def edge_kernel(state_ref, east_ref, west_ref, rows_ref):
    chans, cells_x, cells_y = state_ref.shape
    slot = lax.broadcasted_iota(jnp.int32, (16, cells_y), 0)
    lane = lanes_of((16, cells_y))
    wanted = jnp.where(slot < 8, slot + cells_y - DEEP, slot - 8)
    valid = (slot % 8) < DEEP
    pick = jnp.where(valid & (lane == wanted), 1.0, 0.0).astype(BF16)
    for c in range(chans):
        block = state_ref[c].astype(BF16)
        strips = lax.dot_general(
            pick, block, (((1,), (1,)), ((), ())), preferred_element_type=F32
        ).astype(BF16)
        east_ref[c] = strips[0:8]
        west_ref[c] = strips[8:16]
        rows_ref[c] = jnp.concatenate(
            [state_ref[c, 0:DEEP], state_ref[c, cells_x - DEEP : cells_x], state_ref[c, 0:2]], axis=0
        ).astype(BF16)


def pack_kernel(rows_ref, west_in, east_in, west_own, east_own, out_ref, column_ref, wide, *, chans):
    width = rows_ref.shape[1]
    lane = lanes_of((chans, width))
    for n, ref in enumerate((rows_ref, west_in, east_in, west_own, east_own)):
        wide[n] = ref[...].astype(F32)
    sources = [(1, 0), (1, 1), (1, 2), (3, 0), (3, 1), (4, 1), (4, 2), (2, 0), (2, 1), (2, 2)]
    corner = jnp.zeros((chans, width), F32)
    for k, (n, slot) in enumerate(sources):
        line = wide[n, pl.ds(slot, chans, stride=8), :]
        column_ref[k] = line
        at = 2 * DEEP * k
        corner = jnp.where(
            (lane >= at) & (lane < at + 2 * DEEP), pltpu.roll(line, at + DEEP, 1), corner
        )
    wide[0, pl.ds(2 * DEEP, chans, stride=8), :] = corner
    out_ref[...] = wide[0].astype(BF16)


def shift_matrix(width):
    k = lax.broadcasted_iota(jnp.int32, (4 * width, 2 * width), 0)
    n = lax.broadcasted_iota(jnp.int32, (4 * width, 2 * width), 1)
    m = k % width
    lower = (n < width) & (n == m + 1)
    upper = (n >= width) & (n - width == m - 1)
    west = (k >= 2 * width) & (k < 3 * width) & (n == 0)
    east = (k >= 3 * width) & (n == 2 * width - 1)
    return jnp.where(((k < 2 * width) & (lower | upper)) | west | east, 1.0, 0.0).astype(BF16)


def transport_kernel(
    state_ref, speed_ref, coef_ref, column_ref, up_ref, down_ref,
    moved_ref, mine0, mine1, theirs0, theirs1,
    border, extra, raw_s, once_s, last_s, line_s, matrix, sem, *, chans,
):
    cells_x, width = state_ref.shape[1:]
    half = cells_x // 2
    part = half // 2
    message = up_ref.shape[0] // chans
    own = lax.axis_index("group")
    place = lax.axis_index("tile") % TILE_ROWS
    fetch = pltpu.make_async_copy(state_ref, raw_s.at[:, pl.ds(MARGIN, cells_x)], sem.at[0])
    fetch.start()
    lane = lanes_of((chans, width))
    first, last = lane == 0, lane == width - 1
    for s, ref in enumerate((up_ref, down_ref)):
        border[s] = ref[...].astype(F32)
    coefs = [jnp.broadcast_to(coef_ref[:, n : n + 1], (chans, width)) for n in range(5)]
    matrix[...] = shift_matrix(width)

    above, below = [border[s, pl.ds(2 * DEEP, chans, stride=message), :] for s in range(2)]
    corners = jnp.where(lane % (2 * DEEP) < DEEP, above, below)

    def pair(k):
        return column_ref[k], roll(corners, width - (2 * DEEP * k + DEEP))

    def roll(x, by):
        return pltpu.roll(x, by, 1)

    def both_ways(main, aux):
        ml, al = roll(main, 1), roll(aux, 1)
        mu, au = roll(main, width - 1), roll(aux, width - 1)
        lower = jnp.where(first, al, ml), jnp.where(first, ml, al)
        upper = jnp.where(last, au, mu), jnp.where(last, mu, au)
        return lower, upper

    def column(west, mid, east, keep):
        c0, cxl, cxu, cyl, cyu = coefs
        lower, upper = both_ways(*mid)
        return tuple(
            (c0 * mid[n] + cxl * lower[n] + cxu * upper[n] + cyl * west[n] + cyu * east[n]) * keep
            for n in range(2)
        )

    keeps = (
        jnp.where(place == 0, 0.0, 1.0),
        jnp.where(place == TILE_ROWS - 1, 0.0, 1.0),
    )
    for side in range(2):
        raw = [pair(5 * side + k) for k in range(5)]
        keep = keeps[side]
        inside = 3 if side == 0 else 1
        once = [
            column(raw[k - 1], raw[k], raw[k + 1], 1.0 if k == inside else keep)
            for k in (1, 2, 3)
        ]
        main, aux = column(once[0], once[1], once[2], keep)
        for level, edge in enumerate((raw[2], once[1])):
            for n in range(2):
                line_s[level, side, n] = edge[n]
        for q in range(2):
            if q == 0:
                lineup = jnp.where(first, roll(aux, 1), roll(main, 1))
            else:
                by = width - half + 1
                lineup = jnp.where(lane <= half, roll(main, by), roll(aux, by))
            extra[q, pl.ds(2 + side, chans, stride=EXTRA), :] = lineup

    rows = cells_x + 16
    at = lax.broadcasted_iota(jnp.int32, (rows, width), 0) - 8
    diagonal = (at + width) % width == lanes_of((rows, width))
    fetch.wait()

    group = next(n for n in (GROUP, 2, 1) if chans % n == 0)

    def sweep(level, src, dst, base):
        parts = []
        for g in range(group):
            c = base + g
            q = src[c, pl.ds(8, rows), :]
            hi = q.astype(BF16)
            lo = (q - hi.astype(F32)).astype(BF16)
            sides = []
            for side in range(2):
                main = line_s[level, side, 0, pl.ds(c, 1), :]
                aux = line_s[level, side, 1, pl.ds(c, 1), :]
                values = jnp.concatenate(
                    [
                        jnp.broadcast_to(aux, (8, width)),
                        jnp.broadcast_to(main, (cells_x, width)),
                        jnp.broadcast_to(aux, (8, width)),
                    ],
                    axis=0,
                )
                sides.append(jnp.where(diagonal, values, 0.0).astype(BF16))
            parts.append(jnp.concatenate([hi, lo] + sides, axis=1))
        near = lax.dot_general(
            jnp.concatenate(parts, axis=0),
            matrix[...],
            (((1,), (0,)), ((), ())),
            preferred_element_type=F32,
        )
        for g in range(group):
            c = base + g
            lower, upper = near[g * rows : (g + 1) * rows, :width], near[g * rows : (g + 1) * rows, width:]
            c0, cxl, cxu, cyl, cyu = [speed_ref[n, c] for n in range(5)]
            dst[c, pl.ds(8, rows), :] = (
                c0 * src[c, pl.ds(8, rows), :]
                + cxl * src[c, pl.ds(7, rows), :]
                + cxu * src[c, pl.ds(9, rows), :]
                + cyl * lower
                + cyu * upper
            )

    def finish(base):
        for g in range(group):
            c = base + g
            moved_ref[c] = last_s[c, pl.ds(MARGIN, cells_x), :]
            for q in range(2):
                for k, i in ((0, -1), (1, half), (4, part)):
                    extra[q, pl.ds(c * EXTRA + k, 1), :] = last_s[c, pl.ds(MARGIN + q * half + i, 1), :]
            for dst0, dst1, q in ((mine0, mine1, own), (theirs0, theirs1, 1 - own)):
                start = pl.multiple_of(MARGIN + q * half, 8)
                dst0[c, 0:EXTRA] = extra[q, pl.ds(c * EXTRA, EXTRA), :].astype(BF16)
                dst0[c, EXTRA : EXTRA + part] = last_s[c, pl.ds(start, part), :].astype(BF16)
                dst1[c] = last_s[c, pl.ds(start + part, part), :].astype(BF16)

    for c in range(chans):
        raw_s[c, pl.ds(MARGIN - DEEP, DEEP), :] = border[0, pl.ds(c * message + DEEP, DEEP), :]
        raw_s[c, pl.ds(MARGIN + cells_x, DEEP), :] = border[1, pl.ds(c * message, DEEP), :]
    for base in range(0, chans + group, group):
        if base < chans:
            sweep(0, raw_s, once_s, base)
        if base:
            sweep(1, once_s, last_s, base - group)
            finish(base - group)


def physics_kernel(chunk, table_ref, w1_ref, w2_ref, w3_ref, *rest):
    count = 2 if chunk == 0 else 4
    ins, rest = rest[:count], rest[count + (chunk > 0) :]
    own_out, other_out, wide0, wide1, slab, packed, mask, table, stacked, terms, sem = rest
    chans, part, width = own_out.shape
    half = 2 * part
    pad = slab.shape[1] // 2
    both = 2 * pad
    own = lax.axis_index("group")
    top = own * half + chunk * part
    copies = []
    for n, k in enumerate((5, 7)):
        copies.append(
            pltpu.make_async_copy(table_ref.at[k, 0, pl.ds(top, part)], table.at[n], sem.at[n])
        )
        copies[-1].start()
    height0 = EXTRA + part
    for s in range(2):
        wide0[s] = ins[s][...].reshape(chans * height0, width).astype(F32)
        if chunk:
            wide1[s] = ins[2 + s][...].reshape(chans * part, width).astype(F32)

    slab[...] = jnp.zeros_like(slab)

    def source(s, l):
        if chunk == 0:
            if l < 0:
                return wide0[s, pl.ds(0, chans, stride=height0), :]
            if l >= part:
                return wide0[s, pl.ds(4, chans, stride=height0), :]
            return wide0[s, pl.ds(EXTRA + l, chans, stride=height0), :]
        if l < 0:
            return wide0[s, pl.ds(height0 - 1, chans, stride=height0), :]
        if l >= part:
            return wide0[s, pl.ds(1, chans, stride=height0), :]
        return wide1[s, pl.ds(l, chans, stride=part), :]

    for s in range(2):
        for l in range(-1, part + 1):
            slab[l + 1, pl.ds(s * pad, chans)] = source(s, l)
        for k in range(2):
            slab[part + 2 + k, pl.ds(s * pad, chans)] = wide0[s, pl.ds(2 + k, chans, stride=height0), :]

    lane = lanes_of((both, width))

    def shift(r, _):
        q = slab[r]
        idx = r + chunk * part
        low = jnp.where(lane == 0, pltpu.roll(slab[part + 2], lax.rem(width - idx, width), 1), pltpu.roll(q, 1, 1))
        high = jnp.where(lane == width - 1, pltpu.roll(slab[part + 3], lax.rem(2 * width - 1 - idx, width), 1), pltpu.roll(q, width - 1, 1))
        packed[0, r] = low.astype(BF16)
        packed[1, r] = q.astype(BF16)
        packed[2, r] = high.astype(BF16)
        return 0

    lax.fori_loop(0, part + 2, shift, 0, unroll=2)
    for copy in copies:
        copy.wait()
    rows_i = lax.broadcasted_iota(jnp.int32, (part, width), 0) + top
    centre = (rows_i + 1) * (width + 2) + lanes_of((part, width)) + 1
    along_y = table[0] - centre
    along_x = table[1] - centre
    turned = jnp.abs(along_x) == 1
    mask[0] = jnp.where(jnp.where(turned, along_y, along_x) < 0, 1.0, 0.0)
    mask[1] = jnp.where(jnp.where(turned, along_x, along_y) < 0, 1.0, 0.0)
    mask[2] = jnp.where(turned, 1.0, 0.0)

    rows_step = stacked.shape[1] // width

    def choose(m, a, b):
        return jnp.where(m, a, b), jnp.where(m, b, a)

    def block(b, _):
        for u in range(rows_step):
            l = b * rows_step + u
            m = []
            for n in range(3):
                line = jnp.broadcast_to(mask[n, pl.ds(l, 1), :], (16, width)).astype(BF16)
                m.append(jnp.concatenate([line] * (both // 16), axis=0) > 0.5)
            x = [[packed[bb, l + aa] for bb in range(3)] for aa in range(3)]
            for bb in range(3):
                x[0][bb], x[2][bb] = choose(m[0], x[2][bb], x[0][bb])
            for aa in range(3):
                x[aa][0], x[aa][2] = choose(m[1], x[aa][2], x[aa][0])
            for aa, bb in ((0, 1), (0, 2), (1, 2)):
                x[aa][bb], x[bb][aa] = choose(m[2], x[bb][aa], x[aa][bb])
            for k in range(9):
                stacked[pl.ds(k * both, both), pl.ds(u * width, width)] = x[k // 3][k % 3]
        dot = functools.partial(
            lax.dot_general,
            dimension_numbers=(((1,), (0,)), ((), ())),
            preferred_element_type=F32,
        )

        def silu(v):
            h = v * 0.5
            return (h * jnp.tanh(h) + h).astype(BF16)

        first = silu(dot(w1_ref[...], stacked[...]))
        second = silu(dot(w2_ref[...], first))
        tend = dot(w3_ref[...], second)
        for u in range(rows_step):
            l = b * rows_step + u
            cols = slice(u * width, (u + 1) * width)
            terms[0, pl.ds(l, chans, stride=part), :] = tend[0:chans, cols]
            terms[1, pl.ds(l, chans, stride=part), :] = tend[pad : pad + chans, cols]
        return 0

    lax.fori_loop(0, part // rows_step, block, 0)
    own_out[...] = terms[0].reshape(chans, part, width).astype(BF16)
    other_out[...] = terms[1].reshape(chans, part, width).astype(BF16)


def finish_kernel(moved_ref, a0, a1, b0, b1, out_ref):
    _, part, _ = a0.shape
    own = lax.axis_index("group")
    for q, pair in ((own, (a0, a1)), (1 - own, (b0, b1))):
        for n in range(2):
            rows = pl.ds(pl.multiple_of(q * 2 * part + n * part, 8), part)
            out_ref[:, rows, :] = moved_ref[:, rows, :] + pair[n][...].astype(F32)


def call(kernel, outs, ins, scratch=(), flops=10**9):
    return pl.pallas_call(
        kernel,
        out_shape=outs,
        in_specs=ins,
        out_specs=jax.tree.map(lambda _: VMEM_SPEC, outs),
        scratch_shapes=list(scratch),
        compiler_params=PARAMS,
        cost_estimate=pl.CostEstimate(flops=flops, bytes_accessed=10**6, transcendentals=0),
    )


def shards(state, courant_x, courant_y, diffusion, neighbours, w_in, w_mid, w_out):
    levels, fields, single, cells_x, cells_y = state.shape
    chans = levels * fields
    hidden = w_mid.shape[0]
    tiles = lax.axis_size("tile")
    part = cells_x // 4
    pad = -(-chans // 8) * 8
    block = state.reshape(chans, cells_x, cells_y)
    sds = jax.ShapeDtypeStruct

    strip = sds((chans, 8, cells_y), BF16)
    to_east, to_west, rows = call(edge_kernel, (strip, strip, strip), [VMEM_SPEC])(block)

    def beside(by):
        return [(i, i + by) for i in range(tiles) if 0 <= i % TILE_ROWS + by < TILE_ROWS]

    from_west = lax.ppermute(to_east, "tile", beside(1))
    from_east = lax.ppermute(to_west, "tile", beside(-1))

    def flat(x):
        return x.reshape(-1, cells_y)

    message, columns = call(
        functools.partial(pack_kernel, chans=chans),
        (sds((chans * 8, cells_y), BF16), sds((10, chans, cells_y), F32)),
        [VMEM_SPEC] * 5,
        [pltpu.VMEM((5, chans * 8, cells_y), F32)],
    )(flat(rows), flat(from_west), flat(from_east), flat(to_west), flat(to_east))

    def across(x, by):
        return lax.ppermute(x, "tile", [(i, (i + by) % tiles) for i in range(tiles)])

    up = across(message, TILE_ROWS)
    down = up if tiles == 2 * TILE_ROWS else across(message, -TILE_ROWS)

    ax = jnp.repeat(courant_x, fields)
    ay = jnp.repeat(courant_y, fields)
    nu = jnp.tile(diffusion, levels)
    coef = jnp.stack(
        [
            1.0 - jnp.abs(ax) - jnp.abs(ay) - 4.0 * nu,
            jnp.maximum(ax, 0.0) + nu,
            nu - jnp.minimum(ax, 0.0),
            jnp.maximum(ay, 0.0) + nu,
            nu - jnp.minimum(ay, 0.0),
        ]
    )

    win0 = sds((chans, EXTRA + part, cells_y), BF16)
    win1 = sds((chans, part, cells_y), BF16)
    tall = pltpu.VMEM((chans, cells_x + 2 * MARGIN, cells_y), F32)
    moved, mine0, mine1, theirs0, theirs1 = call(
        functools.partial(transport_kernel, chans=chans),
        (sds((chans, cells_x, cells_y), F32), win0, win1, win0, win1),
        [ANY_SPEC, pl.BlockSpec(memory_space=pltpu.SMEM)] + [VMEM_SPEC] * 4,
        [
            pltpu.VMEM((2, chans * 8, cells_y), F32),
            pltpu.VMEM((2, chans * EXTRA, cells_y), F32),
            tall,
            tall,
            tall,
            pltpu.VMEM((2, 2, 2, chans, cells_y), F32),
            pltpu.VMEM((4 * cells_y, 2 * cells_y), BF16),
            pltpu.SemaphoreType.DMA((1,)),
        ],
        flops=5 * 10**9,
    )(block, coef, coef.T, columns, up, down)

    def swap(x):
        return lax.ppermute(x, "group", [(0, 1), (1, 0)])

    got0 = swap(theirs0)
    got1 = swap(theirs1)

    own = lax.axis_index("group")
    both = 2 * pad

    def ordered(w):
        return jnp.where(own == 0, w, w[::-1])

    w1 = ordered(w_in.reshape(2, chans, 9, hidden)).transpose(3, 2, 0, 1)
    w1 = jnp.pad(w1, ((0, 0), (0, 0), (0, 0), (0, pad - chans))).reshape(hidden, 9 * both)
    w3 = ordered(w_out.T.reshape(2, chans, hidden))
    w3 = jnp.pad(w3, ((0, 0), (0, pad - chans), (0, 0))).reshape(both, hidden)
    w2 = w_mid.T

    def physics(chunk, *windows):
        return call(
            functools.partial(physics_kernel, chunk),
            (win1, win1),
            [ANY_SPEC] + [VMEM_SPEC] * (3 + 2 + 2 * chunk) + [ANY_SPEC] * chunk,
            [
                pltpu.VMEM((2, chans * (EXTRA + part), cells_y), F32),
                pltpu.VMEM((2, chans * part, cells_y), F32),
                pltpu.VMEM((part + 4, both, cells_y), F32),
                pltpu.VMEM((3, part + 2, both, cells_y), BF16),
                pltpu.VMEM((3, part, cells_y), F32),
                pltpu.VMEM((2, part, cells_y), jnp.int32),
                pltpu.VMEM((9 * both, 16 * cells_y), BF16),
                pltpu.VMEM((2, chans * part, cells_y), F32),
                pltpu.SemaphoreType.DMA((2,)),
            ],
            flops=7 * 10**9,
        )(neighbours, w1, w2, w3, *windows)

    own0, other0 = physics(0, mine0, got0)
    back0 = swap(other0)
    own1, other1 = physics(1, mine0, got0, mine1, got1, own0)
    back1 = swap(other1)
    updated = call(
        finish_kernel, sds((chans, cells_x, cells_y), F32), [VMEM_SPEC] * 5
    )(moved, own0, own1, back0, back1)
    return updated.reshape(levels, fields, single, cells_x, cells_y)


def solution(mesh):
    return jax.shard_map(
        shards,
        mesh=mesh,
        in_specs=(
            P("group", None, "tile", None, None),
            P("group"),
            P("group"),
            P(),
            P(None, "tile", None, None),
            P(),
            P(),
            P(),
        ),
        out_specs=P("group", None, "tile", None, None),
        check_vma=False,
    )
```

```python
import functools

import jax
import jax.numpy as jnp
from jax import lax
from jax.experimental import pallas as pl
from jax.experimental.pallas import tpu as pltpu
from jax.sharding import PartitionSpec as P


TILE_ROWS = 8
DEEP = 3
EXTRA = 8
BLOCK_ROWS = 16
MARGIN = 16
GROUP = 4

F32 = jnp.float32
BF16 = jnp.bfloat16
VMEM_SPEC = pl.BlockSpec(memory_space=pltpu.VMEM)
ANY_SPEC = pl.BlockSpec(memory_space=pl.ANY)
PARAMS = pltpu.CompilerParams(vmem_limit_bytes=56 << 20)


def lanes_of(shape):
    return lax.broadcasted_iota(jnp.int32, shape, len(shape) - 1)


def edge_kernel(state_ref, east_ref, west_ref, rows_ref):
    chans, cells_x, cells_y = state_ref.shape
    slot = lax.broadcasted_iota(jnp.int32, (16, cells_y), 0)
    lane = lanes_of((16, cells_y))
    wanted = jnp.where(slot < 8, slot + cells_y - DEEP, slot - 8)
    valid = (slot % 8) < DEEP
    pick = jnp.where(valid & (lane == wanted), 1.0, 0.0).astype(BF16)
    for c in range(chans):
        block = state_ref[c].astype(BF16)
        strips = lax.dot_general(
            pick, block, (((1,), (1,)), ((), ())), preferred_element_type=F32
        ).astype(BF16)
        east_ref[c] = strips[0:8]
        west_ref[c] = strips[8:16]
        rows_ref[c] = jnp.concatenate(
            [state_ref[c, 0:DEEP], state_ref[c, cells_x - DEEP : cells_x], state_ref[c, 0:2]], axis=0
        ).astype(BF16)


def pack_kernel(rows_ref, west_in, east_in, west_own, east_own, out_ref, column_ref, wide, *, chans):
    width = rows_ref.shape[1]
    lane = lanes_of((chans, width))
    for n, ref in enumerate((rows_ref, west_in, east_in, west_own, east_own)):
        wide[n] = ref[...].astype(F32)
    sources = [(1, 0), (1, 1), (1, 2), (3, 0), (3, 1), (4, 1), (4, 2), (2, 0), (2, 1), (2, 2)]
    corner = jnp.zeros((chans, width), F32)
    for k, (n, slot) in enumerate(sources):
        line = wide[n, pl.ds(slot, chans, stride=8), :]
        column_ref[k] = line
        at = 2 * DEEP * k
        corner = jnp.where(
            (lane >= at) & (lane < at + 2 * DEEP), pltpu.roll(line, at + DEEP, 1), corner
        )
    wide[0, pl.ds(2 * DEEP, chans, stride=8), :] = corner
    out_ref[...] = wide[0].astype(BF16)


def shift_matrix(width):
    k = lax.broadcasted_iota(jnp.int32, (4 * width, 2 * width), 0)
    n = lax.broadcasted_iota(jnp.int32, (4 * width, 2 * width), 1)
    m = k % width
    lower = (n < width) & (n == m + 1)
    upper = (n >= width) & (n - width == m - 1)
    west = (k >= 2 * width) & (k < 3 * width) & (n == 0)
    east = (k >= 3 * width) & (n == 2 * width - 1)
    return jnp.where(((k < 2 * width) & (lower | upper)) | west | east, 1.0, 0.0).astype(BF16)


def transport_kernel(
    state_ref, speed_ref, coef_ref, column_ref, up_ref, down_ref,
    moved_ref, *rest, chans, chunks,
):
    count = len(chunks)
    mine, theirs, rest = rest[:count], rest[count : 2 * count], rest[2 * count :]
    windows, (border, raw_s, once_s, last_s, line_s, matrix, sem) = rest[:count], rest[count:]
    cells_x, width = state_ref.shape[1:]
    half = cells_x // 2
    message = up_ref.shape[0] // chans
    own = lax.axis_index("group")
    place = lax.axis_index("tile") % TILE_ROWS
    fetch = pltpu.make_async_copy(state_ref, raw_s.at[:, pl.ds(MARGIN, cells_x)], sem.at[0])
    fetch.start()
    lane = lanes_of((chans, width))
    first, last = lane == 0, lane == width - 1
    low_lanes = lane < width // 2
    for s, ref in enumerate((up_ref, down_ref)):
        border[s] = ref[...].astype(F32)
    coefs = [jnp.broadcast_to(coef_ref[:, n : n + 1], (chans, width)) for n in range(5)]
    matrix[...] = shift_matrix(width)

    above, below = [border[s, pl.ds(2 * DEEP, chans, stride=message), :] for s in range(2)]
    corners = jnp.where(lane % (2 * DEEP) < DEEP, above, below)

    def pair(k):
        return column_ref[k], roll(corners, width - (2 * DEEP * k + DEEP))

    def roll(x, by):
        return pltpu.roll(x, by, 1)

    def both_ways(main, aux):
        ml, al = roll(main, 1), roll(aux, 1)
        mu, au = roll(main, width - 1), roll(aux, width - 1)
        lower = jnp.where(first, al, ml), jnp.where(first, ml, al)
        upper = jnp.where(last, au, mu), jnp.where(last, mu, au)
        return lower, upper

    def column(west, mid, east, keep):
        c0, cxl, cxu, cyl, cyu = coefs
        lower, upper = both_ways(*mid)
        return tuple(
            (c0 * mid[n] + cxl * lower[n] + cxu * upper[n] + cyl * west[n] + cyu * east[n]) * keep
            for n in range(2)
        )

    keeps = (
        jnp.where(place == 0, 0.0, 1.0),
        jnp.where(place == TILE_ROWS - 1, 0.0, 1.0),
    )
    edges = []
    for side in range(2):
        raw = [pair(5 * side + k) for k in range(5)]
        keep = keeps[side]
        inside = 3 if side == 0 else 1
        once = [
            column(raw[k - 1], raw[k], raw[k + 1], 1.0 if k == inside else keep)
            for k in (1, 2, 3)
        ]
        main, aux = column(once[0], once[1], once[2], keep)
        for level, edge in enumerate((raw[2], once[1])):
            for n in range(2):
                line_s[level, side, n] = edge[n]
        edges.append((main, aux))
    for q in range(2):
        for window, (start, size) in zip(windows, chunks):
            at = q * half + start - 1
            sides = []
            for side, first_lane in enumerate((0, width // 2)):
                main, aux = edges[side]
                by = (first_lane - at) % width
                row_of = lane - first_lane + at
                off = (row_of < 0) | (row_of >= cells_x)
                sides.append(jnp.where(off, roll(aux, by), roll(main, by)))
            window[q, pl.ds(2, chans, stride=EXTRA + size), :] = jnp.where(low_lanes, *sides)

    rows = cells_x + 16
    at = lax.broadcasted_iota(jnp.int32, (rows, width), 0) - 8
    diagonal = (at + width) % width == lanes_of((rows, width))
    fetch.wait()

    group = next(n for n in (GROUP, 2, 1) if chans % n == 0)

    def sweep(level, src, dst, base):
        parts = []
        for g in range(group):
            c = base + g
            q = src[c, pl.ds(8, rows), :]
            hi = q.astype(BF16)
            lo = (q - hi.astype(F32)).astype(BF16)
            sides = []
            for side in range(2):
                main = line_s[level, side, 0, pl.ds(c, 1), :]
                aux = line_s[level, side, 1, pl.ds(c, 1), :]
                values = jnp.concatenate(
                    [
                        jnp.broadcast_to(aux, (8, width)),
                        jnp.broadcast_to(main, (cells_x, width)),
                        jnp.broadcast_to(aux, (8, width)),
                    ],
                    axis=0,
                )
                sides.append(jnp.where(diagonal, values, 0.0).astype(BF16))
            parts.append(jnp.concatenate([hi, lo] + sides, axis=1))
        near = lax.dot_general(
            jnp.concatenate(parts, axis=0),
            matrix[...],
            (((1,), (0,)), ((), ())),
            preferred_element_type=F32,
        )
        for g in range(group):
            c = base + g
            lower, upper = near[g * rows : (g + 1) * rows, :width], near[g * rows : (g + 1) * rows, width:]
            c0, cxl, cxu, cyl, cyu = [speed_ref[n, c] for n in range(5)]
            dst[c, pl.ds(8, rows), :] = (
                c0 * src[c, pl.ds(8, rows), :]
                + cxl * src[c, pl.ds(7, rows), :]
                + cxu * src[c, pl.ds(9, rows), :]
                + cyl * lower
                + cyu * upper
            )

    outs = []

    def finish(base):
        for g in range(group):
            c = base + g
            for q in range(2):
                for window, (start, size) in zip(windows, chunks):
                    at = MARGIN + q * half + start
                    to = c * (EXTRA + size)
                    window[q, pl.ds(to, 1), :] = last_s[c, pl.ds(at - 1, 1), :]
                    window[q, pl.ds(to + 1, 1), :] = last_s[c, pl.ds(at + size, 1), :]
                    window[q, pl.ds(to + EXTRA, size), :] = last_s[c, pl.ds(at, size), :]
        outs.append(
            pltpu.make_async_copy(
                last_s.at[pl.ds(base, group), pl.ds(MARGIN, cells_x)],
                moved_ref.at[pl.ds(base, group)],
                sem.at[1 + base // group],
            )
        )
        outs[-1].start()

    for c in range(chans):
        raw_s[c, pl.ds(MARGIN - DEEP, DEEP), :] = border[0, pl.ds(c * message + DEEP, DEEP), :]
        raw_s[c, pl.ds(MARGIN + cells_x, DEEP), :] = border[1, pl.ds(c * message, DEEP), :]
    for base in range(0, chans + group, group):
        if base < chans:
            sweep(0, raw_s, once_s, base)
        if base:
            sweep(1, once_s, last_s, base - group)
            finish(base - group)
    for n in range(count):
        mine[n][...] = windows[n][own].astype(BF16)
        theirs[n][...] = windows[n][1 - own].astype(BF16)
    for copy in outs:
        copy.wait()


def physics_kernel(
    table_ref, w1_ref, w2_ref, w3_ref, mine_ref, got_ref, image_in,
    image_ref, other_ref, wide, packed, mask, table, even, odd, terms, patch, sem, *, start, chans,
):
    size, width = table.shape[1:]
    cells_x = image_in.shape[1]
    half = cells_x // 2
    height = EXTRA + size
    pad = -(-chans // 8) * 8
    both = 2 * pad
    top = lax.axis_index("group") * half + start
    copies = [
        pltpu.make_async_copy(table_ref.at[k, 0, pl.ds(top, size)], table.at[n], sem.at[n])
        for n, k in enumerate((5, 7))
    ]
    fetch = pltpu.make_async_copy(image_in.at[:, pl.ds(top, size)], patch, sem.at[2])
    for copy in copies:
        copy.start()
    fetch.start()

    k = lax.broadcasted_iota(jnp.int32, (2 * width, 2 * width), 0)
    n = lax.broadcasted_iota(jnp.int32, (2 * width, 2 * width), 1)
    inner = (k < width) & (((n < width) & (n == k + 1)) | ((n >= width) & (n - width == k - 1)))
    west = (k >= width) & (k < width + width // 2) & (n == 0)
    east = (k >= width + width // 2) & (n == 2 * width - 1)
    matrix = jnp.where(inner | west | east, 1.0, 0.0).astype(BF16)
    slot = lax.broadcasted_iota(jnp.int32, (height, width), 0)
    line = jnp.where(
        slot >= EXTRA, slot - EXTRA + 1, jnp.where(slot == 0, 0, jnp.where(slot == 1, size + 1, -1))
    )
    diagonal = lanes_of((height, width)) % (width // 2) == line
    for s, ref in enumerate((mine_ref, got_ref)):
        cells = ref[...]
        flat = cells.astype(F32)
        wide[1, s, pl.ds(0, chans * height)] = flat
        edges = [
            jnp.where(diagonal, flat[c * height + 2 : c * height + 3], 0.0) for c in range(chans)
        ]
        edges = jnp.concatenate(edges, axis=0).astype(BF16)
        near = lax.dot_general(
            jnp.concatenate([cells, edges], axis=1),
            matrix,
            (((1,), (0,)), ((), ())),
            preferred_element_type=F32,
        )
        wide[0, s, pl.ds(0, chans * height)] = near[:, :width]
        wide[2, s, pl.ds(0, chans * height)] = near[:, width:]
        if pad > chans:
            for b in range(3):
                wide[b, s, pl.ds(chans * height, (pad - chans) * height)] = jnp.zeros(
                    ((pad - chans) * height, width), F32
                )

    for l in range(-1, size + 1):
        at = 0 if l < 0 else 1 if l == size else EXTRA + l
        for b in range(3):
            pair = [wide[b, s, pl.ds(at, pad, stride=height), :] for s in range(2)]
            packed[b, l + 1] = jnp.concatenate(pair, axis=0).astype(BF16)

    for copy in copies:
        copy.wait()
    rows_i = lax.broadcasted_iota(jnp.int32, (size, width), 0) + top
    centre = (rows_i + 1) * (width + 2) + lanes_of((size, width)) + 1
    along_y = table[0] - centre
    along_x = table[1] - centre
    turned = jnp.abs(along_x) == 1
    mask[0] = jnp.where(jnp.where(turned, along_y, along_x) < 0, 1.0, 0.0)
    mask[1] = jnp.where(jnp.where(turned, along_x, along_y) < 0, 1.0, 0.0)
    mask[2] = jnp.where(turned, 1.0, 0.0)

    def choose(m, a, b):
        return jnp.where(m, a, b), jnp.where(m, b, a)

    rows_step = even.shape[1] // width

    def stack(n, dst):
        for u in range(rows_step):
            l = n * rows_step + u
            m = []
            for k in range(3):
                line = jnp.broadcast_to(mask[k, pl.ds(l, 1), :], (16, width)).astype(BF16)
                m.append(jnp.concatenate([line] * (both // 16), axis=0) > 0.5)
            x = [[packed[bb, l + aa] for bb in range(3)] for aa in range(3)]
            for bb in range(3):
                x[0][bb], x[2][bb] = choose(m[0], x[2][bb], x[0][bb])
            for aa in range(3):
                x[aa][0], x[aa][2] = choose(m[1], x[aa][2], x[aa][0])
            for aa, bb in ((0, 1), (0, 2), (1, 2)):
                x[aa][bb], x[bb][aa] = choose(m[2], x[bb][aa], x[aa][bb])
            for k in range(9):
                dst[pl.ds(k * both, both), pl.ds(u * width, width)] = x[k // 3][k % 3]

    dot = functools.partial(
        lax.dot_general,
        dimension_numbers=(((1,), (0,)), ((), ())),
        preferred_element_type=F32,
    )

    def silu(v):
        h = v * 0.5
        return (h * jnp.tanh(h) + h).astype(BF16)

    def network(n, src):
        first = silu(dot(w1_ref[...], src[...]))
        second = silu(dot(w2_ref[...], first))
        tend = dot(w3_ref[...], second)
        for u in range(rows_step):
            l = n * rows_step + u
            cols = slice(u * width, (u + 1) * width)
            terms[0, pl.ds(l, chans, stride=size), :] = tend[0:chans, cols]
            terms[1, pl.ds(l, chans, stride=size), :] = tend[pad : pad + chans, cols]

    steps = size // rows_step
    slots = (even, odd)
    stack(0, even)
    for n in range(steps):
        if n + 1 < steps:
            stack(n + 1, slots[(n + 1) % 2])
        network(n, slots[n % 2])
    other_ref[...] = terms[1].astype(BF16)
    fetch.wait()
    patch[...] = patch[...] + terms[0].reshape(patch.shape)
    put = pltpu.make_async_copy(patch, image_ref.at[:, pl.ds(top, size)], sem.at[3])
    put.start()
    put.wait()


def finish_kernel(back_ref, image_in, image_ref, patch, sem, *, start):
    size = patch.shape[1]
    half = image_in.shape[1] // 2
    rows = pl.ds((1 - lax.axis_index("group")) * half + start, size)
    fetch = pltpu.make_async_copy(image_in.at[:, rows], patch, sem.at[0])
    fetch.start()
    fetch.wait()
    patch[...] = patch[...] + back_ref[...].astype(F32).reshape(patch.shape)
    put = pltpu.make_async_copy(patch, image_ref.at[:, rows], sem.at[1])
    put.start()
    put.wait()


def call(kernel, outs, ins, scratch=(), flops=10**9, out_specs=None, aliases=None):
    return pl.pallas_call(
        kernel,
        out_shape=jax.tree.map(lambda x: jax.ShapeDtypeStruct(x.shape, x.dtype), outs),
        in_specs=ins,
        out_specs=jax.tree.map(lambda _: VMEM_SPEC, outs) if out_specs is None else out_specs,
        input_output_aliases=aliases or {},
        scratch_shapes=list(scratch),
        compiler_params=PARAMS,
        cost_estimate=pl.CostEstimate(flops=flops, bytes_accessed=10**6, transcendentals=0),
    )


def shards(state, courant_x, courant_y, diffusion, neighbours, w_in, w_mid, w_out):
    levels, fields, single, cells_x, cells_y = state.shape
    chans = levels * fields
    hidden = w_mid.shape[0]
    tiles = lax.axis_size("tile")
    pad = -(-chans // 8) * 8
    block = state.reshape(chans, cells_x, cells_y)
    sds = jax.ShapeDtypeStruct

    strip = sds((chans, 8, cells_y), BF16)
    to_east, to_west, rows = call(edge_kernel, (strip, strip, strip), [VMEM_SPEC])(block)

    def beside(by):
        return [(i, i + by) for i in range(tiles) if 0 <= i % TILE_ROWS + by < TILE_ROWS]

    from_west = lax.ppermute(to_east, "tile", beside(1))
    from_east = lax.ppermute(to_west, "tile", beside(-1))

    def flat(x):
        return x.reshape(-1, cells_y)

    message, columns = call(
        functools.partial(pack_kernel, chans=chans),
        (sds((chans * 8, cells_y), BF16), sds((10, chans, cells_y), F32)),
        [VMEM_SPEC] * 5,
        [pltpu.VMEM((5, chans * 8, cells_y), F32)],
    )(flat(rows), flat(from_west), flat(from_east), flat(to_west), flat(to_east))

    def across(x, by):
        return lax.ppermute(x, "tile", [(i, (i + by) % tiles) for i in range(tiles)])

    up = across(message, TILE_ROWS)
    down = up if tiles == 2 * TILE_ROWS else across(message, -TILE_ROWS)

    ax = jnp.repeat(courant_x, fields)
    ay = jnp.repeat(courant_y, fields)
    nu = jnp.tile(diffusion, levels)
    coef = jnp.stack(
        [
            1.0 - jnp.abs(ax) - jnp.abs(ay) - 4.0 * nu,
            jnp.maximum(ax, 0.0) + nu,
            nu - jnp.minimum(ax, 0.0),
            jnp.maximum(ay, 0.0) + nu,
            nu - jnp.minimum(ay, 0.0),
        ]
    )

    quarter = cells_x // 4
    chunks = [(n * quarter, quarter) for n in range(2)]
    heights = [chans * (EXTRA + size) for _, size in chunks]
    tall = pltpu.VMEM((chans, cells_x + 2 * MARGIN, cells_y), F32)
    packets = [sds((height, cells_y), BF16) for height in heights]
    image, *windows = call(
        functools.partial(transport_kernel, chans=chans, chunks=chunks),
        (sds((chans, cells_x, cells_y), F32), *packets, *packets),
        [ANY_SPEC, pl.BlockSpec(memory_space=pltpu.SMEM)] + [VMEM_SPEC] * 4,
        [pltpu.VMEM((2, height, cells_y), F32) for height in heights]
        + [
            pltpu.VMEM((2, chans * 8, cells_y), F32),
            tall,
            tall,
            tall,
            pltpu.VMEM((2, 2, 2, chans, cells_y), F32),
            pltpu.VMEM((4 * cells_y, 2 * cells_y), BF16),
            pltpu.SemaphoreType.DMA((1 + chans,)),
        ],
        flops=5 * 10**9,
        out_specs=(ANY_SPEC,) + (VMEM_SPEC,) * (2 * len(chunks)),
    )(block, coef, coef.T, columns, up, down)
    mine, theirs = windows[: len(chunks)], windows[len(chunks) :]

    def swap(x):
        return lax.ppermute(x, "group", [(0, 1), (1, 0)])

    got = [swap(packet) for packet in theirs]

    own = lax.axis_index("group")
    both = 2 * pad

    def ordered(w):
        return jnp.where(own == 0, w, w[::-1])

    w1 = ordered(w_in.reshape(2, chans, 9, hidden)).transpose(3, 2, 0, 1)
    w1 = jnp.pad(w1, ((0, 0), (0, 0), (0, 0), (0, pad - chans))).reshape(hidden, 9 * both)
    w3 = ordered(w_out.T.reshape(2, chans, hidden))
    w3 = jnp.pad(w3, ((0, 0), (0, pad - chans), (0, 0))).reshape(both, hidden)
    w2 = w_mid.T

    back = []
    for n, (start, size) in enumerate(chunks):
        depth = 8 * (-(-chans // 8)) * (EXTRA + size)
        wide = pltpu.VMEM((3, 2, depth, cells_y), F32)
        blocks = pltpu.VMEM((9 * both, min(BLOCK_ROWS, size) * cells_y), BF16)
        image, other = call(
            functools.partial(physics_kernel, start=start, chans=chans),
            (image, sds((chans * size, cells_y), BF16)),
            [ANY_SPEC] + [VMEM_SPEC] * 5 + [ANY_SPEC],
            [
                wide,
                pltpu.VMEM((3, size + 2, both, cells_y), BF16),
                pltpu.VMEM((3, size, cells_y), F32),
                pltpu.VMEM((2, size, cells_y), jnp.int32),
                blocks,
                blocks,
                pltpu.VMEM((2, chans * size, cells_y), F32),
                pltpu.VMEM((chans, size, cells_y), F32),
                pltpu.SemaphoreType.DMA((4,)),
            ],
            flops=7 * 10**9,
            out_specs=(ANY_SPEC, VMEM_SPEC),
            aliases={6: 0},
        )(neighbours, w1, w2, w3, mine[n], got[n], image)
        back.append(swap(other))
    for n, (start, size) in enumerate(chunks):
        image = call(
            functools.partial(finish_kernel, start=start),
            image,
            [VMEM_SPEC, ANY_SPEC],
            [pltpu.VMEM((chans, size, cells_y), F32), pltpu.SemaphoreType.DMA((2,))],
            out_specs=ANY_SPEC,
            aliases={1: 0},
        )(back[n], image)
    return image.reshape(levels, fields, single, cells_x, cells_y)


def solution(mesh):
    return jax.shard_map(
        shards,
        mesh=mesh,
        in_specs=(
            P("group", None, "tile", None, None),
            P("group"),
            P("group"),
            P(),
            P(None, "tile", None, None),
            P(),
            P(),
            P(),
        ),
        out_specs=P("group", None, "tile", None, None),
        check_vma=False,
    )
```

```python
import functools

import jax
import jax.numpy as jnp
from jax import lax
from jax.experimental import pallas as pl
from jax.experimental.pallas import tpu as pltpu
from jax.sharding import PartitionSpec as P


TILE_ROWS = 8
DEEP = 3
EXTRA = 8
BLOCK_ROWS = 16
MARGIN = 16
GROUP = 4

F32 = jnp.float32
BF16 = jnp.bfloat16
VMEM_SPEC = pl.BlockSpec(memory_space=pltpu.VMEM)
ANY_SPEC = pl.BlockSpec(memory_space=pl.ANY)


def lanes_of(shape):
    return lax.broadcasted_iota(jnp.int32, shape, len(shape) - 1)


def edge_kernel(state_ref, east_ref, west_ref, rows_ref):
    chans, cells_x, cells_y = state_ref.shape
    slot = lax.broadcasted_iota(jnp.int32, (16, cells_y), 0)
    lane = lanes_of((16, cells_y))
    wanted = jnp.where(slot < 8, slot + cells_y - DEEP, slot - 8)
    valid = (slot % 8) < DEEP
    pick = jnp.where(valid & (lane == wanted), 1.0, 0.0).astype(BF16)
    for c in range(chans):
        block = state_ref[c].astype(BF16)
        strips = lax.dot_general(
            pick, block, (((1,), (1,)), ((), ())), preferred_element_type=F32
        ).astype(BF16)
        east_ref[c] = strips[0:8]
        west_ref[c] = strips[8:16]
        rows_ref[c] = jnp.concatenate(
            [state_ref[c, 0:DEEP], state_ref[c, cells_x - DEEP : cells_x], state_ref[c, 0:2]], axis=0
        ).astype(BF16)


def pack_kernel(rows_ref, west_in, east_in, west_own, east_own, out_ref, column_ref, wide, *, chans):
    width = rows_ref.shape[1]
    lane = lanes_of((chans, width))
    for n, ref in enumerate((rows_ref, west_in, east_in, west_own, east_own)):
        wide[n] = ref[...].astype(F32)
    sources = [(1, 0), (1, 1), (1, 2), (3, 0), (3, 1), (4, 1), (4, 2), (2, 0), (2, 1), (2, 2)]
    corner = jnp.zeros((chans, width), F32)
    for k, (n, slot) in enumerate(sources):
        line = wide[n, pl.ds(slot, chans, stride=8), :]
        column_ref[k] = line
        at = 2 * DEEP * k
        corner = jnp.where(
            (lane >= at) & (lane < at + 2 * DEEP), pltpu.roll(line, at + DEEP, 1), corner
        )
    wide[0, pl.ds(2 * DEEP, chans, stride=8), :] = corner
    out_ref[...] = wide[0].astype(BF16)


def shift_matrix(width):
    k = lax.broadcasted_iota(jnp.int32, (4 * width, 2 * width), 0)
    n = lax.broadcasted_iota(jnp.int32, (4 * width, 2 * width), 1)
    m = k % width
    lower = (n < width) & (n == m + 1)
    upper = (n >= width) & (n - width == m - 1)
    west = (k >= 2 * width) & (k < 3 * width) & (n == 0)
    east = (k >= 3 * width) & (n == 2 * width - 1)
    return jnp.where(((k < 2 * width) & (lower | upper)) | west | east, 1.0, 0.0).astype(BF16)


def transport_kernel(
    state_ref, speed_ref, coef_ref, column_ref, up_ref, down_ref, *rest, chans, jobs, ahead,
):
    count = len(jobs)
    moved_ref, rest = (None, rest) if ahead else (rest[0], rest[1:])
    packets, windows, rest = rest[:count], rest[count : 2 * count], rest[2 * count :]
    border, raw_s, once_s, last_s, line_s, matrix, up_s, down_s, sem = rest
    cells_x, width = state_ref.shape[1:]
    half = cells_x // 2
    message = up_ref.shape[0] // chans
    own = lax.axis_index("group")
    place = lax.axis_index("tile") % TILE_ROWS
    base_of = [jnp.where(whose == 0, own, 1 - own) * half + start for whose, start, _ in jobs]
    fetch = pltpu.make_async_copy(state_ref, raw_s.at[:, pl.ds(MARGIN, cells_x)], sem.at[0])
    halo = [
        pltpu.make_async_copy(up_ref, up_s, sem.at[1]),
        pltpu.make_async_copy(down_ref, down_s, sem.at[2]),
    ]
    for copy in halo:
        copy.start()
    fetch.start()
    matrix[...] = shift_matrix(width)
    for copy in halo:
        copy.wait()
    lane = lanes_of((chans, width))
    first, last = lane == 0, lane == width - 1
    low_lanes = lane < width // 2
    for s, ref in enumerate((up_s, down_s)):
        border[s] = ref[...].astype(F32)
    coefs = [jnp.broadcast_to(coef_ref[:, n : n + 1], (chans, width)) for n in range(5)]

    above, below = [border[s, pl.ds(2 * DEEP, chans, stride=message), :] for s in range(2)]
    corners = jnp.where(lane % (2 * DEEP) < DEEP, above, below)

    def pair(k):
        return column_ref[k], roll(corners, width - (2 * DEEP * k + DEEP))

    def roll(x, by):
        return pltpu.roll(x, by, 1)

    def both_ways(main, aux):
        ml, al = roll(main, 1), roll(aux, 1)
        mu, au = roll(main, width - 1), roll(aux, width - 1)
        lower = jnp.where(first, al, ml), jnp.where(first, ml, al)
        upper = jnp.where(last, au, mu), jnp.where(last, mu, au)
        return lower, upper

    def column(west, mid, east, keep):
        c0, cxl, cxu, cyl, cyu = coefs
        lower, upper = both_ways(*mid)
        return tuple(
            (c0 * mid[n] + cxl * lower[n] + cxu * upper[n] + cyl * west[n] + cyu * east[n]) * keep
            for n in range(2)
        )

    keeps = (
        jnp.where(place == 0, 0.0, 1.0),
        jnp.where(place == TILE_ROWS - 1, 0.0, 1.0),
    )
    edges = []
    for side in range(2):
        raw = [pair(5 * side + k) for k in range(5)]
        keep = keeps[side]
        inside = 3 if side == 0 else 1
        once = [
            column(raw[k - 1], raw[k], raw[k + 1], 1.0 if k == inside else keep)
            for k in (1, 2, 3)
        ]
        main, aux = column(once[0], once[1], once[2], keep)
        for level, edge in enumerate((raw[2], once[1])):
            for n in range(2):
                line_s[level, side, n] = edge[n]
        edges.append((main, aux))
    for window, base, (_, _, size) in zip(windows, base_of, jobs):
        at = base - 1
        sides = []
        for side, first_lane in enumerate((0, width // 2)):
            main, aux = edges[side]
            by = lax.rem(first_lane - at + width, width)
            row_of = lane - first_lane + at
            off = (row_of < 0) | (row_of >= cells_x)
            sides.append(jnp.where(off, roll(aux, by), roll(main, by)))
        window[pl.ds(2, chans, stride=EXTRA + size), :] = jnp.where(low_lanes, *sides)

    rows = jobs[0][2] + 16 if ahead else cells_x + 16
    origin = base_of[0] - 8 if ahead else -8
    top = pl.multiple_of(origin + MARGIN, 8) if ahead else 8
    at = lax.broadcasted_iota(jnp.int32, (rows, width), 0) + origin
    diagonal = lax.rem(at + width, width) == lanes_of((rows, width))
    within = (at >= 0) & (at < cells_x)
    fetch.wait()
    group = next(n for n in (10 if ahead else GROUP, 2, 1) if chans % n == 0)

    def sweep(level, src, dst, base):
        parts = []
        for g in range(group):
            c = base + g
            q = src[c, pl.ds(top, rows), :]
            hi = q.astype(BF16)
            lo = (q - hi.astype(F32)).astype(BF16)
            sides = []
            for side in range(2):
                main = line_s[level, side, 0, pl.ds(c, 1), :]
                aux = line_s[level, side, 1, pl.ds(c, 1), :]
                values = jnp.where(within, main, aux)
                sides.append(jnp.where(diagonal, values, 0.0).astype(BF16))
            parts.append(jnp.concatenate([hi, lo] + sides, axis=1))
        near = lax.dot_general(
            jnp.concatenate(parts, axis=0),
            matrix[...],
            (((1,), (0,)), ((), ())),
            preferred_element_type=F32,
        )
        for g in range(group):
            c = base + g
            lower, upper = near[g * rows : (g + 1) * rows, :width], near[g * rows : (g + 1) * rows, width:]
            c0, cxl, cxu, cyl, cyu = [speed_ref[n, c] for n in range(5)]
            dst[c, pl.ds(top, rows), :] = (
                c0 * src[c, pl.ds(top, rows), :]
                + cxl * src[c, pl.ds(top - 1, rows), :]
                + cxu * src[c, pl.ds(top + 1, rows), :]
                + cyl * lower
                + cyu * upper
            )

    outs = []

    def finish(base):
        for g in range(group):
            c = base + g
            for window, row, (_, _, size) in zip(windows, base_of, jobs):
                at = MARGIN + row
                to = c * (EXTRA + size)
                window[pl.ds(to, 1), :] = last_s[c, pl.ds(at - 1, 1), :]
                window[pl.ds(to + 1, 1), :] = last_s[c, pl.ds(at + size, 1), :]
                window[pl.ds(to + EXTRA, size), :] = last_s[c, pl.ds(pl.multiple_of(at, 8), size), :]
        if not ahead:
            outs.append(
                pltpu.make_async_copy(
                    last_s.at[pl.ds(base, group), pl.ds(MARGIN, cells_x)],
                    moved_ref.at[pl.ds(base, group)],
                    sem.at[3 + base // group],
                )
            )
            outs[-1].start()

    for c in range(chans):
        raw_s[c, pl.ds(MARGIN - DEEP, DEEP), :] = border[0, pl.ds(c * message + DEEP, DEEP), :]
        raw_s[c, pl.ds(MARGIN + cells_x, DEEP), :] = border[1, pl.ds(c * message, DEEP), :]
    for base in range(0, chans + group, group):
        if base < chans:
            sweep(0, raw_s, once_s, base)
        if base:
            sweep(1, once_s, last_s, base - group)
            finish(base - group)
    for packet, window in zip(packets, windows):
        packet[...] = window[...].astype(BF16)
    for copy in outs:
        copy.wait()


def physics_kernel(
    table_ref, w1_ref, w2_ref, w3_ref, mine_ref, got_ref, image_in,
    image_ref, other_ref, wide, packed, mask, table, even, odd, terms, patch, got, sem, *, start, chans,
):
    size, width = table.shape[1:]
    cells_x = image_in.shape[1]
    half = cells_x // 2
    height = EXTRA + size
    pad = -(-chans // 8) * 8
    both = 2 * pad
    top = lax.axis_index("group") * half + start
    copies = [
        pltpu.make_async_copy(table_ref.at[k, 0, pl.ds(top, size)], table.at[n], sem.at[n])
        for n, k in enumerate((5, 7))
    ]
    fetch = pltpu.make_async_copy(image_in.at[:, pl.ds(top, size)], patch, sem.at[2])
    arrive = pltpu.make_async_copy(got_ref, got, sem.at[4])
    for copy in copies:
        copy.start()
    arrive.start()
    fetch.start()

    k = lax.broadcasted_iota(jnp.int32, (2 * width, 2 * width), 0)
    n = lax.broadcasted_iota(jnp.int32, (2 * width, 2 * width), 1)
    inner = (k < width) & (((n < width) & (n == k + 1)) | ((n >= width) & (n - width == k - 1)))
    west = (k >= width) & (k < width + width // 2) & (n == 0)
    east = (k >= width + width // 2) & (n == 2 * width - 1)
    matrix = jnp.where(inner | west | east, 1.0, 0.0).astype(BF16)
    slot = lax.broadcasted_iota(jnp.int32, (height, width), 0)
    line = jnp.where(
        slot >= EXTRA, slot - EXTRA + 1, jnp.where(slot == 0, 0, jnp.where(slot == 1, size + 1, -1))
    )
    diagonal = lanes_of((height, width)) % (width // 2) == line
    for s, ref in enumerate((mine_ref, got)):
        if s == 1:
            arrive.wait()
        cells = ref[...]
        flat = cells.astype(F32)
        wide[1, s, pl.ds(0, chans * height)] = flat
        edges = [
            jnp.where(diagonal, flat[c * height + 2 : c * height + 3], 0.0) for c in range(chans)
        ]
        edges = jnp.concatenate(edges, axis=0).astype(BF16)
        near = lax.dot_general(
            jnp.concatenate([cells, edges], axis=1),
            matrix,
            (((1,), (0,)), ((), ())),
            preferred_element_type=F32,
        )
        wide[0, s, pl.ds(0, chans * height)] = near[:, :width]
        wide[2, s, pl.ds(0, chans * height)] = near[:, width:]
        if pad > chans:
            for b in range(3):
                wide[b, s, pl.ds(chans * height, (pad - chans) * height)] = jnp.zeros(
                    ((pad - chans) * height, width), F32
                )

    for l in range(-1, size + 1):
        at = 0 if l < 0 else 1 if l == size else EXTRA + l
        for b in range(3):
            pair = [wide[b, s, pl.ds(at, pad, stride=height), :] for s in range(2)]
            packed[b, l + 1] = jnp.concatenate(pair, axis=0).astype(BF16)

    for copy in copies:
        copy.wait()
    rows_i = lax.broadcasted_iota(jnp.int32, (size, width), 0) + top
    centre = (rows_i + 1) * (width + 2) + lanes_of((size, width)) + 1
    along_y = table[0] - centre
    along_x = table[1] - centre
    turned = jnp.abs(along_x) == 1
    mask[0] = jnp.where(jnp.where(turned, along_y, along_x) < 0, 1.0, 0.0)
    mask[1] = jnp.where(jnp.where(turned, along_x, along_y) < 0, 1.0, 0.0)
    mask[2] = jnp.where(turned, 1.0, 0.0)

    def choose(m, a, b):
        return jnp.where(m, a, b), jnp.where(m, b, a)

    rows_step = even.shape[1] // width

    def stack(n, dst):
        for u in range(rows_step):
            l = n * rows_step + u
            m = []
            for k in range(3):
                line = jnp.broadcast_to(mask[k, pl.ds(l, 1), :], (16, width)).astype(BF16)
                m.append(jnp.concatenate([line] * (both // 16), axis=0) > 0.5)
            x = [[packed[bb, l + aa] for bb in range(3)] for aa in range(3)]
            for bb in range(3):
                x[0][bb], x[2][bb] = choose(m[0], x[2][bb], x[0][bb])
            for aa in range(3):
                x[aa][0], x[aa][2] = choose(m[1], x[aa][2], x[aa][0])
            for aa, bb in ((0, 1), (0, 2), (1, 2)):
                x[aa][bb], x[bb][aa] = choose(m[2], x[bb][aa], x[aa][bb])
            for k in range(9):
                dst[pl.ds(k * both, both), pl.ds(u * width, width)] = x[k // 3][k % 3]

    dot = functools.partial(
        lax.dot_general,
        dimension_numbers=(((1,), (0,)), ((), ())),
        preferred_element_type=F32,
    )

    def silu(v):
        return (v * jnp.tanh(v) + v).astype(BF16)

    def network(n, src):
        first = silu(dot(w1_ref[...], src[...]))
        second = silu(dot(w2_ref[...], first))
        tend = dot(w3_ref[...], second)
        for u in range(rows_step):
            l = n * rows_step + u
            cols = slice(u * width, (u + 1) * width)
            terms[0, pl.ds(l, chans, stride=size), :] = tend[0:chans, cols]
            terms[1, pl.ds(l, chans, stride=size), :] = tend[pad : pad + chans, cols]

    steps = size // rows_step
    slots = (even, odd)
    stack(0, even)
    for n in range(steps):
        if n + 1 < steps:
            stack(n + 1, slots[(n + 1) % 2])
        network(n, slots[n % 2])
    other_ref[...] = terms[1].astype(BF16)
    fetch.wait()
    patch[...] = patch[...] + terms[0].reshape(patch.shape)
    put = pltpu.make_async_copy(patch, image_ref.at[:, pl.ds(top, size)], sem.at[3])
    put.start()
    put.wait()


def finish_kernel(back_ref, image_in, image_ref, patch, back, sem, *, start, parts):
    chans, size, width = patch.shape
    half = image_in.shape[1] // 2
    rows = pl.ds((1 - lax.axis_index("group")) * half + start, size)
    some = chans // parts
    fetch = []
    for n in range(parts):
        c, r = pl.ds(n * some, some), pl.ds(n * some * size, some * size)
        fetch.append(
            (
                pltpu.make_async_copy(back_ref.at[r], back.at[r], sem.at[n]),
                pltpu.make_async_copy(image_in.at[c, rows], patch.at[c], sem.at[parts + n]),
            )
        )
        for copy in fetch[-1]:
            copy.start()
    put = []
    for n in range(parts):
        for copy in fetch[n]:
            copy.wait()
        c = pl.ds(n * some, some)
        terms = back[pl.ds(n * some * size, some * size)].astype(F32)
        patch[c] = patch[c] + terms.reshape(some, size, width)
        put.append(pltpu.make_async_copy(patch.at[c], image_ref.at[c, rows], sem.at[2 * parts + n]))
        put[-1].start()
    for copy in put:
        copy.wait()


def call(kernel, outs, ins, scratch=(), flops=10**9, out_specs=None, aliases=None, limit=24):
    return pl.pallas_call(
        kernel,
        out_shape=jax.tree.map(lambda x: jax.ShapeDtypeStruct(x.shape, x.dtype), outs),
        in_specs=ins,
        out_specs=jax.tree.map(lambda _: VMEM_SPEC, outs) if out_specs is None else out_specs,
        input_output_aliases=aliases or {},
        scratch_shapes=list(scratch),
        compiler_params=pltpu.CompilerParams(vmem_limit_bytes=limit << 20),
        cost_estimate=pl.CostEstimate(flops=flops, bytes_accessed=10**6, transcendentals=0),
    )


def shards(state, courant_x, courant_y, diffusion, neighbours, w_in, w_mid, w_out):
    levels, fields, single, cells_x, cells_y = state.shape
    chans = levels * fields
    hidden = w_mid.shape[0]
    tiles = lax.axis_size("tile")
    pad = -(-chans // 8) * 8
    block = state.reshape(chans, cells_x, cells_y)
    sds = jax.ShapeDtypeStruct

    strip = sds((chans, 8, cells_y), BF16)
    to_east, to_west, rows = call(edge_kernel, (strip, strip, strip), [VMEM_SPEC])(block)

    def beside(by):
        return [(i, i + by) for i in range(tiles) if 0 <= i % TILE_ROWS + by < TILE_ROWS]

    from_west = lax.ppermute(to_east, "tile", beside(1))
    from_east = lax.ppermute(to_west, "tile", beside(-1))

    def flat(x):
        return x.reshape(-1, cells_y)

    message, columns = call(
        functools.partial(pack_kernel, chans=chans),
        (sds((chans * 8, cells_y), BF16), sds((10, chans, cells_y), F32)),
        [VMEM_SPEC] * 5,
        [pltpu.VMEM((5, chans * 8, cells_y), F32)],
    )(flat(rows), flat(from_west), flat(from_east), flat(to_west), flat(to_east))

    def across(x, by):
        return lax.ppermute(x, "tile", [(i, (i + by) % tiles) for i in range(tiles)])

    up = across(message, TILE_ROWS)
    down = up if tiles == 2 * TILE_ROWS else across(message, -TILE_ROWS)

    ax = jnp.repeat(courant_x, fields)
    ay = jnp.repeat(courant_y, fields)
    nu = jnp.tile(diffusion, levels)
    coef = jnp.stack(
        [
            1.0 - jnp.abs(ax) - jnp.abs(ay) - 4.0 * nu,
            jnp.maximum(ax, 0.0) + nu,
            nu - jnp.minimum(ax, 0.0),
            jnp.maximum(ay, 0.0) + nu,
            nu - jnp.minimum(ay, 0.0),
        ]
    )

    quarter = cells_x // 4
    chunks = [(n * quarter, quarter) for n in range(2)]
    tall = pltpu.VMEM((chans, cells_x + 2 * MARGIN, cells_y), F32)

    def transport(jobs, ahead):
        heights = [chans * (EXTRA + size) for _, _, size in jobs]
        packets = [sds((height, cells_y), BF16) for height in heights]
        moved = () if ahead else (sds((chans, cells_x, cells_y), F32),)
        return call(
            functools.partial(transport_kernel, chans=chans, jobs=jobs, ahead=ahead),
            (*moved, *packets),
            [ANY_SPEC, pl.BlockSpec(memory_space=pltpu.SMEM)] + [VMEM_SPEC] * 2 + [ANY_SPEC] * 2,
            [pltpu.VMEM((height, cells_y), F32) for height in heights]
            + [
                pltpu.VMEM((2, chans * 8, cells_y), F32),
                tall,
                tall,
                tall,
                pltpu.VMEM((2, 2, 2, chans, cells_y), F32),
                pltpu.VMEM((4 * cells_y, 2 * cells_y), BF16),
                pltpu.VMEM(up.shape, BF16),
                pltpu.VMEM(up.shape, BF16),
                pltpu.SemaphoreType.DMA((3 + chans,)),
            ],
            flops=5 * 10**9,
            out_specs=(ANY_SPEC,) * len(moved) + (VMEM_SPEC,) * len(jobs),
        )(block, coef, coef.T, columns, up, down)

    def swap(x):
        return lax.ppermute(x, "group", [(0, 1), (1, 0)])

    (packet,) = transport([(1, *chunks[0])], True)
    got = [swap(packet)]
    image, *packets = transport(
        [(1, *chunk) for chunk in chunks[1:]] + [(0, *chunk) for chunk in chunks], False
    )
    theirs, mine = packets[: len(chunks) - 1], packets[len(chunks) - 1 :]
    got += [swap(packet) for packet in theirs]

    own = lax.axis_index("group")
    both = 2 * pad

    def ordered(w):
        return jnp.where(own == 0, w, w[::-1])

    w1 = ordered((w_in * 0.5).reshape(2, chans, 9, hidden)).transpose(3, 2, 0, 1)
    w1 = jnp.pad(w1, ((0, 0), (0, 0), (0, 0), (0, pad - chans))).reshape(hidden, 9 * both)
    w3 = ordered(w_out.T.reshape(2, chans, hidden))
    w3 = jnp.pad(w3, ((0, 0), (0, pad - chans), (0, 0))).reshape(both, hidden)
    w2 = (w_mid * 0.5).T

    parts = 4 if chans % 4 == 0 else 1
    back = []
    for n, (start, size) in enumerate(chunks):
        depth = 8 * (-(-chans // 8)) * (EXTRA + size)
        wide = pltpu.VMEM((3, 2, depth, cells_y), F32)
        blocks = pltpu.VMEM((9 * both, min(BLOCK_ROWS, size) * cells_y), BF16)
        image, other = call(
            functools.partial(physics_kernel, start=start, chans=chans),
            (image, sds((chans * size, cells_y), BF16)),
            [ANY_SPEC] + [VMEM_SPEC] * 4 + [ANY_SPEC] * 2,
            [
                wide,
                pltpu.VMEM((3, size + 2, both, cells_y), BF16),
                pltpu.VMEM((3, size, cells_y), F32),
                pltpu.VMEM((2, size, cells_y), jnp.int32),
                blocks,
                blocks,
                pltpu.VMEM((2, chans * size, cells_y), F32),
                pltpu.VMEM((chans, size, cells_y), F32),
                pltpu.VMEM((chans * (EXTRA + size), cells_y), BF16),
                pltpu.SemaphoreType.DMA((5,)),
            ],
            flops=7 * 10**9,
            out_specs=(ANY_SPEC, VMEM_SPEC),
            aliases={6: 0},
        )(neighbours, w1, w2, w3, mine[n], got[n], image)
        back.append(swap(other))
    for n, (start, size) in enumerate(chunks):
        image = call(
            functools.partial(finish_kernel, start=start, parts=parts),
            image,
            [ANY_SPEC, ANY_SPEC],
            [
                pltpu.VMEM((chans, size, cells_y), F32),
                pltpu.VMEM((chans * size, cells_y), BF16),
                pltpu.SemaphoreType.DMA((3 * parts,)),
            ],
            out_specs=ANY_SPEC,
            aliases={1: 0},
            limit=4,
        )(back[n], image)
    return image.reshape(levels, fields, single, cells_x, cells_y)


def solution(mesh):
    return jax.shard_map(
        shards,
        mesh=mesh,
        in_specs=(
            P("group", None, "tile", None, None),
            P("group"),
            P("group"),
            P(),
            P(None, "tile", None, None),
            P(),
            P(),
            P(),
        ),
        out_specs=P("group", None, "tile", None, None),
        check_vma=False,
    )
```

```python
import functools

import jax
import jax.numpy as jnp
from jax import lax
from jax.experimental import pallas as pl
from jax.experimental.pallas import tpu as pltpu
from jax.sharding import PartitionSpec as P


TILE_ROWS = 8
DEEP = 3
EXTRA = 8
BLOCK_ROWS = 16
MARGIN = 16
GROUP = 4

F32 = jnp.float32
BF16 = jnp.bfloat16
VMEM_SPEC = pl.BlockSpec(memory_space=pltpu.VMEM)
ANY_SPEC = pl.BlockSpec(memory_space=pl.ANY)


def lanes_of(shape):
    return lax.broadcasted_iota(jnp.int32, shape, len(shape) - 1)


def first_row(q, n, quarter):
    return quarter * (1 + q) if n == 0 else 3 * quarter * q


def edge_kernel(source_ref, east_ref, west_ref, rows_ref, state_ref, sem):
    chans, cells_x, cells_y = state_ref.shape
    parts = sem.shape[0]
    some = chans // parts
    fetch = [
        pltpu.make_async_copy(
            source_ref.at[pl.ds(n * some, some)], state_ref.at[pl.ds(n * some, some)], sem.at[n]
        )
        for n in range(parts)
    ]
    for copy in fetch:
        copy.start()
    slot = lax.broadcasted_iota(jnp.int32, (16, cells_y), 0)
    lane = lanes_of((16, cells_y))
    wanted = jnp.where(slot < 8, slot + cells_y - DEEP, slot - 8)
    valid = (slot % 8) < DEEP
    pick = jnp.where(valid & (lane == wanted), 1.0, 0.0).astype(BF16)
    for c in range(chans):
        if c % some == 0:
            fetch[c // some].wait()
        block = state_ref[c].astype(BF16)
        strips = lax.dot_general(
            pick, block, (((1,), (1,)), ((), ())), preferred_element_type=F32
        ).astype(BF16)
        east_ref[c] = strips[0:8]
        west_ref[c] = strips[8:16]
        rows_ref[c] = jnp.concatenate(
            [state_ref[c, 0:DEEP], state_ref[c, cells_x - DEEP : cells_x], state_ref[c, 0:2]], axis=0
        ).astype(BF16)


def pack_kernel(rows_ref, west_in, east_in, west_own, east_own, out_ref, column_ref, wide, *, chans):
    width = rows_ref.shape[1]
    lane = lanes_of((chans, width))
    for n, ref in enumerate((rows_ref, west_in, east_in, west_own, east_own)):
        wide[n] = ref[...].astype(F32)
    sources = [(1, 0), (1, 1), (1, 2), (3, 0), (3, 1), (4, 1), (4, 2), (2, 0), (2, 1), (2, 2)]
    corner = jnp.zeros((chans, width), F32)
    for k, (n, slot) in enumerate(sources):
        line = wide[n, pl.ds(slot, chans, stride=8), :]
        column_ref[k] = line
        at = 2 * DEEP * k
        corner = jnp.where(
            (lane >= at) & (lane < at + 2 * DEEP), pltpu.roll(line, at + DEEP, 1), corner
        )
    wide[0, pl.ds(2 * DEEP, chans, stride=8), :] = corner
    out_ref[...] = wide[0].astype(BF16)


def shift_matrix(width):
    k = lax.broadcasted_iota(jnp.int32, (4 * width, 2 * width), 0)
    n = lax.broadcasted_iota(jnp.int32, (4 * width, 2 * width), 1)
    m = k % width
    lower = (n < width) & (n == m + 1)
    upper = (n >= width) & (n - width == m - 1)
    west = (k >= 2 * width) & (k < 3 * width) & (n == 0)
    east = (k >= 3 * width) & (n == 2 * width - 1)
    return jnp.where(((k < 2 * width) & (lower | upper)) | west | east, 1.0, 0.0).astype(BF16)


def transport_kernel(state_ref, speed_ref, coef_ref, column_ref, *rest, chans, jobs, size, ahead):
    count = len(jobs)
    halos, rest = ((), rest) if ahead else (rest[:2], rest[2:])
    packets, rest = rest[:count], rest[count:]
    quarters, rest = ((), rest) if ahead else (rest[:4], rest[4:])
    windows, rest = rest[:count], rest[count:]
    border, raw_s, once_s, last_s, line_s, matrix, sem = rest
    cells_x, width = state_ref.shape[1:]
    own = lax.axis_index("group")
    place = lax.axis_index("tile") % TILE_ROWS
    half_of = (own, 1 - own)
    base_of = [first_row(half_of[whose], n, size) for whose, n in jobs]
    fetch = pltpu.make_async_copy(state_ref, raw_s.at[:, pl.ds(MARGIN, cells_x)], sem.at[0])
    fetch.start()
    matrix[...] = shift_matrix(width)
    lane = lanes_of((chans, width))
    first, last = lane == 0, lane == width - 1
    low_lanes = lane < width // 2
    for s, ref in enumerate(halos):
        border[s] = ref[...].astype(F32)
    coefs = [jnp.broadcast_to(coef_ref[:, n : n + 1], (chans, width)) for n in range(5)]
    message = border.shape[1] // chans

    if ahead:
        corners = jnp.zeros((chans, width), F32)
    else:
        above, below = [border[s, pl.ds(2 * DEEP, chans, stride=message), :] for s in range(2)]
        corners = jnp.where(lane % (2 * DEEP) < DEEP, above, below)

    def pair(k):
        return column_ref[k], roll(corners, width - (2 * DEEP * k + DEEP))

    def roll(x, by):
        return pltpu.roll(x, by, 1)

    def both_ways(main, aux):
        ml, al = roll(main, 1), roll(aux, 1)
        mu, au = roll(main, width - 1), roll(aux, width - 1)
        lower = jnp.where(first, al, ml), jnp.where(first, ml, al)
        upper = jnp.where(last, au, mu), jnp.where(last, mu, au)
        return lower, upper

    def column(west, mid, east, keep):
        c0, cxl, cxu, cyl, cyu = coefs
        lower, upper = both_ways(*mid)
        return tuple(
            (c0 * mid[n] + cxl * lower[n] + cxu * upper[n] + cyl * west[n] + cyu * east[n]) * keep
            for n in range(2)
        )

    keeps = (
        jnp.where(place == 0, 0.0, 1.0),
        jnp.where(place == TILE_ROWS - 1, 0.0, 1.0),
    )
    edges = []
    for side in range(2):
        raw = [pair(5 * side + k) for k in range(5)]
        keep = keeps[side]
        inside = 3 if side == 0 else 1
        once = [
            column(raw[k - 1], raw[k], raw[k + 1], 1.0 if k == inside else keep)
            for k in (1, 2, 3)
        ]
        main, aux = column(once[0], once[1], once[2], keep)
        for level, edge in enumerate((raw[2], once[1])):
            for n in range(2):
                line_s[level, side, n] = edge[n]
        edges.append((main, aux))
    for window, base in zip(windows, base_of):
        at = base - 1
        sides = []
        for side, first_lane in enumerate((0, width // 2)):
            main, aux = edges[side]
            by = lax.rem(first_lane - at + width, width)
            row_of = lane - first_lane + at
            off = (row_of < 0) | (row_of >= cells_x)
            sides.append(jnp.where(off, roll(aux, by), roll(main, by)))
        window[pl.ds(2, chans, stride=EXTRA + size), :] = jnp.where(low_lanes, *sides)

    rows = size + 16 if ahead else cells_x + 16
    origin = base_of[0] - 8 if ahead else -8
    top = pl.multiple_of(origin + MARGIN, 8) if ahead else 8
    at = lax.broadcasted_iota(jnp.int32, (rows, width), 0) + origin
    diagonal = lax.rem(at + width, width) == lanes_of((rows, width))
    within = (at >= 0) & (at < cells_x)
    fetch.wait()
    group = next(n for n in (10 if ahead else GROUP, 2, 1) if chans % n == 0)

    def sweep(level, src, dst, base):
        parts = []
        for g in range(group):
            c = base + g
            q = src[c, pl.ds(top, rows), :]
            hi = q.astype(BF16)
            lo = (q - hi.astype(F32)).astype(BF16)
            sides = []
            for side in range(2):
                main = line_s[level, side, 0, pl.ds(c, 1), :]
                aux = line_s[level, side, 1, pl.ds(c, 1), :]
                values = jnp.where(within, main, aux)
                sides.append(jnp.where(diagonal, values, 0.0).astype(BF16))
            parts.append(jnp.concatenate([hi, lo] + sides, axis=1))
        near = lax.dot_general(
            jnp.concatenate(parts, axis=0),
            matrix[...],
            (((1,), (0,)), ((), ())),
            preferred_element_type=F32,
        )
        for g in range(group):
            c = base + g
            lower, upper = near[g * rows : (g + 1) * rows, :width], near[g * rows : (g + 1) * rows, width:]
            c0, cxl, cxu, cyl, cyu = [speed_ref[n, c] for n in range(5)]
            dst[c, pl.ds(top, rows), :] = (
                c0 * src[c, pl.ds(top, rows), :]
                + cxl * src[c, pl.ds(top - 1, rows), :]
                + cxu * src[c, pl.ds(top + 1, rows), :]
                + cyl * lower
                + cyu * upper
            )

    def finish(base):
        for g in range(group):
            c = base + g
            for window, row in zip(windows, base_of):
                at = MARGIN + row
                to = c * (EXTRA + size)
                window[pl.ds(to, 1), :] = last_s[c, pl.ds(at - 1, 1), :]
                window[pl.ds(to + 1, 1), :] = last_s[c, pl.ds(at + size, 1), :]
                window[pl.ds(to + EXTRA, size), :] = last_s[c, pl.ds(pl.multiple_of(at, 8), size), :]
            for k, quarter in enumerate(quarters):
                at = pl.multiple_of(MARGIN + first_row(half_of[k // 2], k % 2, size), 8)
                quarter[pl.ds(c * size, size), :] = last_s[c, pl.ds(at, size), :]

    for c in range(0 if ahead else chans):
        raw_s[c, pl.ds(MARGIN - DEEP, DEEP), :] = border[0, pl.ds(c * message + DEEP, DEEP), :]
        raw_s[c, pl.ds(MARGIN + cells_x, DEEP), :] = border[1, pl.ds(c * message, DEEP), :]
    for base in range(0, chans + group, group):
        if base < chans:
            sweep(0, raw_s, once_s, base)
        if base:
            sweep(1, once_s, last_s, base - group)
            finish(base - group)
    for packet, window in zip(packets, windows):
        packet[...] = window[...].astype(BF16)


def physics_kernel(chunk, table_ref, w1_ref, w2_ref, w3_ref, mine_ref, got_ref, kept_ref, *rest, chans):
    (
        image_ref, other_ref, wide, packed, mask, table, even, odd, terms, patch, got, sem
    ) = rest[-12:]
    size, width = table.shape[1:]
    height = EXTRA + size
    pad = -(-chans // 8) * 8
    both = 2 * pad
    top = first_row(lax.axis_index("group"), chunk, size)
    copies = [
        pltpu.make_async_copy(table_ref.at[k, 0, pl.ds(top, size)], table.at[n], sem.at[n])
        for n, k in enumerate((5, 7))
    ]
    arrive = pltpu.make_async_copy(got_ref, got, sem.at[2])
    for copy in copies:
        copy.start()
    arrive.start()

    k = lax.broadcasted_iota(jnp.int32, (2 * width, 2 * width), 0)
    n = lax.broadcasted_iota(jnp.int32, (2 * width, 2 * width), 1)
    inner = (k < width) & (((n < width) & (n == k + 1)) | ((n >= width) & (n - width == k - 1)))
    west = (k >= width) & (k < width + width // 2) & (n == 0)
    east = (k >= width + width // 2) & (n == 2 * width - 1)
    matrix = jnp.where(inner | west | east, 1.0, 0.0).astype(BF16)
    slot = lax.broadcasted_iota(jnp.int32, (height, width), 0)
    line = jnp.where(
        slot >= EXTRA, slot - EXTRA + 1, jnp.where(slot == 0, 0, jnp.where(slot == 1, size + 1, -1))
    )
    diagonal = lanes_of((height, width)) % (width // 2) == line
    for s, ref in enumerate((mine_ref, got)):
        if s == 1:
            arrive.wait()
        cells = ref[...]
        flat = cells.astype(F32)
        wide[1, s, pl.ds(0, chans * height)] = flat
        edges = [
            jnp.where(diagonal, flat[c * height + 2 : c * height + 3], 0.0) for c in range(chans)
        ]
        edges = jnp.concatenate(edges, axis=0).astype(BF16)
        near = lax.dot_general(
            jnp.concatenate([cells, edges], axis=1),
            matrix,
            (((1,), (0,)), ((), ())),
            preferred_element_type=F32,
        )
        wide[0, s, pl.ds(0, chans * height)] = near[:, :width]
        wide[2, s, pl.ds(0, chans * height)] = near[:, width:]
        if pad > chans:
            for b in range(3):
                wide[b, s, pl.ds(chans * height, (pad - chans) * height)] = jnp.zeros(
                    ((pad - chans) * height, width), F32
                )

    for l in range(-1, size + 1):
        at = 0 if l < 0 else 1 if l == size else EXTRA + l
        for b in range(3):
            pair = [wide[b, s, pl.ds(at, pad, stride=height), :] for s in range(2)]
            packed[b, l + 1] = jnp.concatenate(pair, axis=0).astype(BF16)

    for copy in copies:
        copy.wait()
    rows_i = lax.broadcasted_iota(jnp.int32, (size, width), 0) + top
    centre = (rows_i + 1) * (width + 2) + lanes_of((size, width)) + 1
    along_y = table[0] - centre
    along_x = table[1] - centre
    turned = jnp.abs(along_x) == 1
    mask[0] = jnp.where(jnp.where(turned, along_y, along_x) < 0, 1.0, 0.0)
    mask[1] = jnp.where(jnp.where(turned, along_x, along_y) < 0, 1.0, 0.0)
    mask[2] = jnp.where(turned, 1.0, 0.0)

    def choose(m, a, b):
        return jnp.where(m, a, b), jnp.where(m, b, a)

    rows_step = even.shape[1] // width

    def stack(n, dst):
        for u in range(rows_step):
            l = n * rows_step + u
            m = []
            for k in range(3):
                line = jnp.broadcast_to(mask[k, pl.ds(l, 1), :], (16, width)).astype(BF16)
                m.append(jnp.concatenate([line] * (both // 16), axis=0) > 0.5)
            x = [[packed[bb, l + aa] for bb in range(3)] for aa in range(3)]
            for bb in range(3):
                x[0][bb], x[2][bb] = choose(m[0], x[2][bb], x[0][bb])
            for aa in range(3):
                x[aa][0], x[aa][2] = choose(m[1], x[aa][2], x[aa][0])
            for aa, bb in ((0, 1), (0, 2), (1, 2)):
                x[aa][bb], x[bb][aa] = choose(m[2], x[bb][aa], x[aa][bb])
            for k in range(9):
                dst[pl.ds(k * both, both), pl.ds(u * width, width)] = x[k // 3][k % 3]

    dot = functools.partial(
        lax.dot_general,
        dimension_numbers=(((1,), (0,)), ((), ())),
        preferred_element_type=F32,
    )

    def silu(v):
        return (v * jnp.tanh(v) + v).astype(BF16)

    def network(n, src):
        first = silu(dot(w1_ref[...], src[...]))
        second = silu(dot(w2_ref[...], first))
        tend = dot(w3_ref[...], second)
        for u in range(rows_step):
            l = n * rows_step + u
            cols = slice(u * width, (u + 1) * width)
            terms[0, pl.ds(l, chans, stride=size), :] = tend[0:chans, cols]
            terms[1, pl.ds(l, chans, stride=size), :] = tend[pad : pad + chans, cols]

    steps = size // rows_step
    slots = (even, odd)
    stack(0, even)
    for n in range(steps):
        if n + 1 < steps:
            stack(n + 1, slots[(n + 1) % 2])
        network(n, slots[n % 2])
    other_ref[...] = terms[1].astype(BF16)
    patch[...] = (kept_ref[...] + terms[0]).reshape(patch.shape)
    put = pltpu.make_async_copy(patch, image_ref.at[:, pl.ds(top, size)], sem.at[3])
    put.start()
    put.wait()


def finish_kernel(chunk, back_ref, moved_ref, image_in, image_ref, patch, sem, *, parts):
    chans, size, width = patch.shape
    rows = pl.ds(first_row(1 - lax.axis_index("group"), chunk, size), size)
    some = chans // parts
    put = []
    for n in range(parts):
        c, r = pl.ds(n * some, some), pl.ds(n * some * size, some * size)
        patch[c] = (moved_ref[r] + back_ref[r].astype(F32)).reshape(some, size, width)
        put.append(pltpu.make_async_copy(patch.at[c], image_ref.at[c, rows], sem.at[n]))
        put[-1].start()
    for copy in put:
        copy.wait()


def call(kernel, outs, ins, scratch=(), flops=10**9, out_specs=None, aliases=None, limit=24):
    return pl.pallas_call(
        kernel,
        out_shape=jax.tree.map(lambda x: jax.ShapeDtypeStruct(x.shape, x.dtype), outs),
        in_specs=ins,
        out_specs=jax.tree.map(lambda _: VMEM_SPEC, outs) if out_specs is None else out_specs,
        input_output_aliases=aliases or {},
        scratch_shapes=list(scratch),
        compiler_params=pltpu.CompilerParams(vmem_limit_bytes=limit << 20),
        cost_estimate=pl.CostEstimate(flops=flops, bytes_accessed=10**6, transcendentals=0),
    )


def shards(state, courant_x, courant_y, diffusion, neighbours, w_in, w_mid, w_out):
    levels, fields, single, cells_x, cells_y = state.shape
    chans = levels * fields
    hidden = w_mid.shape[0]
    tiles = lax.axis_size("tile")
    pad = -(-chans // 8) * 8
    block = state.reshape(chans, cells_x, cells_y)
    sds = jax.ShapeDtypeStruct

    strip = sds((chans, 8, cells_y), BF16)
    to_east, to_west, rows = call(
        edge_kernel,
        (strip, strip, strip),
        [pl.BlockSpec(memory_space=pltpu.HBM)],
        [pltpu.VMEM(block.shape, F32), pltpu.SemaphoreType.DMA((chans // 2,))],
    )(block)

    def beside(by):
        return [(i, i + by) for i in range(tiles) if 0 <= i % TILE_ROWS + by < TILE_ROWS]

    from_west = lax.ppermute(to_east, "tile", beside(1))
    from_east = lax.ppermute(to_west, "tile", beside(-1))

    def flat(x):
        return x.reshape(-1, cells_y)

    message, columns = call(
        functools.partial(pack_kernel, chans=chans),
        (sds((chans * 8, cells_y), BF16), sds((10, chans, cells_y), F32)),
        [VMEM_SPEC] * 5,
        [pltpu.VMEM((5, chans * 8, cells_y), F32)],
    )(flat(rows), flat(from_west), flat(from_east), flat(to_west), flat(to_east))

    def across(x, by):
        return lax.ppermute(x, "tile", [(i, (i + by) % tiles) for i in range(tiles)])

    up = across(message, TILE_ROWS)
    down = up if tiles == 2 * TILE_ROWS else across(message, -TILE_ROWS)

    ax = jnp.repeat(courant_x, fields)
    ay = jnp.repeat(courant_y, fields)
    nu = jnp.tile(diffusion, levels)
    coef = jnp.stack(
        [
            1.0 - jnp.abs(ax) - jnp.abs(ay) - 4.0 * nu,
            jnp.maximum(ax, 0.0) + nu,
            nu - jnp.minimum(ax, 0.0),
            jnp.maximum(ay, 0.0) + nu,
            nu - jnp.minimum(ay, 0.0),
        ]
    )

    size = cells_x // 4
    tall = pltpu.VMEM((chans, cells_x + 2 * MARGIN, cells_y), F32)
    height = chans * (EXTRA + size)
    moved = sds((chans * size, cells_y), F32)

    def transport(jobs, *halos):
        ahead = len(halos) == 0
        return call(
            functools.partial(transport_kernel, chans=chans, jobs=jobs, size=size, ahead=ahead),
            (sds((height, cells_y), BF16),) * len(jobs) + (() if ahead else (moved,) * 4),
            [ANY_SPEC, pl.BlockSpec(memory_space=pltpu.SMEM)] + [VMEM_SPEC] * (2 + len(halos)),
            [pltpu.VMEM((height, cells_y), F32) for _ in jobs]
            + [
                pltpu.VMEM((2, chans * 8, cells_y), F32),
                tall,
                tall,
                tall,
                pltpu.VMEM((2, 2, 2, chans, cells_y), F32),
                pltpu.VMEM((4 * cells_y, 2 * cells_y), BF16),
                pltpu.SemaphoreType.DMA((1,)),
            ],
            flops=5 * 10**9,
        )(block, coef, coef.T, columns, *halos)

    def swap(x):
        return lax.ppermute(x, "group", [(0, 1), (1, 0)])

    (theirs0,) = transport([(1, 0)])
    theirs1, *rest = transport([(1, 1), (0, 0), (0, 1)], up, down)
    mine, kept, others = rest[:2], rest[2:4], rest[4:]
    got = [swap(theirs0), swap(theirs1)]

    own = lax.axis_index("group")
    both = 2 * pad

    def ordered(w):
        return jnp.where(own == 0, w, w[::-1])

    w1 = ordered((w_in * 0.5).reshape(2, chans, 9, hidden)).transpose(3, 2, 0, 1)
    w1 = jnp.pad(w1, ((0, 0), (0, 0), (0, 0), (0, pad - chans))).reshape(hidden, 9 * both)
    w3 = ordered(w_out.T.reshape(2, chans, hidden))
    w3 = jnp.pad(w3, ((0, 0), (0, pad - chans), (0, 0))).reshape(both, hidden)
    w2 = (w_mid * 0.5).T

    back = []
    image = None
    blocks = pltpu.VMEM((9 * both, BLOCK_ROWS * cells_y), BF16)
    whole = sds((chans, cells_x, cells_y), F32)
    for n in range(2):
        images = () if image is None else (image,)
        image, other = call(
            functools.partial(physics_kernel, n, chans=chans),
            (whole, sds((chans * size, cells_y), BF16)),
            [ANY_SPEC] + [VMEM_SPEC] * 4 + [ANY_SPEC, VMEM_SPEC] + [ANY_SPEC] * len(images),
            [
                pltpu.VMEM((3, 2, pad * (EXTRA + size), cells_y), F32),
                pltpu.VMEM((3, size + 2, both, cells_y), BF16),
                pltpu.VMEM((3, size, cells_y), F32),
                pltpu.VMEM((2, size, cells_y), jnp.int32),
                blocks,
                blocks,
                pltpu.VMEM((2, chans * size, cells_y), F32),
                pltpu.VMEM((chans, size, cells_y), F32),
                pltpu.VMEM((height, cells_y), BF16),
                pltpu.SemaphoreType.DMA((4,)),
            ],
            flops=7 * 10**9,
            out_specs=(ANY_SPEC, VMEM_SPEC),
            aliases={7: 0} if images else {},
        )(neighbours, w1, w2, w3, mine[n], got[n], kept[n], *images)
        back.append(swap(other))
    parts = 4 if chans % 4 == 0 else 1
    for n in range(2):
        image = call(
            functools.partial(finish_kernel, n, parts=parts),
            whole,
            [VMEM_SPEC, VMEM_SPEC, ANY_SPEC],
            [pltpu.VMEM((chans, size, cells_y), F32), pltpu.SemaphoreType.DMA((parts,))],
            out_specs=ANY_SPEC,
            aliases={2: 0},
            limit=4,
        )(back[n], others[n], image)
    return image.reshape(levels, fields, single, cells_x, cells_y)


def solution(mesh):
    return jax.shard_map(
        shards,
        mesh=mesh,
        in_specs=(
            P("group", None, "tile", None, None),
            P("group"),
            P("group"),
            P(),
            P(None, "tile", None, None),
            P(),
            P(),
            P(),
        ),
        out_specs=P("group", None, "tile", None, None),
        check_vma=False,
    )
```

```python
import functools

import jax
import jax.numpy as jnp
from jax import lax
from jax.experimental import pallas as pl
from jax.experimental.pallas import tpu as pltpu
from jax.sharding import PartitionSpec as P


TILE_ROWS = 8
DEEP = 3
EXTRA = 8
BLOCK_ROWS = 16
MARGIN = 16
GROUP = 4

F32 = jnp.float32
BF16 = jnp.bfloat16
VMEM_SPEC = pl.BlockSpec(memory_space=pltpu.VMEM)
ANY_SPEC = pl.BlockSpec(memory_space=pl.ANY)


def lanes_of(shape):
    return lax.broadcasted_iota(jnp.int32, shape, len(shape) - 1)


def first_row(q, n, quarter):
    return quarter * (1 + q) if n == 0 else 3 * quarter * q


def edge_kernel(state_ref, east_ref, west_ref, rows_ref):
    chans, cells_x, cells_y = state_ref.shape
    slot = lax.broadcasted_iota(jnp.int32, (16, cells_y), 0)
    lane = lanes_of((16, cells_y))
    wanted = jnp.where(slot < 8, slot + cells_y - DEEP, slot - 8)
    valid = (slot % 8) < DEEP
    pick = jnp.where(valid & (lane == wanted), 1.0, 0.0).astype(BF16)
    for c in range(chans):
        block = state_ref[c].astype(BF16)
        strips = lax.dot_general(
            pick, block, (((1,), (1,)), ((), ())), preferred_element_type=F32
        ).astype(BF16)
        east_ref[c] = strips[0:8]
        west_ref[c] = strips[8:16]
        rows_ref[c] = jnp.concatenate(
            [state_ref[c, 0:DEEP], state_ref[c, cells_x - DEEP : cells_x], state_ref[c, 0:2]], axis=0
        ).astype(BF16)


def pack_kernel(rows_ref, west_in, east_in, west_own, east_own, out_ref, column_ref, wide, *, chans):
    width = rows_ref.shape[1]
    lane = lanes_of((chans, width))
    for n, ref in enumerate((rows_ref, west_in, east_in, west_own, east_own)):
        wide[n] = ref[...].astype(F32)
    sources = [(1, 0), (1, 1), (1, 2), (3, 0), (3, 1), (4, 1), (4, 2), (2, 0), (2, 1), (2, 2)]
    corner = jnp.zeros((chans, width), F32)
    for k, (n, slot) in enumerate(sources):
        line = wide[n, pl.ds(slot, chans, stride=8), :]
        column_ref[k] = line
        at = 2 * DEEP * k
        corner = jnp.where(
            (lane >= at) & (lane < at + 2 * DEEP), pltpu.roll(line, at + DEEP, 1), corner
        )
    wide[0, pl.ds(2 * DEEP, chans, stride=8), :] = corner
    out_ref[...] = wide[0].astype(BF16)


def shift_matrix(width):
    k = lax.broadcasted_iota(jnp.int32, (4 * width, 2 * width), 0)
    n = lax.broadcasted_iota(jnp.int32, (4 * width, 2 * width), 1)
    m = k % width
    lower = (n < width) & (n == m + 1)
    upper = (n >= width) & (n - width == m - 1)
    west = (k >= 2 * width) & (k < 3 * width) & (n == 0)
    east = (k >= 3 * width) & (n == 2 * width - 1)
    return jnp.where(((k < 2 * width) & (lower | upper)) | west | east, 1.0, 0.0).astype(BF16)


def transport_kernel(state_ref, speed_ref, coef_ref, column_ref, *rest, chans, jobs, size, ahead):
    count = len(jobs)
    halos, rest = ((), rest) if ahead else (rest[:2], rest[2:])
    packets, rest = rest[:count], rest[count:]
    quarters, rest = ((), rest) if ahead else (rest[:4], rest[4:])
    windows, rest = rest[:count], rest[count:]
    border, raw_s, once_s, last_s, line_s, matrix, sem = rest
    cells_x, width = state_ref.shape[1:]
    own = lax.axis_index("group")
    place = lax.axis_index("tile") % TILE_ROWS
    half_of = (own, 1 - own)
    base_of = [first_row(half_of[whose], n, size) for whose, n in jobs]
    fetch = pltpu.make_async_copy(state_ref, raw_s.at[:, pl.ds(MARGIN, cells_x)], sem.at[0])
    if not ahead:
        fetch.start()
    matrix[...] = shift_matrix(width)
    lane = lanes_of((chans, width))
    first, last = lane == 0, lane == width - 1
    low_lanes = lane < width // 2
    for s, ref in enumerate(halos):
        border[s] = ref[...].astype(F32)
    coefs = [jnp.broadcast_to(coef_ref[:, n : n + 1], (chans, width)) for n in range(5)]
    message = border.shape[1] // chans

    if ahead:
        corners = jnp.zeros((chans, width), F32)
    else:
        above, below = [border[s, pl.ds(2 * DEEP, chans, stride=message), :] for s in range(2)]
        corners = jnp.where(lane % (2 * DEEP) < DEEP, above, below)

    def pair(k):
        return column_ref[k], roll(corners, width - (2 * DEEP * k + DEEP))

    def roll(x, by):
        return pltpu.roll(x, by, 1)

    def both_ways(main, aux):
        ml, al = roll(main, 1), roll(aux, 1)
        mu, au = roll(main, width - 1), roll(aux, width - 1)
        lower = jnp.where(first, al, ml), jnp.where(first, ml, al)
        upper = jnp.where(last, au, mu), jnp.where(last, mu, au)
        return lower, upper

    def column(west, mid, east, keep):
        c0, cxl, cxu, cyl, cyu = coefs
        lower, upper = both_ways(*mid)
        return tuple(
            (c0 * mid[n] + cxl * lower[n] + cxu * upper[n] + cyl * west[n] + cyu * east[n]) * keep
            for n in range(2)
        )

    keeps = (
        jnp.where(place == 0, 0.0, 1.0),
        jnp.where(place == TILE_ROWS - 1, 0.0, 1.0),
    )
    edges = []
    for side in range(2):
        raw = [pair(5 * side + k) for k in range(5)]
        keep = keeps[side]
        inside = 3 if side == 0 else 1
        once = [
            column(raw[k - 1], raw[k], raw[k + 1], 1.0 if k == inside else keep)
            for k in (1, 2, 3)
        ]
        main, aux = column(once[0], once[1], once[2], keep)
        for level, edge in enumerate((raw[2], once[1])):
            for n in range(2):
                line_s[level, side, n] = edge[n]
        edges.append((main, aux))
    for window, base in zip(windows, base_of):
        at = base - 1
        sides = []
        for side, first_lane in enumerate((0, width // 2)):
            main, aux = edges[side]
            by = lax.rem(first_lane - at + width, width)
            row_of = lane - first_lane + at
            off = (row_of < 0) | (row_of >= cells_x)
            sides.append(jnp.where(off, roll(aux, by), roll(main, by)))
        window[pl.ds(2, chans, stride=EXTRA + size), :] = jnp.where(low_lanes, *sides)

    rows = size + 16 if ahead else cells_x + 16
    origin = base_of[0] - 8 if ahead else -8
    top = pl.multiple_of(origin + MARGIN, 8) if ahead else 8
    at = lax.broadcasted_iota(jnp.int32, (rows, width), 0) + origin
    diagonal = lax.rem(at + width, width) == lanes_of((rows, width))
    within = (at >= 0) & (at < cells_x)
    if not ahead:
        fetch.wait()
    group = next(n for n in (10 if ahead else GROUP, 2, 1) if chans % n == 0)

    def sweep(level, src, dst, base):
        near_top = pl.multiple_of(origin, 8) if ahead and level == 0 else top
        parts = []
        for g in range(group):
            c = base + g
            q = src[c, pl.ds(near_top, rows), :]
            hi = q.astype(BF16)
            lo = (q - hi.astype(F32)).astype(BF16)
            sides = []
            for side in range(2):
                main = line_s[level, side, 0, pl.ds(c, 1), :]
                aux = line_s[level, side, 1, pl.ds(c, 1), :]
                values = jnp.where(within, main, aux)
                sides.append(jnp.where(diagonal, values, 0.0).astype(BF16))
            parts.append(jnp.concatenate([hi, lo] + sides, axis=1))
        near = lax.dot_general(
            jnp.concatenate(parts, axis=0),
            matrix[...],
            (((1,), (0,)), ((), ())),
            preferred_element_type=F32,
        )
        for g in range(group):
            c = base + g
            lower, upper = near[g * rows : (g + 1) * rows, :width], near[g * rows : (g + 1) * rows, width:]
            c0, cxl, cxu, cyl, cyu = [speed_ref[n, c] for n in range(5)]
            dst[c, pl.ds(top, rows), :] = (
                c0 * src[c, pl.ds(near_top, rows), :]
                + cxl * src[c, pl.ds(near_top - 1, rows), :]
                + cxu * src[c, pl.ds(near_top + 1, rows), :]
                + cyl * lower
                + cyu * upper
            )

    def finish(base):
        for g in range(group):
            c = base + g
            for window, row in zip(windows, base_of):
                at = MARGIN + row
                to = c * (EXTRA + size)
                window[pl.ds(to, 1), :] = last_s[c, pl.ds(at - 1, 1), :]
                window[pl.ds(to + 1, 1), :] = last_s[c, pl.ds(at + size, 1), :]
                window[pl.ds(to + EXTRA, size), :] = last_s[c, pl.ds(pl.multiple_of(at, 8), size), :]
            for k, quarter in enumerate(quarters):
                at = pl.multiple_of(MARGIN + first_row(half_of[k // 2], k % 2, size), 8)
                quarter[pl.ds(c * size, size), :] = last_s[c, pl.ds(at, size), :]

    for c in range(0 if ahead else chans):
        raw_s[c, pl.ds(MARGIN - DEEP, DEEP), :] = border[0, pl.ds(c * message + DEEP, DEEP), :]
        raw_s[c, pl.ds(MARGIN + cells_x, DEEP), :] = border[1, pl.ds(c * message, DEEP), :]
    for base in range(0, chans + group, group):
        if base < chans:
            sweep(0, state_ref if ahead else raw_s, once_s, base)
        if base:
            sweep(1, once_s, last_s, base - group)
            finish(base - group)
    for packet, window in zip(packets, windows):
        packet[...] = window[...].astype(BF16)


def physics_kernel(chunk, table_ref, w1_ref, w2_ref, w3_ref, mine_ref, got_ref, kept_ref, *rest, chans):
    (
        image_ref, other_ref, wide, packed, mask, table, even, odd, terms, patch, got, sem
    ) = rest[-12:]
    size, width = table.shape[1:]
    height = EXTRA + size
    pad = -(-chans // 8) * 8
    both = 2 * pad
    top = first_row(lax.axis_index("group"), chunk, size)
    copies = [
        pltpu.make_async_copy(table_ref.at[k, 0, pl.ds(top, size)], table.at[n], sem.at[n])
        for n, k in enumerate((5, 7))
    ]
    arrive = pltpu.make_async_copy(got_ref, got, sem.at[2])
    for copy in copies:
        copy.start()
    arrive.start()

    k = lax.broadcasted_iota(jnp.int32, (2 * width, 2 * width), 0)
    n = lax.broadcasted_iota(jnp.int32, (2 * width, 2 * width), 1)
    inner = (k < width) & (((n < width) & (n == k + 1)) | ((n >= width) & (n - width == k - 1)))
    west = (k >= width) & (k < width + width // 2) & (n == 0)
    east = (k >= width + width // 2) & (n == 2 * width - 1)
    matrix = jnp.where(inner | west | east, 1.0, 0.0).astype(BF16)
    slot = lax.broadcasted_iota(jnp.int32, (height, width), 0)
    line = jnp.where(
        slot >= EXTRA, slot - EXTRA + 1, jnp.where(slot == 0, 0, jnp.where(slot == 1, size + 1, -1))
    )
    diagonal = lanes_of((height, width)) % (width // 2) == line
    for s, ref in enumerate((mine_ref, got)):
        if s == 1:
            arrive.wait()
        cells = ref[...]
        flat = cells.astype(F32)
        wide[1, s, pl.ds(0, chans * height)] = flat
        edges = [
            jnp.where(diagonal, flat[c * height + 2 : c * height + 3], 0.0) for c in range(chans)
        ]
        edges = jnp.concatenate(edges, axis=0).astype(BF16)
        near = lax.dot_general(
            jnp.concatenate([cells, edges], axis=1),
            matrix,
            (((1,), (0,)), ((), ())),
            preferred_element_type=F32,
        )
        wide[0, s, pl.ds(0, chans * height)] = near[:, :width]
        wide[2, s, pl.ds(0, chans * height)] = near[:, width:]
        if pad > chans:
            for b in range(3):
                wide[b, s, pl.ds(chans * height, (pad - chans) * height)] = jnp.zeros(
                    ((pad - chans) * height, width), F32
                )

    for l in range(-1, size + 1):
        at = 0 if l < 0 else 1 if l == size else EXTRA + l
        for b in range(3):
            pair = [wide[b, s, pl.ds(at, pad, stride=height), :] for s in range(2)]
            packed[b, l + 1] = jnp.concatenate(pair, axis=0).astype(BF16)

    for copy in copies:
        copy.wait()
    rows_i = lax.broadcasted_iota(jnp.int32, (size, width), 0) + top
    centre = (rows_i + 1) * (width + 2) + lanes_of((size, width)) + 1
    along_y = table[0] - centre
    along_x = table[1] - centre
    turned = jnp.abs(along_x) == 1
    mask[0] = jnp.where(jnp.where(turned, along_y, along_x) < 0, 1.0, 0.0)
    mask[1] = jnp.where(jnp.where(turned, along_x, along_y) < 0, 1.0, 0.0)
    mask[2] = jnp.where(turned, 1.0, 0.0)

    def choose(m, a, b):
        return jnp.where(m, a, b), jnp.where(m, b, a)

    rows_step = even.shape[1] // width

    def stack(n, dst):
        for u in range(rows_step):
            l = n * rows_step + u
            m = []
            for k in range(3):
                line = jnp.broadcast_to(mask[k, pl.ds(l, 1), :], (16, width)).astype(BF16)
                m.append(jnp.concatenate([line] * (both // 16), axis=0) > 0.5)
            x = [[packed[bb, l + aa] for bb in range(3)] for aa in range(3)]
            for bb in range(3):
                x[0][bb], x[2][bb] = choose(m[0], x[2][bb], x[0][bb])
            for aa in range(3):
                x[aa][0], x[aa][2] = choose(m[1], x[aa][2], x[aa][0])
            for aa, bb in ((0, 1), (0, 2), (1, 2)):
                x[aa][bb], x[bb][aa] = choose(m[2], x[bb][aa], x[aa][bb])
            for k in range(9):
                dst[pl.ds(k * both, both), pl.ds(u * width, width)] = x[k // 3][k % 3]

    dot = functools.partial(
        lax.dot_general,
        dimension_numbers=(((1,), (0,)), ((), ())),
        preferred_element_type=F32,
    )

    def silu(v):
        return (v * jnp.tanh(v) + v).astype(BF16)

    def network(n, src):
        first = silu(dot(w1_ref[...], src[...]))
        second = silu(dot(w2_ref[...], first))
        tend = dot(w3_ref[...], second)
        for u in range(rows_step):
            l = n * rows_step + u
            cols = slice(u * width, (u + 1) * width)
            terms[0, pl.ds(l, chans, stride=size), :] = tend[0:chans, cols]
            terms[1, pl.ds(l, chans, stride=size), :] = tend[pad : pad + chans, cols]

    steps = size // rows_step
    slots = (even, odd)
    stack(0, even)
    for n in range(steps):
        if n + 1 < steps:
            stack(n + 1, slots[(n + 1) % 2])
        network(n, slots[n % 2])
    other_ref[...] = terms[1].astype(BF16)
    patch[...] = (kept_ref[...] + terms[0]).reshape(patch.shape)
    put = pltpu.make_async_copy(patch, image_ref.at[:, pl.ds(top, size)], sem.at[3])
    put.start()
    put.wait()


def finish_kernel(chunk, back_ref, moved_ref, image_in, image_ref, patch, sem, *, parts):
    chans, size, width = patch.shape
    rows = pl.ds(first_row(1 - lax.axis_index("group"), chunk, size), size)
    some = chans // parts
    put = []
    for n in range(parts):
        c, r = pl.ds(n * some, some), pl.ds(n * some * size, some * size)
        patch[c] = (moved_ref[r] + back_ref[r].astype(F32)).reshape(some, size, width)
        put.append(pltpu.make_async_copy(patch.at[c], image_ref.at[c, rows], sem.at[n]))
        put[-1].start()
    for copy in put:
        copy.wait()


def call(kernel, outs, ins, scratch=(), flops=10**9, out_specs=None, aliases=None, limit=24):
    return pl.pallas_call(
        kernel,
        out_shape=jax.tree.map(lambda x: jax.ShapeDtypeStruct(x.shape, x.dtype), outs),
        in_specs=ins,
        out_specs=jax.tree.map(lambda _: VMEM_SPEC, outs) if out_specs is None else out_specs,
        input_output_aliases=aliases or {},
        scratch_shapes=list(scratch),
        compiler_params=pltpu.CompilerParams(vmem_limit_bytes=limit << 20),
        cost_estimate=pl.CostEstimate(flops=flops, bytes_accessed=10**6, transcendentals=0),
    )


def shards(state, courant_x, courant_y, diffusion, neighbours, w_in, w_mid, w_out):
    levels, fields, single, cells_x, cells_y = state.shape
    chans = levels * fields
    hidden = w_mid.shape[0]
    tiles = lax.axis_size("tile")
    pad = -(-chans // 8) * 8
    block = state.reshape(chans, cells_x, cells_y)
    sds = jax.ShapeDtypeStruct

    strip = sds((chans, 8, cells_y), BF16)
    to_east, to_west, rows = call(edge_kernel, (strip, strip, strip), [VMEM_SPEC])(block)

    def beside(by):
        return [(i, i + by) for i in range(tiles) if 0 <= i % TILE_ROWS + by < TILE_ROWS]

    from_west = lax.ppermute(to_east, "tile", beside(1))
    from_east = lax.ppermute(to_west, "tile", beside(-1))

    def flat(x):
        return x.reshape(-1, cells_y)

    message, columns = call(
        functools.partial(pack_kernel, chans=chans),
        (sds((chans * 8, cells_y), BF16), sds((10, chans, cells_y), F32)),
        [VMEM_SPEC] * 5,
        [pltpu.VMEM((5, chans * 8, cells_y), F32)],
    )(flat(rows), flat(from_west), flat(from_east), flat(to_west), flat(to_east))

    def across(x, by):
        return lax.ppermute(x, "tile", [(i, (i + by) % tiles) for i in range(tiles)])

    up = across(message, TILE_ROWS)
    down = up if tiles == 2 * TILE_ROWS else across(message, -TILE_ROWS)

    ax = jnp.repeat(courant_x, fields)
    ay = jnp.repeat(courant_y, fields)
    nu = jnp.tile(diffusion, levels)
    coef = jnp.stack(
        [
            1.0 - jnp.abs(ax) - jnp.abs(ay) - 4.0 * nu,
            jnp.maximum(ax, 0.0) + nu,
            nu - jnp.minimum(ax, 0.0),
            jnp.maximum(ay, 0.0) + nu,
            nu - jnp.minimum(ay, 0.0),
        ]
    )

    size = cells_x // 4
    tall = pltpu.VMEM((chans, cells_x + 2 * MARGIN, cells_y), F32)
    height = chans * (EXTRA + size)
    moved = sds((chans * size, cells_y), F32)

    def transport(jobs, *halos):
        ahead = len(halos) == 0
        return call(
            functools.partial(transport_kernel, chans=chans, jobs=jobs, size=size, ahead=ahead),
            (sds((height, cells_y), BF16),) * len(jobs) + (() if ahead else (moved,) * 4),
            [VMEM_SPEC if ahead else ANY_SPEC, pl.BlockSpec(memory_space=pltpu.SMEM)]
            + [VMEM_SPEC] * (2 + len(halos)),
            [pltpu.VMEM((height, cells_y), F32) for _ in jobs]
            + [
                pltpu.VMEM((2, chans * 8, cells_y), F32),
                tall,
                tall,
                tall,
                pltpu.VMEM((2, 2, 2, chans, cells_y), F32),
                pltpu.VMEM((4 * cells_y, 2 * cells_y), BF16),
                pltpu.SemaphoreType.DMA((1,)),
            ],
            flops=5 * 10**9,
        )(block, coef, coef.T, columns, *halos)

    def swap(x):
        return lax.ppermute(x, "group", [(0, 1), (1, 0)])

    (theirs0,) = transport([(1, 0)])
    theirs1, *rest = transport([(1, 1), (0, 0), (0, 1)], up, down)
    mine, kept, others = rest[:2], rest[2:4], rest[4:]
    got = [swap(theirs0), swap(theirs1)]

    own = lax.axis_index("group")
    both = 2 * pad

    def ordered(w):
        return jnp.where(own == 0, w, w[::-1])

    w1 = ordered((w_in * 0.5).reshape(2, chans, 9, hidden)).transpose(3, 2, 0, 1)
    w1 = jnp.pad(w1, ((0, 0), (0, 0), (0, 0), (0, pad - chans))).reshape(hidden, 9 * both)
    w3 = ordered(w_out.T.reshape(2, chans, hidden))
    w3 = jnp.pad(w3, ((0, 0), (0, pad - chans), (0, 0))).reshape(both, hidden)
    w2 = (w_mid * 0.5).T

    back = []
    image = None
    blocks = pltpu.VMEM((9 * both, BLOCK_ROWS * cells_y), BF16)
    whole = sds((chans, cells_x, cells_y), F32)
    for n in range(2):
        images = () if image is None else (image,)
        image, other = call(
            functools.partial(physics_kernel, n, chans=chans),
            (whole, sds((chans * size, cells_y), BF16)),
            [ANY_SPEC] + [VMEM_SPEC] * 4 + [ANY_SPEC, VMEM_SPEC] + [ANY_SPEC] * len(images),
            [
                pltpu.VMEM((3, 2, pad * (EXTRA + size), cells_y), F32),
                pltpu.VMEM((3, size + 2, both, cells_y), BF16),
                pltpu.VMEM((3, size, cells_y), F32),
                pltpu.VMEM((2, size, cells_y), jnp.int32),
                blocks,
                blocks,
                pltpu.VMEM((2, chans * size, cells_y), F32),
                pltpu.VMEM((chans, size, cells_y), F32),
                pltpu.VMEM((height, cells_y), BF16),
                pltpu.SemaphoreType.DMA((4,)),
            ],
            flops=7 * 10**9,
            out_specs=(ANY_SPEC, VMEM_SPEC),
            aliases={7: 0} if images else {},
        )(neighbours, w1, w2, w3, mine[n], got[n], kept[n], *images)
        back.append(swap(other))
    parts = 4 if chans % 4 == 0 else 1
    for n in range(2):
        image = call(
            functools.partial(finish_kernel, n, parts=parts),
            whole,
            [VMEM_SPEC, VMEM_SPEC, ANY_SPEC],
            [pltpu.VMEM((chans, size, cells_y), F32), pltpu.SemaphoreType.DMA((parts,))],
            out_specs=ANY_SPEC,
            aliases={2: 0},
            limit=4,
        )(back[n], others[n], image)
    return image.reshape(levels, fields, single, cells_x, cells_y)


def solution(mesh):
    return jax.shard_map(
        shards,
        mesh=mesh,
        in_specs=(
            P("group", None, "tile", None, None),
            P("group"),
            P("group"),
            P(),
            P(None, "tile", None, None),
            P(),
            P(),
            P(),
        ),
        out_specs=P("group", None, "tile", None, None),
        check_vma=False,
    )
```

```python
import functools

import jax
import jax.numpy as jnp
from jax import lax
from jax.experimental import pallas as pl
from jax.experimental.pallas import tpu as pltpu
from jax.sharding import PartitionSpec as P


TILE_ROWS = 8
DEEP = 3
EXTRA = 8
BLOCK_ROWS = 16
MARGIN = 16
GROUP = 4

F32 = jnp.float32
BF16 = jnp.bfloat16
VMEM_SPEC = pl.BlockSpec(memory_space=pltpu.VMEM)
ANY_SPEC = pl.BlockSpec(memory_space=pl.ANY)


def lanes_of(shape):
    return lax.broadcasted_iota(jnp.int32, shape, len(shape) - 1)


def first_row(q, n, quarter):
    return quarter * (1 + q) if n == 0 else 3 * quarter * q


def edge_kernel(state_ref, east_ref, west_ref, rows_ref):
    chans, cells_x, cells_y = state_ref.shape
    slot = lax.broadcasted_iota(jnp.int32, (16, cells_y), 0)
    lane = lanes_of((16, cells_y))
    wanted = jnp.where(slot < 8, slot + cells_y - DEEP, slot - 8)
    valid = (slot % 8) < DEEP
    pick = jnp.where(valid & (lane == wanted), 1.0, 0.0).astype(BF16)
    for c in range(chans):
        block = state_ref[c].astype(BF16)
        strips = lax.dot_general(
            pick, block, (((1,), (1,)), ((), ())), preferred_element_type=F32
        ).astype(BF16)
        east_ref[c] = strips[0:8]
        west_ref[c] = strips[8:16]
        rows_ref[c] = jnp.concatenate(
            [state_ref[c, 0:DEEP], state_ref[c, cells_x - DEEP : cells_x], state_ref[c, 0:2]], axis=0
        ).astype(BF16)


def pack_kernel(
    rows_ref, west_in, east_in, west_own, east_own, coef_ref, out_ref, column_ref, wide_ref, wide, *, chans
):
    width = rows_ref.shape[1]
    lane = lanes_of((chans, width))
    for n, ref in enumerate((rows_ref, west_in, east_in, west_own, east_own)):
        wide[n] = ref[...].astype(F32)
    sources = [(1, 0), (1, 1), (1, 2), (3, 0), (3, 1), (4, 1), (4, 2), (2, 0), (2, 1), (2, 2)]
    corner = jnp.zeros((chans, width), F32)
    for k, (n, slot) in enumerate(sources):
        line = wide[n, pl.ds(slot, chans, stride=8), :]
        column_ref[k] = line
        at = 2 * DEEP * k
        corner = jnp.where(
            (lane >= at) & (lane < at + 2 * DEEP), pltpu.roll(line, at + DEEP, 1), corner
        )
    for n in range(wide_ref.shape[0]):
        wide_ref[n] = jnp.broadcast_to(coef_ref[:, n : n + 1], (chans, width))
    wide[0, pl.ds(2 * DEEP, chans, stride=8), :] = corner
    out_ref[...] = wide[0].astype(BF16)


def shift_matrix(width):
    k = lax.broadcasted_iota(jnp.int32, (4 * width, 2 * width), 0)
    n = lax.broadcasted_iota(jnp.int32, (4 * width, 2 * width), 1)
    m = k % width
    lower = (n < width) & (n == m + 1)
    upper = (n >= width) & (n - width == m - 1)
    west = (k >= 2 * width) & (k < 3 * width) & (n == 0)
    east = (k >= 3 * width) & (n == 2 * width - 1)
    return jnp.where(((k < 2 * width) & (lower | upper)) | west | east, 1.0, 0.0).astype(BF16)


def transport_kernel(state_ref, coef_ref, column_ref, *rest, chans, jobs, size, ahead):
    count = len(jobs)
    halos, rest = ((), rest) if ahead else (rest[:2], rest[2:])
    packets, rest = rest[:count], rest[count:]
    quarters, rest = ((), rest) if ahead else (rest[:4], rest[4:])
    windows, rest = rest[:count], rest[count:]
    border, raw_s, once_s, last_s, line_s, matrix, sem = rest
    cells_x, width = state_ref.shape[1:]
    own = lax.axis_index("group")
    place = lax.axis_index("tile") % TILE_ROWS
    half_of = (own, 1 - own)
    base_of = [first_row(half_of[whose], n, size) for whose, n in jobs]
    fetch = pltpu.make_async_copy(state_ref, raw_s.at[:, pl.ds(MARGIN, cells_x)], sem.at[0])
    if not ahead:
        fetch.start()
    matrix[...] = shift_matrix(width)
    lane = lanes_of((chans, width))
    first, last = lane == 0, lane == width - 1
    low_lanes = lane < width // 2
    for s, ref in enumerate(halos):
        border[s] = ref[...].astype(F32)
    coefs = [coef_ref[n] for n in range(5)]
    message = border.shape[1] // chans

    if ahead:
        corners = jnp.zeros((chans, width), F32)
    else:
        above, below = [border[s, pl.ds(2 * DEEP, chans, stride=message), :] for s in range(2)]
        corners = jnp.where(lane % (2 * DEEP) < DEEP, above, below)

    def pair(k):
        return column_ref[k], roll(corners, width - (2 * DEEP * k + DEEP))

    def roll(x, by):
        return pltpu.roll(x, by, 1)

    def both_ways(main, aux):
        ml, al = roll(main, 1), roll(aux, 1)
        mu, au = roll(main, width - 1), roll(aux, width - 1)
        lower = jnp.where(first, al, ml), jnp.where(first, ml, al)
        upper = jnp.where(last, au, mu), jnp.where(last, mu, au)
        return lower, upper

    def column(west, mid, east, keep):
        c0, cxl, cxu, cyl, cyu = coefs
        lower, upper = both_ways(*mid)
        return tuple(
            (c0 * mid[n] + cxl * lower[n] + cxu * upper[n] + cyl * west[n] + cyu * east[n]) * keep
            for n in range(2)
        )

    keeps = (
        jnp.where(place == 0, 0.0, 1.0),
        jnp.where(place == TILE_ROWS - 1, 0.0, 1.0),
    )
    edges = []
    for side in range(2):
        raw = [pair(5 * side + k) for k in range(5)]
        keep = keeps[side]
        inside = 3 if side == 0 else 1
        once = [
            column(raw[k - 1], raw[k], raw[k + 1], 1.0 if k == inside else keep)
            for k in (1, 2, 3)
        ]
        main, aux = column(once[0], once[1], once[2], keep)
        for level, edge in enumerate((raw[2], once[1])):
            for n in range(2):
                line_s[level, side, n] = edge[n]
        edges.append((main, aux))
    for window, base in zip(windows, base_of):
        at = base - 1
        sides = []
        for side, first_lane in enumerate((0, width // 2)):
            main, aux = edges[side]
            by = lax.rem(first_lane - at + width, width)
            row_of = lane - first_lane + at
            off = (row_of < 0) | (row_of >= cells_x)
            sides.append(jnp.where(off, roll(aux, by), roll(main, by)))
        window[pl.ds(2, chans, stride=EXTRA + size), :] = jnp.where(low_lanes, *sides)

    rows = size + 16 if ahead else cells_x + 16
    origin = base_of[0] - 8 if ahead else -8
    top = pl.multiple_of(origin + MARGIN, 8) if ahead else 8
    at = lax.broadcasted_iota(jnp.int32, (rows, width), 0) + origin
    diagonal = lax.rem(at + width, width) == lanes_of((rows, width))
    within = (at >= 0) & (at < cells_x)
    if not ahead:
        fetch.wait()
    group = next(n for n in (10 if ahead else GROUP, 2, 1) if chans % n == 0)

    def sweep(level, src, dst, base):
        near_top = pl.multiple_of(origin, 8) if ahead and level == 0 else top
        parts = []
        for g in range(group):
            c = base + g
            q = src[c, pl.ds(near_top, rows), :]
            hi = q.astype(BF16)
            lo = (q - hi.astype(F32)).astype(BF16)
            sides = []
            for side in range(2):
                main = line_s[level, side, 0, pl.ds(c, 1), :]
                aux = line_s[level, side, 1, pl.ds(c, 1), :]
                values = jnp.where(within, main, aux)
                sides.append(jnp.where(diagonal, values, 0.0).astype(BF16))
            parts.append(jnp.concatenate([hi, lo] + sides, axis=1))
        near = lax.dot_general(
            jnp.concatenate(parts, axis=0),
            matrix[...],
            (((1,), (0,)), ((), ())),
            preferred_element_type=F32,
        )
        for g in range(group):
            c = base + g
            lower, upper = near[g * rows : (g + 1) * rows, :width], near[g * rows : (g + 1) * rows, width:]
            c0, cxl, cxu, cyl, cyu = [coef_ref[n, pl.ds(c, 1), :] for n in range(5)]
            dst[c, pl.ds(top, rows), :] = (
                c0 * src[c, pl.ds(near_top, rows), :]
                + cxl * src[c, pl.ds(near_top - 1, rows), :]
                + cxu * src[c, pl.ds(near_top + 1, rows), :]
                + cyl * lower
                + cyu * upper
            )

    def finish(base):
        for g in range(group):
            c = base + g
            for window, row in zip(windows, base_of):
                at = MARGIN + row
                to = c * (EXTRA + size)
                window[pl.ds(to, 1), :] = last_s[c, pl.ds(at - 1, 1), :]
                window[pl.ds(to + 1, 1), :] = last_s[c, pl.ds(at + size, 1), :]
                window[pl.ds(to + EXTRA, size), :] = last_s[c, pl.ds(pl.multiple_of(at, 8), size), :]
            for k, quarter in enumerate(quarters):
                at = pl.multiple_of(MARGIN + first_row(half_of[k // 2], k % 2, size), 8)
                quarter[pl.ds(c * size, size), :] = last_s[c, pl.ds(at, size), :]

    for c in range(0 if ahead else chans):
        raw_s[c, pl.ds(MARGIN - DEEP, DEEP), :] = border[0, pl.ds(c * message + DEEP, DEEP), :]
        raw_s[c, pl.ds(MARGIN + cells_x, DEEP), :] = border[1, pl.ds(c * message, DEEP), :]
    for base in range(0, chans + group, group):
        if base < chans:
            sweep(0, state_ref if ahead else raw_s, once_s, base)
        if base:
            sweep(1, once_s, last_s, base - group)
            finish(base - group)
    for packet, window in zip(packets, windows):
        packet[...] = window[...].astype(BF16)


def physics_kernel(
    chunk, table_ref, w1_ref, w2_ref, w3_ref, mine_ref, got_ref, kept_ref, *rest, chans
):
    own_ref, other_ref, wide, packed, mask, table, even, odd, terms, sem = rest[-10:]
    size, width = table.shape[1:]
    height = EXTRA + size
    pad = -(-chans // 8) * 8
    both = 2 * pad
    top = first_row(lax.axis_index("group"), chunk, size)
    copies = [
        pltpu.make_async_copy(table_ref.at[k, 0, pl.ds(top, size)], table.at[n], sem.at[n])
        for n, k in enumerate((5, 7))
    ]
    for copy in copies:
        copy.start()

    k = lax.broadcasted_iota(jnp.int32, (2 * width, 2 * width), 0)
    n = lax.broadcasted_iota(jnp.int32, (2 * width, 2 * width), 1)
    inner = (k < width) & (((n < width) & (n == k + 1)) | ((n >= width) & (n - width == k - 1)))
    west = (k >= width) & (k < width + width // 2) & (n == 0)
    east = (k >= width + width // 2) & (n == 2 * width - 1)
    matrix = jnp.where(inner | west | east, 1.0, 0.0).astype(BF16)
    slot = lax.broadcasted_iota(jnp.int32, (height, width), 0)
    line = jnp.where(
        slot >= EXTRA, slot - EXTRA + 1, jnp.where(slot == 0, 0, jnp.where(slot == 1, size + 1, -1))
    )
    diagonal = lanes_of((height, width)) % (width // 2) == line
    for s, ref in enumerate((mine_ref, got_ref)):
        cells = ref[...]
        flat = cells.astype(F32)
        wide[1, s, pl.ds(0, chans * height)] = flat
        edges = [
            jnp.where(diagonal, flat[c * height + 2 : c * height + 3], 0.0) for c in range(chans)
        ]
        edges = jnp.concatenate(edges, axis=0).astype(BF16)
        near = lax.dot_general(
            jnp.concatenate([cells, edges], axis=1),
            matrix,
            (((1,), (0,)), ((), ())),
            preferred_element_type=F32,
        )
        wide[0, s, pl.ds(0, chans * height)] = near[:, :width]
        wide[2, s, pl.ds(0, chans * height)] = near[:, width:]
        if pad > chans:
            for b in range(3):
                wide[b, s, pl.ds(chans * height, (pad - chans) * height)] = jnp.zeros(
                    ((pad - chans) * height, width), F32
                )

    for l in range(-1, size + 1):
        at = 0 if l < 0 else 1 if l == size else EXTRA + l
        for b in range(3):
            pair = [wide[b, s, pl.ds(at, pad, stride=height), :] for s in range(2)]
            packed[b, l + 1] = jnp.concatenate(pair, axis=0).astype(BF16)

    for copy in copies:
        copy.wait()
    rows_i = lax.broadcasted_iota(jnp.int32, (size, width), 0) + top
    centre = (rows_i + 1) * (width + 2) + lanes_of((size, width)) + 1
    along_y = table[0] - centre
    along_x = table[1] - centre
    turned = jnp.abs(along_x) == 1
    mask[0] = jnp.where(jnp.where(turned, along_y, along_x) < 0, 1.0, 0.0)
    mask[1] = jnp.where(jnp.where(turned, along_x, along_y) < 0, 1.0, 0.0)
    mask[2] = jnp.where(turned, 1.0, 0.0)

    def choose(m, a, b):
        return jnp.where(m, a, b), jnp.where(m, b, a)

    rows_step = even.shape[1] // width

    def stack(n, dst):
        for u in range(rows_step):
            l = n * rows_step + u
            m = []
            for k in range(3):
                line = jnp.broadcast_to(mask[k, pl.ds(l, 1), :], (16, width)).astype(BF16)
                m.append(jnp.concatenate([line] * (both // 16), axis=0) > 0.5)
            x = [[packed[bb, l + aa] for bb in range(3)] for aa in range(3)]
            for bb in range(3):
                x[0][bb], x[2][bb] = choose(m[0], x[2][bb], x[0][bb])
            for aa in range(3):
                x[aa][0], x[aa][2] = choose(m[1], x[aa][2], x[aa][0])
            for aa, bb in ((0, 1), (0, 2), (1, 2)):
                x[aa][bb], x[bb][aa] = choose(m[2], x[bb][aa], x[aa][bb])
            for k in range(9):
                dst[pl.ds(k * both, both), pl.ds(u * width, width)] = x[k // 3][k % 3]

    dot = functools.partial(
        lax.dot_general,
        dimension_numbers=(((1,), (0,)), ((), ())),
        preferred_element_type=F32,
    )

    def silu(v):
        return (v * jnp.tanh(v) + v).astype(BF16)

    def network(n, src):
        first = silu(dot(w1_ref[...], src[...]))
        second = silu(dot(w2_ref[...], first))
        tend = dot(w3_ref[...], second)
        for u in range(rows_step):
            l = n * rows_step + u
            cols = slice(u * width, (u + 1) * width)
            terms[0, pl.ds(l, chans, stride=size), :] = tend[0:chans, cols]
            terms[1, pl.ds(l, chans, stride=size), :] = tend[pad : pad + chans, cols]

    steps = size // rows_step
    slots = (even, odd)
    stack(0, even)
    for n in range(steps):
        if n + 1 < steps:
            stack(n + 1, slots[(n + 1) % 2])
        network(n, slots[n % 2])
    other_ref[...] = terms[1].astype(BF16)
    own_ref[...] = kept_ref[...] + terms[0]


def finish_kernel(chunk, back_ref, moved_ref, *rest, parts):
    image_ref, patch, sem = rest[-3:]
    chans, size, width = patch.shape
    own = lax.axis_index("group")
    put = []
    if chunk == 0:
        for n in range(2):
            rows = pl.ds(first_row(own, n, size), size)
            put.append(pltpu.make_async_copy(rest[n], image_ref.at[:, rows], sem.at[parts + n]))
            put[-1].start()
    rows = pl.ds(first_row(1 - own, chunk, size), size)
    some = chans // parts
    for n in range(parts):
        c, r = pl.ds(n * some, some), pl.ds(n * some * size, some * size)
        patch[c] = (moved_ref[r] + back_ref[r].astype(F32)).reshape(some, size, width)
        put.append(pltpu.make_async_copy(patch.at[c], image_ref.at[c, rows], sem.at[n]))
        put[-1].start()
    for copy in put:
        copy.wait()


def call(kernel, outs, ins, scratch=(), flops=10**9, out_specs=None, aliases=None, limit=24):
    return pl.pallas_call(
        kernel,
        out_shape=jax.tree.map(lambda x: jax.ShapeDtypeStruct(x.shape, x.dtype), outs),
        in_specs=ins,
        out_specs=jax.tree.map(lambda _: VMEM_SPEC, outs) if out_specs is None else out_specs,
        input_output_aliases=aliases or {},
        scratch_shapes=list(scratch),
        compiler_params=pltpu.CompilerParams(vmem_limit_bytes=limit << 20),
        cost_estimate=pl.CostEstimate(flops=flops, bytes_accessed=10**6, transcendentals=0),
    )


def shards(state, courant_x, courant_y, diffusion, neighbours, w_in, w_mid, w_out):
    levels, fields, single, cells_x, cells_y = state.shape
    chans = levels * fields
    hidden = w_mid.shape[0]
    tiles = lax.axis_size("tile")
    pad = -(-chans // 8) * 8
    block = state.reshape(chans, cells_x, cells_y)
    sds = jax.ShapeDtypeStruct

    strip = sds((chans, 8, cells_y), BF16)
    to_east, to_west, rows = call(edge_kernel, (strip, strip, strip), [VMEM_SPEC])(block)

    def beside(by):
        return [(i, i + by) for i in range(tiles) if 0 <= i % TILE_ROWS + by < TILE_ROWS]

    from_west = lax.ppermute(to_east, "tile", beside(1))
    from_east = lax.ppermute(to_west, "tile", beside(-1))

    def flat(x):
        return x.reshape(-1, cells_y)

    ax = jnp.repeat(courant_x, fields)
    ay = jnp.repeat(courant_y, fields)
    nu = jnp.tile(diffusion, levels)
    coef = jnp.stack(
        [
            1.0 - jnp.abs(ax) - jnp.abs(ay) - 4.0 * nu,
            jnp.maximum(ax, 0.0) + nu,
            nu - jnp.minimum(ax, 0.0),
            jnp.maximum(ay, 0.0) + nu,
            nu - jnp.minimum(ay, 0.0),
        ]
    )

    message, columns, wide_coef = call(
        functools.partial(pack_kernel, chans=chans),
        (
            sds((chans * 8, cells_y), BF16),
            sds((10, chans, cells_y), F32),
            sds((5, chans, cells_y), F32),
        ),
        [VMEM_SPEC] * 6,
        [pltpu.VMEM((5, chans * 8, cells_y), F32)],
    )(flat(rows), flat(from_west), flat(from_east), flat(to_west), flat(to_east), coef.T)

    def across(x, by):
        return lax.ppermute(x, "tile", [(i, (i + by) % tiles) for i in range(tiles)])

    up = across(message, TILE_ROWS)
    down = up if tiles == 2 * TILE_ROWS else across(message, -TILE_ROWS)

    size = cells_x // 4
    tall = pltpu.VMEM((chans, cells_x + 2 * MARGIN, cells_y), F32)
    height = chans * (EXTRA + size)
    moved = sds((chans * size, cells_y), F32)

    def transport(jobs, *halos):
        ahead = len(halos) == 0
        return call(
            functools.partial(transport_kernel, chans=chans, jobs=jobs, size=size, ahead=ahead),
            (sds((height, cells_y), BF16),) * len(jobs) + (() if ahead else (moved,) * 4),
            [VMEM_SPEC if ahead else ANY_SPEC] + [VMEM_SPEC] * (2 + len(halos)),
            [pltpu.VMEM((height, cells_y), F32) for _ in jobs]
            + [
                pltpu.VMEM((2, chans * 8, cells_y), F32),
                tall,
                tall,
                tall,
                pltpu.VMEM((2, 2, 2, chans, cells_y), F32),
                pltpu.VMEM((4 * cells_y, 2 * cells_y), BF16),
                pltpu.SemaphoreType.DMA((1,)),
            ],
            flops=5 * 10**9,
        )(block, wide_coef, columns, *halos)

    def swap(x):
        return lax.ppermute(x, "group", [(0, 1), (1, 0)])

    (theirs0,) = transport([(1, 0)])
    theirs1, *rest = transport([(1, 1), (0, 0), (0, 1)], up, down)
    mine, kept, others = rest[:2], rest[2:4], rest[4:]
    got = [swap(theirs0), swap(theirs1)]

    own = lax.axis_index("group")
    both = 2 * pad

    def ordered(w):
        return jnp.where(own == 0, w, w[::-1])

    w1 = ordered((w_in * 0.5).reshape(2, chans, 9, hidden)).transpose(3, 2, 0, 1)
    w1 = jnp.pad(w1, ((0, 0), (0, 0), (0, 0), (0, pad - chans))).reshape(hidden, 9 * both)
    w3 = ordered(w_out.T.reshape(2, chans, hidden))
    w3 = jnp.pad(w3, ((0, 0), (0, pad - chans), (0, 0))).reshape(both, hidden)
    w2 = (w_mid * 0.5).T

    back, owned = [], []
    blocks = pltpu.VMEM((9 * both, BLOCK_ROWS * cells_y), BF16)
    for n in range(2):
        mixed, other = call(
            functools.partial(physics_kernel, n, chans=chans),
            (moved, sds((chans * size, cells_y), BF16)),
            [ANY_SPEC] + [VMEM_SPEC] * 6 + [ANY_SPEC] * n,
            [
                pltpu.VMEM((3, 2, pad * (EXTRA + size), cells_y), F32),
                pltpu.VMEM((3, size + 2, both, cells_y), BF16),
                pltpu.VMEM((3, size, cells_y), F32),
                pltpu.VMEM((2, size, cells_y), jnp.int32),
                blocks,
                blocks,
                pltpu.VMEM((2, chans * size, cells_y), F32),
                pltpu.SemaphoreType.DMA((2,)),
            ],
            flops=7 * 10**9,
        )(neighbours, w1, w2, w3, mine[n], got[n], kept[n], *owned)
        owned.append(mixed)
        back.append(swap(other))
    owned = [x.reshape(chans, size, cells_y) for x in owned]
    parts = 4 if chans % 4 == 0 else 1
    whole = sds((chans, cells_x, cells_y), F32)
    image = call(
        functools.partial(finish_kernel, 0, parts=parts),
        whole,
        [VMEM_SPEC] * 4,
        [pltpu.VMEM((chans, size, cells_y), F32), pltpu.SemaphoreType.DMA((parts + 2,))],
        out_specs=ANY_SPEC,
        limit=4,
    )(back[0], others[0], *owned)
    image = call(
        functools.partial(finish_kernel, 1, parts=parts),
        whole,
        [VMEM_SPEC, VMEM_SPEC, ANY_SPEC],
        [pltpu.VMEM((chans, size, cells_y), F32), pltpu.SemaphoreType.DMA((parts,))],
        out_specs=ANY_SPEC,
        aliases={2: 0},
        limit=4,
    )(back[1], others[1], image)
    return image.reshape(levels, fields, single, cells_x, cells_y)


def solution(mesh):
    return jax.shard_map(
        shards,
        mesh=mesh,
        in_specs=(
            P("group", None, "tile", None, None),
            P("group"),
            P("group"),
            P(),
            P(None, "tile", None, None),
            P(),
            P(),
            P(),
        ),
        out_specs=P("group", None, "tile", None, None),
        check_vma=False,
    )
```

```python
import functools

import jax
import jax.numpy as jnp
from jax import lax
from jax.experimental import pallas as pl
from jax.experimental.pallas import tpu as pltpu
from jax.sharding import PartitionSpec as P


TILE_ROWS = 8
DEEP = 3
EXTRA = 8
BLOCK_ROWS = 16
MARGIN = 16
GROUP = 4

F32 = jnp.float32
BF16 = jnp.bfloat16
VMEM_SPEC = pl.BlockSpec(memory_space=pltpu.VMEM)
ANY_SPEC = pl.BlockSpec(memory_space=pl.ANY)


def lanes_of(shape):
    return lax.broadcasted_iota(jnp.int32, shape, len(shape) - 1)


def first_row(q, n, quarter):
    return quarter * (1 + q) if n == 0 else 3 * quarter * q


def edge_kernel(state_ref, first_ref, second_ref, rows_ref):
    chans, cells_x, cells_y = state_ref.shape
    even = lax.axis_index("tile") % 2 == 0
    slot = lax.broadcasted_iota(jnp.int32, (16, cells_y), 0)
    lane = lanes_of((16, cells_y))
    wanted = jnp.where(slot < 8, slot + cells_y - DEEP, slot - 8)
    valid = (slot % 8) < DEEP
    pick = jnp.where(valid & (lane == wanted), 1.0, 0.0).astype(BF16)
    for c in range(chans):
        block = state_ref[c].astype(BF16)
        strips = lax.dot_general(
            pick, block, (((1,), (1,)), ((), ())), preferred_element_type=F32
        )
        east, west = strips[0:8], strips[8:16]
        first_ref[c] = jnp.where(even, east, west).astype(BF16)
        second_ref[c] = jnp.where(even, west, east).astype(BF16)
        rows_ref[c] = jnp.concatenate(
            [state_ref[c, 0:DEEP], state_ref[c, cells_x - DEEP : cells_x], state_ref[c, 0:2]], axis=0
        ).astype(BF16)


def pack_kernel(
    rows_ref, first_in, second_in, first_own, second_own, coef_ref, out_ref, column_ref, wide_ref, wide, *, chans
):
    width = rows_ref.shape[1]
    lane = lanes_of((chans, width))
    even = lax.axis_index("tile") % 2 == 0
    wide[0] = rows_ref[...].astype(F32)
    got = first_in[...].astype(F32), second_in[...].astype(F32)
    sent = first_own[...].astype(F32), second_own[...].astype(F32)
    wide[1] = jnp.where(even, got[1], got[0])
    wide[2] = jnp.where(even, got[0], got[1])
    wide[3] = jnp.where(even, sent[1], sent[0])
    wide[4] = jnp.where(even, sent[0], sent[1])
    sources = [(1, 0), (1, 1), (1, 2), (3, 0), (3, 1), (4, 1), (4, 2), (2, 0), (2, 1), (2, 2)]
    corner = jnp.zeros((chans, width), F32)
    for k, (n, slot) in enumerate(sources):
        line = wide[n, pl.ds(slot, chans, stride=8), :]
        column_ref[k] = line
        at = 2 * DEEP * k
        corner = jnp.where(
            (lane >= at) & (lane < at + 2 * DEEP), pltpu.roll(line, at + DEEP, 1), corner
        )
    for n in range(wide_ref.shape[0]):
        wide_ref[n] = jnp.broadcast_to(coef_ref[:, n : n + 1], (chans, width))
    wide[0, pl.ds(2 * DEEP, chans, stride=8), :] = corner
    out_ref[...] = wide[0].astype(BF16)


def shift_matrix(width):
    k = lax.broadcasted_iota(jnp.int32, (4 * width, 2 * width), 0)
    n = lax.broadcasted_iota(jnp.int32, (4 * width, 2 * width), 1)
    m = k % width
    lower = (n < width) & (n == m + 1)
    upper = (n >= width) & (n - width == m - 1)
    west = (k >= 2 * width) & (k < 3 * width) & (n == 0)
    east = (k >= 3 * width) & (n == 2 * width - 1)
    return jnp.where(((k < 2 * width) & (lower | upper)) | west | east, 1.0, 0.0).astype(BF16)


def transport_kernel(state_ref, coef_ref, column_ref, *rest, chans, jobs, size, ahead):
    count = len(jobs)
    halos, rest = ((), rest) if ahead else (rest[:2], rest[2:])
    packets, rest = rest[:count], rest[count:]
    quarters, rest = ((), rest) if ahead else (rest[:4], rest[4:])
    windows, rest = rest[:count], rest[count:]
    border, raw_s, once_s, last_s, line_s, matrix, sem = rest
    cells_x, width = state_ref.shape[1:]
    own = lax.axis_index("group")
    place = lax.axis_index("tile") % TILE_ROWS
    half_of = (own, 1 - own)
    base_of = [first_row(half_of[whose], n, size) for whose, n in jobs]
    fetch = pltpu.make_async_copy(state_ref, raw_s.at[:, pl.ds(MARGIN, cells_x)], sem.at[0])
    if not ahead:
        fetch.start()
    matrix[...] = shift_matrix(width)
    lane = lanes_of((chans, width))
    first, last = lane == 0, lane == width - 1
    low_lanes = lane < width // 2
    for s, ref in enumerate(halos):
        border[s] = ref[...].astype(F32)
    coefs = [coef_ref[n] for n in range(5)]
    message = border.shape[1] // chans

    if ahead:
        corners = jnp.zeros((chans, width), F32)
    else:
        above, below = [border[s, pl.ds(2 * DEEP, chans, stride=message), :] for s in range(2)]
        corners = jnp.where(lane % (2 * DEEP) < DEEP, above, below)

    def pair(k):
        return column_ref[k], roll(corners, width - (2 * DEEP * k + DEEP))

    def roll(x, by):
        return pltpu.roll(x, by, 1)

    def both_ways(main, aux):
        ml, al = roll(main, 1), roll(aux, 1)
        mu, au = roll(main, width - 1), roll(aux, width - 1)
        lower = jnp.where(first, al, ml), jnp.where(first, ml, al)
        upper = jnp.where(last, au, mu), jnp.where(last, mu, au)
        return lower, upper

    def column(west, mid, east, keep):
        c0, cxl, cxu, cyl, cyu = coefs
        lower, upper = both_ways(*mid)
        return tuple(
            (c0 * mid[n] + cxl * lower[n] + cxu * upper[n] + cyl * west[n] + cyu * east[n]) * keep
            for n in range(2)
        )

    keeps = (
        jnp.where(place == 0, 0.0, 1.0),
        jnp.where(place == TILE_ROWS - 1, 0.0, 1.0),
    )
    edges = []
    for side in range(2):
        raw = [pair(5 * side + k) for k in range(5)]
        keep = keeps[side]
        inside = 3 if side == 0 else 1
        once = [
            column(raw[k - 1], raw[k], raw[k + 1], 1.0 if k == inside else keep)
            for k in (1, 2, 3)
        ]
        main, aux = column(once[0], once[1], once[2], keep)
        for level, edge in enumerate((raw[2], once[1])):
            for n in range(2):
                line_s[level, side, n] = edge[n]
        edges.append((main, aux))
    for window, base in zip(windows, base_of):
        at = base - 1
        sides = []
        for side, first_lane in enumerate((0, width // 2)):
            main, aux = edges[side]
            by = lax.rem(first_lane - at + width, width)
            row_of = lane - first_lane + at
            off = (row_of < 0) | (row_of >= cells_x)
            sides.append(jnp.where(off, roll(aux, by), roll(main, by)))
        window[pl.ds(2, chans, stride=EXTRA + size), :] = jnp.where(low_lanes, *sides)

    rows = size + 16 if ahead else cells_x + 16
    origin = base_of[0] - 8 if ahead else -8
    top = pl.multiple_of(origin + MARGIN, 8) if ahead else 8
    at = lax.broadcasted_iota(jnp.int32, (rows, width), 0) + origin
    diagonal = lax.rem(at + width, width) == lanes_of((rows, width))
    within = (at >= 0) & (at < cells_x)
    if not ahead:
        fetch.wait()
    group = next(n for n in (10 if ahead else GROUP, 2, 1) if chans % n == 0)

    def sweep(level, src, dst, base):
        near_top = pl.multiple_of(origin, 8) if ahead and level == 0 else top
        parts = []
        for g in range(group):
            c = base + g
            q = src[c, pl.ds(near_top, rows), :]
            hi = q.astype(BF16)
            lo = (q - hi.astype(F32)).astype(BF16)
            sides = []
            for side in range(2):
                main = line_s[level, side, 0, pl.ds(c, 1), :]
                aux = line_s[level, side, 1, pl.ds(c, 1), :]
                values = jnp.where(within, main, aux)
                sides.append(jnp.where(diagonal, values, 0.0).astype(BF16))
            parts.append(jnp.concatenate([hi, lo] + sides, axis=1))
        near = lax.dot_general(
            jnp.concatenate(parts, axis=0),
            matrix[...],
            (((1,), (0,)), ((), ())),
            preferred_element_type=F32,
        )
        for g in range(group):
            c = base + g
            lower, upper = near[g * rows : (g + 1) * rows, :width], near[g * rows : (g + 1) * rows, width:]
            c0, cxl, cxu, cyl, cyu = [coef_ref[n, pl.ds(c, 1), :] for n in range(5)]
            dst[c, pl.ds(top, rows), :] = (
                c0 * src[c, pl.ds(near_top, rows), :]
                + cxl * src[c, pl.ds(near_top - 1, rows), :]
                + cxu * src[c, pl.ds(near_top + 1, rows), :]
                + cyl * lower
                + cyu * upper
            )

    def finish(base):
        for g in range(group):
            c = base + g
            for window, row in zip(windows, base_of):
                at = MARGIN + row
                to = c * (EXTRA + size)
                window[pl.ds(to, 1), :] = last_s[c, pl.ds(at - 1, 1), :]
                window[pl.ds(to + 1, 1), :] = last_s[c, pl.ds(at + size, 1), :]
                window[pl.ds(to + EXTRA, size), :] = last_s[c, pl.ds(pl.multiple_of(at, 8), size), :]
            for k, quarter in enumerate(quarters):
                at = pl.multiple_of(MARGIN + first_row(half_of[k // 2], k % 2, size), 8)
                quarter[pl.ds(c * size, size), :] = last_s[c, pl.ds(at, size), :]

    for c in range(0 if ahead else chans):
        raw_s[c, pl.ds(MARGIN - DEEP, DEEP), :] = border[0, pl.ds(c * message + DEEP, DEEP), :]
        raw_s[c, pl.ds(MARGIN + cells_x, DEEP), :] = border[1, pl.ds(c * message, DEEP), :]
    for base in range(0, chans + group, group):
        if base < chans:
            sweep(0, state_ref if ahead else raw_s, once_s, base)
        if base:
            sweep(1, once_s, last_s, base - group)
            finish(base - group)
    for packet, window in zip(packets, windows):
        packet[...] = window[...].astype(BF16)


def physics_kernel(
    chunk, table_ref, w1_ref, w2_ref, w3_ref, mine_ref, got_ref, kept_ref, *rest, chans
):
    own_ref, other_ref, wide, packed, mask, table, even, odd, terms, sem = rest[-10:]
    size, width = table.shape[1:]
    height = EXTRA + size
    pad = -(-chans // 8) * 8
    both = 2 * pad
    top = first_row(lax.axis_index("group"), chunk, size)
    copies = [
        pltpu.make_async_copy(table_ref.at[k, 0, pl.ds(top, size)], table.at[n], sem.at[n])
        for n, k in enumerate((5, 7))
    ]
    for copy in copies:
        copy.start()

    k = lax.broadcasted_iota(jnp.int32, (2 * width, 2 * width), 0)
    n = lax.broadcasted_iota(jnp.int32, (2 * width, 2 * width), 1)
    inner = (k < width) & (((n < width) & (n == k + 1)) | ((n >= width) & (n - width == k - 1)))
    west = (k >= width) & (k < width + width // 2) & (n == 0)
    east = (k >= width + width // 2) & (n == 2 * width - 1)
    matrix = jnp.where(inner | west | east, 1.0, 0.0).astype(BF16)
    slot = lax.broadcasted_iota(jnp.int32, (height, width), 0)
    line = jnp.where(
        slot >= EXTRA, slot - EXTRA + 1, jnp.where(slot == 0, 0, jnp.where(slot == 1, size + 1, -1))
    )
    diagonal = lanes_of((height, width)) % (width // 2) == line
    for s, ref in enumerate((mine_ref, got_ref)):
        cells = ref[...]
        flat = cells.astype(F32)
        wide[1, s, pl.ds(0, chans * height)] = flat
        edges = [
            jnp.where(diagonal, flat[c * height + 2 : c * height + 3], 0.0) for c in range(chans)
        ]
        edges = jnp.concatenate(edges, axis=0).astype(BF16)
        near = lax.dot_general(
            jnp.concatenate([cells, edges], axis=1),
            matrix,
            (((1,), (0,)), ((), ())),
            preferred_element_type=F32,
        )
        wide[0, s, pl.ds(0, chans * height)] = near[:, :width]
        wide[2, s, pl.ds(0, chans * height)] = near[:, width:]
        if pad > chans:
            for b in range(3):
                wide[b, s, pl.ds(chans * height, (pad - chans) * height)] = jnp.zeros(
                    ((pad - chans) * height, width), F32
                )

    for l in range(-1, size + 1):
        at = 0 if l < 0 else 1 if l == size else EXTRA + l
        for b in range(3):
            pair = [wide[b, s, pl.ds(at, pad, stride=height), :] for s in range(2)]
            packed[b, l + 1] = jnp.concatenate(pair, axis=0).astype(BF16)

    for copy in copies:
        copy.wait()
    rows_i = lax.broadcasted_iota(jnp.int32, (size, width), 0) + top
    centre = (rows_i + 1) * (width + 2) + lanes_of((size, width)) + 1
    along_y = table[0] - centre
    along_x = table[1] - centre
    turned = jnp.abs(along_x) == 1
    mask[0] = jnp.where(jnp.where(turned, along_y, along_x) < 0, 1.0, 0.0)
    mask[1] = jnp.where(jnp.where(turned, along_x, along_y) < 0, 1.0, 0.0)
    mask[2] = jnp.where(turned, 1.0, 0.0)

    def choose(m, a, b):
        return jnp.where(m, a, b), jnp.where(m, b, a)

    rows_step = even.shape[1] // width

    def stack(n, dst):
        for u in range(rows_step):
            l = n * rows_step + u
            m = []
            for k in range(3):
                line = jnp.broadcast_to(mask[k, pl.ds(l, 1), :], (16, width)).astype(BF16)
                m.append(jnp.concatenate([line] * (both // 16), axis=0) > 0.5)
            x = [[packed[bb, l + aa] for bb in range(3)] for aa in range(3)]
            for bb in range(3):
                x[0][bb], x[2][bb] = choose(m[0], x[2][bb], x[0][bb])
            for aa in range(3):
                x[aa][0], x[aa][2] = choose(m[1], x[aa][2], x[aa][0])
            for aa, bb in ((0, 1), (0, 2), (1, 2)):
                x[aa][bb], x[bb][aa] = choose(m[2], x[bb][aa], x[aa][bb])
            for k in range(9):
                dst[pl.ds(k * both, both), pl.ds(u * width, width)] = x[k // 3][k % 3]

    dot = functools.partial(
        lax.dot_general,
        dimension_numbers=(((1,), (0,)), ((), ())),
        preferred_element_type=F32,
    )

    def silu(v):
        return (v * jnp.tanh(v) + v).astype(BF16)

    def network(n, src):
        first = silu(dot(w1_ref[...], src[...]))
        second = silu(dot(w2_ref[...], first))
        tend = dot(w3_ref[...], second)
        for u in range(rows_step):
            l = n * rows_step + u
            cols = slice(u * width, (u + 1) * width)
            terms[0, pl.ds(l, chans, stride=size), :] = tend[0:chans, cols]
            terms[1, pl.ds(l, chans, stride=size), :] = tend[pad : pad + chans, cols]

    steps = size // rows_step
    slots = (even, odd)
    stack(0, even)
    for n in range(steps):
        if n + 1 < steps:
            stack(n + 1, slots[(n + 1) % 2])
        network(n, slots[n % 2])
    other_ref[...] = terms[1].astype(BF16)
    own_ref[...] = kept_ref[...] + terms[0]


def finish_kernel(chunk, back_ref, moved_ref, *rest, parts):
    image_ref, patch, sem = rest[-3:]
    chans, size, width = patch.shape
    own = lax.axis_index("group")
    put = []
    if chunk == 0:
        for n in range(2):
            rows = pl.ds(first_row(own, n, size), size)
            put.append(pltpu.make_async_copy(rest[n], image_ref.at[:, rows], sem.at[parts + n]))
            put[-1].start()
    rows = pl.ds(first_row(1 - own, chunk, size), size)
    some = chans // parts
    for n in range(parts):
        c, r = pl.ds(n * some, some), pl.ds(n * some * size, some * size)
        patch[c] = (moved_ref[r] + back_ref[r].astype(F32)).reshape(some, size, width)
        put.append(pltpu.make_async_copy(patch.at[c], image_ref.at[c, rows], sem.at[n]))
        put[-1].start()
    for copy in put:
        copy.wait()


def call(kernel, outs, ins, scratch=(), flops=10**9, out_specs=None, aliases=None, limit=24):
    return pl.pallas_call(
        kernel,
        out_shape=jax.tree.map(lambda x: jax.ShapeDtypeStruct(x.shape, x.dtype), outs),
        in_specs=ins,
        out_specs=jax.tree.map(lambda _: VMEM_SPEC, outs) if out_specs is None else out_specs,
        input_output_aliases=aliases or {},
        scratch_shapes=list(scratch),
        compiler_params=pltpu.CompilerParams(vmem_limit_bytes=limit << 20),
        cost_estimate=pl.CostEstimate(flops=flops, bytes_accessed=10**6, transcendentals=0),
    )


def shards(state, courant_x, courant_y, diffusion, neighbours, w_in, w_mid, w_out):
    levels, fields, single, cells_x, cells_y = state.shape
    chans = levels * fields
    hidden = w_mid.shape[0]
    tiles = lax.axis_size("tile")
    pad = -(-chans // 8) * 8
    block = state.reshape(chans, cells_x, cells_y)
    sds = jax.ShapeDtypeStruct

    strip = sds((chans, 8, cells_y), BF16)
    first, second, rows = call(edge_kernel, (strip, strip, strip), [VMEM_SPEC])(block)

    def beside(odd):
        pairs = [(i, i + 1) for i in range(odd, tiles - 1, 2) if i % TILE_ROWS != TILE_ROWS - 1]
        return pairs + [(b, a) for a, b in pairs]

    first_in = lax.ppermute(first, "tile", beside(0))
    second_in = lax.ppermute(second, "tile", beside(1))

    def flat(x):
        return x.reshape(-1, cells_y)

    ax = jnp.repeat(courant_x, fields)
    ay = jnp.repeat(courant_y, fields)
    nu = jnp.tile(diffusion, levels)
    coef = jnp.stack(
        [
            1.0 - jnp.abs(ax) - jnp.abs(ay) - 4.0 * nu,
            jnp.maximum(ax, 0.0) + nu,
            nu - jnp.minimum(ax, 0.0),
            jnp.maximum(ay, 0.0) + nu,
            nu - jnp.minimum(ay, 0.0),
        ]
    )

    message, columns, wide_coef = call(
        functools.partial(pack_kernel, chans=chans),
        (
            sds((chans * 8, cells_y), BF16),
            sds((10, chans, cells_y), F32),
            sds((5, chans, cells_y), F32),
        ),
        [VMEM_SPEC] * 6,
        [pltpu.VMEM((5, chans * 8, cells_y), F32)],
    )(flat(rows), flat(first_in), flat(second_in), flat(first), flat(second), coef.T)

    def across(x, by):
        return lax.ppermute(x, "tile", [(i, (i + by) % tiles) for i in range(tiles)])

    up = across(message, TILE_ROWS)
    down = up if tiles == 2 * TILE_ROWS else across(message, -TILE_ROWS)

    size = cells_x // 4
    tall = pltpu.VMEM((chans, cells_x + 2 * MARGIN, cells_y), F32)
    height = chans * (EXTRA + size)
    moved = sds((chans * size, cells_y), F32)

    def transport(jobs, *halos):
        ahead = len(halos) == 0
        return call(
            functools.partial(transport_kernel, chans=chans, jobs=jobs, size=size, ahead=ahead),
            (sds((height, cells_y), BF16),) * len(jobs) + (() if ahead else (moved,) * 4),
            [VMEM_SPEC if ahead else ANY_SPEC] + [VMEM_SPEC] * (2 + len(halos)),
            [pltpu.VMEM((height, cells_y), F32) for _ in jobs]
            + [
                pltpu.VMEM((2, chans * 8, cells_y), F32),
                tall,
                tall,
                tall,
                pltpu.VMEM((2, 2, 2, chans, cells_y), F32),
                pltpu.VMEM((4 * cells_y, 2 * cells_y), BF16),
                pltpu.SemaphoreType.DMA((1,)),
            ],
            flops=5 * 10**9,
        )(block, wide_coef, columns, *halos)

    def swap(x):
        return lax.ppermute(x, "group", [(0, 1), (1, 0)])

    (theirs0,) = transport([(1, 0)])
    theirs1, *rest = transport([(1, 1), (0, 0), (0, 1)], up, down)
    mine, kept, others = rest[:2], rest[2:4], rest[4:]
    got = [swap(theirs0), swap(theirs1)]

    own = lax.axis_index("group")
    both = 2 * pad

    def ordered(w):
        return jnp.where(own == 0, w, w[::-1])

    w1 = ordered((w_in * 0.5).reshape(2, chans, 9, hidden)).transpose(3, 2, 0, 1)
    w1 = jnp.pad(w1, ((0, 0), (0, 0), (0, 0), (0, pad - chans))).reshape(hidden, 9 * both)
    w3 = ordered(w_out.T.reshape(2, chans, hidden))
    w3 = jnp.pad(w3, ((0, 0), (0, pad - chans), (0, 0))).reshape(both, hidden)
    w2 = (w_mid * 0.5).T

    back, owned = [], []
    blocks = pltpu.VMEM((9 * both, BLOCK_ROWS * cells_y), BF16)
    for n in range(2):
        mixed, other = call(
            functools.partial(physics_kernel, n, chans=chans),
            (moved, sds((chans * size, cells_y), BF16)),
            [ANY_SPEC] + [VMEM_SPEC] * 6 + [ANY_SPEC] * n,
            [
                pltpu.VMEM((3, 2, pad * (EXTRA + size), cells_y), F32),
                pltpu.VMEM((3, size + 2, both, cells_y), BF16),
                pltpu.VMEM((3, size, cells_y), F32),
                pltpu.VMEM((2, size, cells_y), jnp.int32),
                blocks,
                blocks,
                pltpu.VMEM((2, chans * size, cells_y), F32),
                pltpu.SemaphoreType.DMA((2,)),
            ],
            flops=7 * 10**9,
        )(neighbours, w1, w2, w3, mine[n], got[n], kept[n], *owned)
        owned.append(mixed)
        back.append(swap(other))
    owned = [x.reshape(chans, size, cells_y) for x in owned]
    parts = 4 if chans % 4 == 0 else 1
    whole = sds((chans, cells_x, cells_y), F32)
    image = call(
        functools.partial(finish_kernel, 0, parts=parts),
        whole,
        [VMEM_SPEC] * 4,
        [pltpu.VMEM((chans, size, cells_y), F32), pltpu.SemaphoreType.DMA((parts + 2,))],
        out_specs=ANY_SPEC,
        limit=4,
    )(back[0], others[0], *owned)
    image = call(
        functools.partial(finish_kernel, 1, parts=parts),
        whole,
        [VMEM_SPEC, VMEM_SPEC, ANY_SPEC],
        [pltpu.VMEM((chans, size, cells_y), F32), pltpu.SemaphoreType.DMA((parts,))],
        out_specs=ANY_SPEC,
        aliases={2: 0},
        limit=4,
    )(back[1], others[1], image)
    return image.reshape(levels, fields, single, cells_x, cells_y)


def solution(mesh):
    return jax.shard_map(
        shards,
        mesh=mesh,
        in_specs=(
            P("group", None, "tile", None, None),
            P("group"),
            P("group"),
            P(),
            P(None, "tile", None, None),
            P(),
            P(),
            P(),
        ),
        out_specs=P("group", None, "tile", None, None),
        check_vma=False,
    )
```

```python
import functools

import jax
import jax.numpy as jnp
from jax import lax
from jax.experimental import pallas as pl
from jax.experimental.pallas import tpu as pltpu
from jax.sharding import PartitionSpec as P


TILE_ROWS = 8
DEEP = 3
EXTRAS = 3
BLOCK_ROWS = 16
MARGIN = 16
GROUP = 4

F32 = jnp.float32
BF16 = jnp.bfloat16
VMEM_SPEC = pl.BlockSpec(memory_space=pltpu.VMEM)
ANY_SPEC = pl.BlockSpec(memory_space=pl.ANY)


def lanes_of(shape):
    return lax.broadcasted_iota(jnp.int32, shape, len(shape) - 1)


def first_row(q, n, quarter):
    return quarter * (1 + q) if n == 0 else 3 * quarter * q


def edge_kernel(state_ref, first_ref, second_ref, rows_ref):
    chans, cells_x, cells_y = state_ref.shape
    even = lax.axis_index("tile") % 2 == 0
    slot = lax.broadcasted_iota(jnp.int32, (16, cells_y), 0)
    lane = lanes_of((16, cells_y))
    wanted = jnp.where(slot < 8, slot + cells_y - DEEP, slot - 8)
    valid = (slot % 8) < DEEP
    pick = jnp.where(valid & (lane == wanted), 1.0, 0.0).astype(BF16)
    for c in range(chans):
        block = state_ref[c].astype(BF16)
        strips = lax.dot_general(
            pick, block, (((1,), (1,)), ((), ())), preferred_element_type=F32
        )
        east, west = strips[0:8], strips[8:16]
        first_ref[c] = jnp.where(even, east, west).astype(BF16)
        second_ref[c] = jnp.where(even, west, east).astype(BF16)
        rows_ref[c] = jnp.concatenate(
            [state_ref[c, 0:DEEP], state_ref[c, cells_x - DEEP : cells_x], state_ref[c, 0:2]], axis=0
        ).astype(BF16)


def pack_kernel(
    rows_ref, first_in, second_in, first_own, second_own, coef_ref, out_ref, column_ref, wide_ref, wide, *, chans
):
    width = rows_ref.shape[1]
    lane = lanes_of((chans, width))
    even = lax.axis_index("tile") % 2 == 0
    wide[0] = rows_ref[...].astype(F32)
    got = first_in[...].astype(F32), second_in[...].astype(F32)
    sent = first_own[...].astype(F32), second_own[...].astype(F32)
    wide[1] = jnp.where(even, got[1], got[0])
    wide[2] = jnp.where(even, got[0], got[1])
    wide[3] = jnp.where(even, sent[1], sent[0])
    wide[4] = jnp.where(even, sent[0], sent[1])
    sources = [(1, 0), (1, 1), (1, 2), (3, 0), (3, 1), (4, 1), (4, 2), (2, 0), (2, 1), (2, 2)]
    corner = jnp.zeros((chans, width), F32)
    for k, (n, slot) in enumerate(sources):
        line = wide[n, pl.ds(slot, chans, stride=8), :]
        column_ref[k] = line
        at = 2 * DEEP * k
        corner = jnp.where(
            (lane >= at) & (lane < at + 2 * DEEP), pltpu.roll(line, at + DEEP, 1), corner
        )
    for n in range(wide_ref.shape[0]):
        wide_ref[n] = jnp.broadcast_to(coef_ref[:, n : n + 1], (chans, width))
    wide[0, pl.ds(2 * DEEP, chans, stride=8), :] = corner
    out_ref[...] = wide[0].astype(BF16)


def shift_matrix(width):
    k = lax.broadcasted_iota(jnp.int32, (4 * width, 2 * width), 0)
    n = lax.broadcasted_iota(jnp.int32, (4 * width, 2 * width), 1)
    m = k % width
    lower = (n < width) & (n == m + 1)
    upper = (n >= width) & (n - width == m - 1)
    west = (k >= 2 * width) & (k < 3 * width) & (n == 0)
    east = (k >= 3 * width) & (n == 2 * width - 1)
    return jnp.where(((k < 2 * width) & (lower | upper)) | west | east, 1.0, 0.0).astype(BF16)


def transport_kernel(state_ref, coef_ref, column_ref, *rest, chans, jobs, size, ahead):
    count = len(jobs)
    halos, rest = ((), rest) if ahead else (rest[:2], rest[2:])
    packets, rest = rest[:count], rest[count:]
    quarters, rest = ((), rest) if ahead else (rest[:4], rest[4:])
    windows, rest = rest[:count], rest[count:]
    border, raw_s, once_s, last_s, line_s, matrix, sem = rest
    cells_x, width = state_ref.shape[1:]
    own = lax.axis_index("group")
    place = lax.axis_index("tile") % TILE_ROWS
    half_of = (own, 1 - own)
    pad = -(-chans // 8) * 8
    base_of = [first_row(half_of[whose], n, size) for whose, n in jobs]
    if not ahead:
        fetch = pltpu.make_async_copy(state_ref, raw_s.at[:, pl.ds(MARGIN, cells_x)], sem.at[0])
        fetch.start()
    matrix[...] = shift_matrix(width)
    lane = lanes_of((chans, width))
    first, last = lane == 0, lane == width - 1
    low_lanes = lane < width // 2
    for s, ref in enumerate(halos):
        border[s] = ref[...].astype(F32)
    coefs = [coef_ref[n] for n in range(5)]
    message = border.shape[1] // chans

    if ahead:
        corners = jnp.zeros((chans, width), F32)
    else:
        above, below = [border[s, pl.ds(2 * DEEP, chans, stride=message), :] for s in range(2)]
        corners = jnp.where(lane % (2 * DEEP) < DEEP, above, below)

    def pair(k):
        return column_ref[k], roll(corners, width - (2 * DEEP * k + DEEP))

    def roll(x, by):
        return pltpu.roll(x, by, 1)

    def both_ways(main, aux):
        ml, al = roll(main, 1), roll(aux, 1)
        mu, au = roll(main, width - 1), roll(aux, width - 1)
        lower = jnp.where(first, al, ml), jnp.where(first, ml, al)
        upper = jnp.where(last, au, mu), jnp.where(last, mu, au)
        return lower, upper

    def column(west, mid, east, keep):
        c0, cxl, cxu, cyl, cyu = coefs
        lower, upper = both_ways(*mid)
        return tuple(
            (c0 * mid[n] + cxl * lower[n] + cxu * upper[n] + cyl * west[n] + cyu * east[n]) * keep
            for n in range(2)
        )

    keeps = (
        jnp.where(place == 0, 0.0, 1.0),
        jnp.where(place == TILE_ROWS - 1, 0.0, 1.0),
    )
    edges = []
    for side in range(2):
        raw = [pair(5 * side + k) for k in range(5)]
        keep = keeps[side]
        inside = 3 if side == 0 else 1
        once = [
            column(raw[k - 1], raw[k], raw[k + 1], 1.0 if k == inside else keep)
            for k in (1, 2, 3)
        ]
        main, aux = column(once[0], once[1], once[2], keep)
        for level, edge in enumerate((raw[2], once[1])):
            for n in range(2):
                line_s[level, side, n] = edge[n]
        edges.append((main, aux))
    for window, base in zip(windows, base_of):
        at = base - 1
        sides = []
        for side, first_lane in enumerate((0, width // 2)):
            main, aux = edges[side]
            by = lax.rem(first_lane - at + width, width)
            row_of = lane - first_lane + at
            off = (row_of < 0) | (row_of >= cells_x)
            sides.append(jnp.where(off, roll(aux, by), roll(main, by)))
        window[pl.ds(chans * size + 2 * pad, chans), :] = jnp.where(low_lanes, *sides)
        for k in range(EXTRAS):
            if pad > chans:
                window[pl.ds(chans * size + k * pad + chans, pad - chans), :] = jnp.zeros(
                    (pad - chans, width), F32
                )

    rows = size + 16 if ahead else cells_x + 16
    origin = base_of[0] - 8 if ahead else -8
    top = pl.multiple_of(origin + MARGIN, 8) if ahead else 8
    at = lax.broadcasted_iota(jnp.int32, (rows, width), 0) + origin
    diagonal = lax.rem(at + width, width) == lanes_of((rows, width))
    within = (at >= 0) & (at < cells_x)
    if not ahead:
        fetch.wait()
    group = next(n for n in (10 if ahead else GROUP, 2, 1) if chans % n == 0)

    def sweep(level, src, dst, base):
        near_top = pl.multiple_of(origin, 8) if ahead and level == 0 else top
        parts = []
        for g in range(group):
            c = base + g
            q = src[c, pl.ds(near_top, rows), :]
            hi = q.astype(BF16)
            lo = (q - hi.astype(F32)).astype(BF16)
            sides = []
            for side in range(2):
                main = line_s[level, side, 0, pl.ds(c, 1), :]
                aux = line_s[level, side, 1, pl.ds(c, 1), :]
                values = jnp.where(within, main, aux)
                sides.append(jnp.where(diagonal, values, 0.0).astype(BF16))
            parts.append(jnp.concatenate([hi, lo] + sides, axis=1))
        near = lax.dot_general(
            jnp.concatenate(parts, axis=0),
            matrix[...],
            (((1,), (0,)), ((), ())),
            preferred_element_type=F32,
        )
        for g in range(group):
            c = base + g
            lower, upper = near[g * rows : (g + 1) * rows, :width], near[g * rows : (g + 1) * rows, width:]
            c0, cxl, cxu, cyl, cyu = [coef_ref[n, pl.ds(c, 1), :] for n in range(5)]
            dst[c, pl.ds(top, rows), :] = (
                c0 * src[c, pl.ds(near_top, rows), :]
                + cxl * src[c, pl.ds(near_top - 1, rows), :]
                + cxu * src[c, pl.ds(near_top + 1, rows), :]
                + cyl * lower
                + cyu * upper
            )

    def finish(base):
        for g in range(group):
            c = base + g
            for window, row in zip(windows, base_of):
                at = MARGIN + row
                to = chans * size + c
                window[pl.ds(to, 1), :] = last_s[c, pl.ds(at - 1, 1), :]
                window[pl.ds(to + pad, 1), :] = last_s[c, pl.ds(at + size, 1), :]
                window[pl.ds(c * size, size), :] = last_s[c, pl.ds(pl.multiple_of(at, 8), size), :]
            for k, quarter in enumerate(quarters):
                at = pl.multiple_of(MARGIN + first_row(half_of[k // 2], k % 2, size), 8)
                quarter[pl.ds(c * size, size), :] = last_s[c, pl.ds(at, size), :]

    for c in range(0 if ahead else chans):
        raw_s[c, pl.ds(MARGIN - DEEP, DEEP), :] = border[0, pl.ds(c * message + DEEP, DEEP), :]
        raw_s[c, pl.ds(MARGIN + cells_x, DEEP), :] = border[1, pl.ds(c * message, DEEP), :]
    for base in range(0, chans + group, group):
        if base < chans:
            sweep(0, state_ref if ahead else raw_s, once_s, base)
        if base:
            sweep(1, once_s, last_s, base - group)
            finish(base - group)
    for packet, window in zip(packets, windows):
        packet[...] = window[...].astype(BF16)


def physics_kernel(
    chunk, table_ref, w1_ref, w2_ref, w3_ref, mine_ref, got_ref, kept_ref, *rest, chans
):
    own_ref, other_ref, wide, ends, packed, mask, table, even, odd, terms, sem = rest[-11:]
    size, width = table.shape[1:]
    height = mine_ref.shape[0]
    pitch = size + 8
    pad = -(-chans // 8) * 8
    both = 2 * pad
    top = first_row(lax.axis_index("group"), chunk, size)
    copies = [
        pltpu.make_async_copy(table_ref.at[k, 0, pl.ds(top, size)], table.at[n], sem.at[n])
        for n, k in enumerate((5, 7))
    ]
    for copy in copies:
        copy.start()

    k = lax.broadcasted_iota(jnp.int32, (2 * width, 2 * width), 0)
    n = lax.broadcasted_iota(jnp.int32, (2 * width, 2 * width), 1)
    inner = (k < width) & (((n < width) & (n == k + 1)) | ((n >= width) & (n - width == k - 1)))
    west = (k >= width) & (k < width + width // 2) & (n == 0)
    east = (k >= width + width // 2) & (n == 2 * width - 1)
    matrix = jnp.where(inner | west | east, 1.0, 0.0).astype(BF16)
    lanes = lanes_of((size, width)) % (width // 2)
    diagonal = lanes == lax.broadcasted_iota(jnp.int32, (size, width), 0) + 1
    lane = lanes_of((pad, width)) % (width // 2)
    end = chans * size
    for s, ref in enumerate((mine_ref, got_ref)):
        cells = ref[...]
        flat = cells.astype(F32)
        sides = flat[end + 2 * pad : end + 3 * pad]
        edges = [jnp.where(diagonal, sides[c : c + 1], 0.0) for c in range(chans)]
        edges += [jnp.where(lane == 0, sides, 0.0), jnp.where(lane == size + 1, sides, 0.0)]
        edges.append(jnp.zeros((height - end - 2 * pad, width), F32))
        edges = jnp.concatenate(edges, axis=0).astype(BF16)
        near = lax.dot_general(
            jnp.concatenate([cells, edges], axis=1),
            matrix,
            (((1,), (0,)), ((), ())),
            preferred_element_type=F32,
        )
        for b, x in enumerate((near[:, :width], flat, near[:, width:])):
            for c in range(chans):
                wide[b, s, pl.ds(c * pitch, size)] = x[c * size : (c + 1) * size]
            for k in range(2):
                ends[b, s, k] = x[end + k * pad : end + (k + 1) * pad]
            if pad > chans:
                wide[b, s, pl.ds(chans * pitch, (pad - chans) * pitch)] = jnp.zeros(
                    ((pad - chans) * pitch, width), F32
                )

    def cells_at(b, s, l):
        if 0 <= l < size:
            return wide[b, s, pl.ds(l, pad, stride=pitch), :]
        return ends[b, s, int(l == size)]

    for l in range(-1, size + 1):
        for b in range(3):
            pair = [cells_at(b, s, l) for s in range(2)]
            packed[b, l + 1] = jnp.concatenate(pair, axis=0).astype(BF16)

    for copy in copies:
        copy.wait()
    rows_i = lax.broadcasted_iota(jnp.int32, (size, width), 0) + top
    centre = (rows_i + 1) * (width + 2) + lanes_of((size, width)) + 1
    along_y = table[0] - centre
    along_x = table[1] - centre
    turned = jnp.abs(along_x) == 1
    mask[0] = jnp.where(jnp.where(turned, along_y, along_x) < 0, 1.0, 0.0)
    mask[1] = jnp.where(jnp.where(turned, along_x, along_y) < 0, 1.0, 0.0)
    mask[2] = jnp.where(turned, 1.0, 0.0)

    def choose(m, a, b):
        return jnp.where(m, a, b), jnp.where(m, b, a)

    rows_step = even.shape[1] // width

    def stack(n, dst):
        for u in range(rows_step):
            l = n * rows_step + u
            m = []
            for k in range(3):
                line = jnp.broadcast_to(mask[k, pl.ds(l, 1), :], (16, width)).astype(BF16)
                m.append(jnp.concatenate([line] * (both // 16), axis=0) > 0.5)
            x = [[packed[bb, l + aa] for bb in range(3)] for aa in range(3)]
            for bb in range(3):
                x[0][bb], x[2][bb] = choose(m[0], x[2][bb], x[0][bb])
            for aa in range(3):
                x[aa][0], x[aa][2] = choose(m[1], x[aa][2], x[aa][0])
            for aa, bb in ((0, 1), (0, 2), (1, 2)):
                x[aa][bb], x[bb][aa] = choose(m[2], x[bb][aa], x[aa][bb])
            for k in range(9):
                dst[pl.ds(k * both, both), pl.ds(u * width, width)] = x[k // 3][k % 3]

    dot = functools.partial(
        lax.dot_general,
        dimension_numbers=(((1,), (0,)), ((), ())),
        preferred_element_type=F32,
    )

    def silu(v):
        return (v * jnp.tanh(v) + v).astype(BF16)

    def network(n, src):
        first = silu(dot(w1_ref[...], src[...]))
        second = silu(dot(w2_ref[...], first))
        tend = dot(w3_ref[...], second)
        for u in range(rows_step):
            l = n * rows_step + u
            cols = slice(u * width, (u + 1) * width)
            terms[0, pl.ds(l, chans, stride=pitch), :] = tend[0:chans, cols]
            terms[1, pl.ds(l, chans, stride=pitch), :] = tend[pad : pad + chans, cols]

    steps = size // rows_step
    slots = (even, odd)
    stack(0, even)
    for n in range(steps):
        if n + 1 < steps:
            stack(n + 1, slots[(n + 1) % 2])
        network(n, slots[n % 2])
    for c in range(chans):
        rows, line = pl.ds(c * size, size), pl.ds(c * pitch, size)
        other_ref[rows] = terms[1, line].astype(BF16)
        own_ref[rows] = kept_ref[rows] + terms[0, line]


def finish_kernel(chunk, back_ref, moved_ref, *rest, parts):
    image_ref, patch, sem = rest[-3:]
    chans, size, width = patch.shape
    own = lax.axis_index("group")
    put = []
    if chunk == 0:
        for n in range(2):
            rows = pl.ds(first_row(own, n, size), size)
            put.append(pltpu.make_async_copy(rest[n], image_ref.at[:, rows], sem.at[parts + n]))
            put[-1].start()
    rows = pl.ds(first_row(1 - own, chunk, size), size)
    some = chans // parts
    for n in range(parts):
        c, r = pl.ds(n * some, some), pl.ds(n * some * size, some * size)
        patch[c] = (moved_ref[r] + back_ref[r].astype(F32)).reshape(some, size, width)
        put.append(pltpu.make_async_copy(patch.at[c], image_ref.at[c, rows], sem.at[n]))
        put[-1].start()
    for copy in put:
        copy.wait()


def call(kernel, outs, ins, scratch=(), flops=10**9, out_specs=None, aliases=None, limit=24):
    return pl.pallas_call(
        kernel,
        out_shape=jax.tree.map(lambda x: jax.ShapeDtypeStruct(x.shape, x.dtype), outs),
        in_specs=ins,
        out_specs=jax.tree.map(lambda _: VMEM_SPEC, outs) if out_specs is None else out_specs,
        input_output_aliases=aliases or {},
        scratch_shapes=list(scratch),
        compiler_params=pltpu.CompilerParams(vmem_limit_bytes=limit << 20),
        cost_estimate=pl.CostEstimate(flops=flops, bytes_accessed=10**6, transcendentals=0),
    )


def shards(state, courant_x, courant_y, diffusion, neighbours, w_in, w_mid, w_out):
    levels, fields, single, cells_x, cells_y = state.shape
    chans = levels * fields
    hidden = w_mid.shape[0]
    tiles = lax.axis_size("tile")
    pad = -(-chans // 8) * 8
    block = state.reshape(chans, cells_x, cells_y)
    sds = jax.ShapeDtypeStruct

    strip = sds((chans, 8, cells_y), BF16)
    first, second, rows = call(edge_kernel, (strip, strip, strip), [VMEM_SPEC])(block)

    def beside(odd):
        pairs = [(i, i + 1) for i in range(odd, tiles - 1, 2) if i % TILE_ROWS != TILE_ROWS - 1]
        return pairs + [(b, a) for a, b in pairs]

    first_in = lax.ppermute(first, "tile", beside(0))
    second_in = lax.ppermute(second, "tile", beside(1))

    def flat(x):
        return x.reshape(-1, cells_y)

    ax = jnp.repeat(courant_x, fields)
    ay = jnp.repeat(courant_y, fields)
    nu = jnp.tile(diffusion, levels)
    coef = jnp.stack(
        [
            1.0 - jnp.abs(ax) - jnp.abs(ay) - 4.0 * nu,
            jnp.maximum(ax, 0.0) + nu,
            nu - jnp.minimum(ax, 0.0),
            jnp.maximum(ay, 0.0) + nu,
            nu - jnp.minimum(ay, 0.0),
        ]
    )

    message, columns, wide_coef = call(
        functools.partial(pack_kernel, chans=chans),
        (
            sds((chans * 8, cells_y), BF16),
            sds((10, chans, cells_y), F32),
            sds((5, chans, cells_y), F32),
        ),
        [VMEM_SPEC] * 6,
        [pltpu.VMEM((5, chans * 8, cells_y), F32)],
    )(flat(rows), flat(first_in), flat(second_in), flat(first), flat(second), coef.T)

    def across(x, by):
        return lax.ppermute(x, "tile", [(i, (i + by) % tiles) for i in range(tiles)])

    up = across(message, TILE_ROWS)
    down = up if tiles == 2 * TILE_ROWS else across(message, -TILE_ROWS)

    size = cells_x // 4
    tall = pltpu.VMEM((chans, cells_x + 2 * MARGIN, cells_y), F32)
    height = -(-(chans * size + EXTRAS * pad) // 16) * 16
    moved = sds((chans * size, cells_y), F32)

    def transport(jobs, *halos):
        ahead = len(halos) == 0
        return call(
            functools.partial(transport_kernel, chans=chans, jobs=jobs, size=size, ahead=ahead),
            (sds((height, cells_y), BF16),) * len(jobs) + (() if ahead else (moved,) * 4),
            [VMEM_SPEC if ahead else ANY_SPEC] + [VMEM_SPEC] * (2 + len(halos)),
            [pltpu.VMEM((height, cells_y), F32) for _ in jobs]
            + [
                pltpu.VMEM((2, chans * 8, cells_y), F32),
                tall,
                tall,
                tall,
                pltpu.VMEM((2, 2, 2, chans, cells_y), F32),
                pltpu.VMEM((4 * cells_y, 2 * cells_y), BF16),
                pltpu.SemaphoreType.DMA((1,)),
            ],
            flops=5 * 10**9,
        )(block, wide_coef, columns, *halos)

    def swap(x):
        return lax.ppermute(x, "group", [(0, 1), (1, 0)])

    (theirs0,) = transport([(1, 0)])
    theirs1, *rest = transport([(1, 1), (0, 0), (0, 1)], up, down)
    mine, kept, others = rest[:2], rest[2:4], rest[4:]
    got = [swap(theirs0), swap(theirs1)]

    own = lax.axis_index("group")
    both = 2 * pad

    def ordered(w):
        return jnp.where(own == 0, w, w[::-1])

    w1 = ordered((w_in * 0.5).reshape(2, chans, 9, hidden)).transpose(3, 2, 0, 1)
    w1 = jnp.pad(w1, ((0, 0), (0, 0), (0, 0), (0, pad - chans))).reshape(hidden, 9 * both)
    w3 = ordered(w_out.T.reshape(2, chans, hidden))
    w3 = jnp.pad(w3, ((0, 0), (0, pad - chans), (0, 0))).reshape(both, hidden)
    w2 = (w_mid * 0.5).T

    back, owned = [], []
    blocks = pltpu.VMEM((9 * both, BLOCK_ROWS * cells_y), BF16)
    for n in range(2):
        mixed, other = call(
            functools.partial(physics_kernel, n, chans=chans),
            (moved, sds((chans * size, cells_y), BF16)),
            [ANY_SPEC] + [VMEM_SPEC] * 6 + [ANY_SPEC] * n,
            [
                pltpu.VMEM((3, 2, pad * (size + 8), cells_y), F32),
                pltpu.VMEM((3, 2, 2, pad, cells_y), F32),
                pltpu.VMEM((3, size + 2, both, cells_y), BF16),
                pltpu.VMEM((3, size, cells_y), F32),
                pltpu.VMEM((2, size, cells_y), jnp.int32),
                blocks,
                blocks,
                pltpu.VMEM((2, chans * (size + 8), cells_y), F32),
                pltpu.SemaphoreType.DMA((2,)),
            ],
            flops=7 * 10**9,
        )(neighbours, w1, w2, w3, mine[n], got[n], kept[n], *owned)
        owned.append(mixed)
        back.append(swap(other))
    owned = [x.reshape(chans, size, cells_y) for x in owned]
    parts = 4 if chans % 4 == 0 else 1
    whole = sds((chans, cells_x, cells_y), F32)
    image = call(
        functools.partial(finish_kernel, 0, parts=parts),
        whole,
        [VMEM_SPEC] * 4,
        [pltpu.VMEM((chans, size, cells_y), F32), pltpu.SemaphoreType.DMA((parts + 2,))],
        out_specs=ANY_SPEC,
        limit=4,
    )(back[0], others[0], *owned)
    image = call(
        functools.partial(finish_kernel, 1, parts=parts),
        whole,
        [VMEM_SPEC, VMEM_SPEC, ANY_SPEC],
        [pltpu.VMEM((chans, size, cells_y), F32), pltpu.SemaphoreType.DMA((parts,))],
        out_specs=ANY_SPEC,
        aliases={2: 0},
        limit=4,
    )(back[1], others[1], image)
    return image.reshape(levels, fields, single, cells_x, cells_y)


def solution(mesh):
    return jax.shard_map(
        shards,
        mesh=mesh,
        in_specs=(
            P("group", None, "tile", None, None),
            P("group"),
            P("group"),
            P(),
            P(None, "tile", None, None),
            P(),
            P(),
            P(),
        ),
        out_specs=P("group", None, "tile", None, None),
        check_vma=False,
    )
```
